32 devices in a mesh: seq: 8 (over y, x, core), batch: 4 (over z).
Axes of the slice: x: 2, y: 2, z: 4, core: 2. Of those that a mesh axis runs over, the one named last changes fastest.
Arguments:
- inputs: bfloat16 [4, 1536, 1024], P('batch', 'seq'), may hold values from -6 to 6
- cotangent: bfloat16 [4, 1536, 1024], P('batch', 'seq'), may hold values from -6 to 6
- lengths: int32 [4, 1], P('batch'), may hold values from 384 to 1536, as said below
- rand_owners: int32 [4, 24, 3], P('batch'), may hold values from 0 to 7, all different within a row; in each aligned block of 3 rows (0 to 2, 3 to 5, ..., all dimensions but the last counted through in order) at most 2 rows name the same one
- rand_offsets: int32 [4, 24, 3], P('batch'), may hold values from 0 to 2
- global_ids: int32 [4, 1, 2], P('batch'), may hold values from 0 to 5
- ln1_gain: bfloat16 [1024], replicated, may hold values from 0.5 to 1.5
- ln1_shift: bfloat16 [1024], replicated, may hold values from -3 to 3
- w_query: bfloat16 [1024, 1024], replicated, may hold values from -0.1875 to 0.1875
- w_key: bfloat16 [1024, 1024], replicated, may hold values from -0.1875 to 0.1875
- w_value: bfloat16 [1024, 1024], replicated, may hold values from -0.1875 to 0.1875
- w_out: bfloat16 [1024, 1024], replicated, may hold values from -2 to 2
- ln2_gain: bfloat16 [1024], replicated, may hold values from 0.5 to 1.5
- ln2_shift: bfloat16 [1024], replicated, may hold values from -3 to 3
- w_in: bfloat16 [1024, 4096], replicated, may hold values from -0.1875 to 0.1875
- b_in: bfloat16 [4096], replicated, may hold values from -3 to 3
- w_back: bfloat16 [4096, 1024], replicated, may hold values from -0.09375 to 0.09375
- b_back: bfloat16 [1024], replicated, may hold values from -3 to 3
Outputs:
- output: bfloat16 [4, 1536, 1024], P('batch', 'seq')
- input_grad: bfloat16 [4, 1536, 1024], P('batch', 'seq')
- ln1_gain_grad: float32 [1024], P(('seq', 'batch'))
- ln1_shift_grad: float32 [1024], P(('seq', 'batch'))
- query_grad: float32 [1024, 1024], P(('seq', 'batch'))
- key_grad: float32 [1024, 1024], P(('seq', 'batch'))
- value_grad: float32 [1024, 1024], P(('seq', 'batch'))
- out_grad: float32 [1024, 1024], P(('seq', 'batch'))
- ln2_gain_grad: float32 [1024], P(('seq', 'batch'))
- ln2_shift_grad: float32 [1024], P(('seq', 'batch'))
- in_grad: float32 [1024, 4096], P(('seq', 'batch'))
- in_bias_grad: float32 [4096], P(('seq', 'batch'))
- back_grad: float32 [4096, 1024], P(('seq', 'batch'))
- back_bias_grad: float32 [1024], P(('seq', 'batch'))
The draws below stay inside these ranges and needn't reach their ends.
Inputs may be any that keep to these rules, and one draw needn't show every extreme that they name: `rand_owners`: each row names 3 different groups of the item, numbered 0 .. 7; among the 3 rows of one group no group is named more than 2 times, and 2 is reached in every draw. `lengths`: most items are about a quarter of 1536 long; some item has exactly 1536 tokens.
All inputs are finite; a program needn't handle non-finite values.
Results may differ from the reference program's by a relative error of at most 0.015.
Values may be sent and summed in bfloat16 or wider, within the bound.
No kernel may reach another device: no remote copies, remote signals or barrier semaphores. Data moves between devices by JAX's collectives and lax.ppermute only.
A program may use at most 320 MiB of HBM per device.

```python
import math
import jax
import jax.numpy as jnp
import numpy as np
from jax import lax

MODEL_DIMENSION = 1024
HEADS = 16
FF = 4096
BLK = 64
RAND = 3
WIN = 3
GLOB = 2
QB_DEV = 3
ITEM_QB = 24
HEAD_DIM = 64
ITEMLEN = 1536
ITEM_DEVS = 8
PACK = 1
PACKED_ROWS = 4
ITEMS = 4
ROW_QB = 24
ROW_TOKENS = 1536
MOST = 2
KEYS = 512


def draw_lengths(key, part):
    first_key, key_second, third_key = jax.random.split(key, 3)
    longer = jax.random.randint(first_key, (PACKED_ROWS, PACK), 0, 4) == 0
    jitter = jax.random.randint(key_second, (PACKED_ROWS, PACK), 0, BLK)
    shorter = ITEMLEN // 4 + jitter
    chosen = jnp.where(longer, ITEMLEN, shorter)
    longest = jax.random.randint(third_key, (), 0, PACKED_ROWS * PACK)
    flat = jnp.where(jnp.arange(PACKED_ROWS * PACK) == longest, ITEMLEN, chosen.reshape(PACKED_ROWS * PACK))
    return flat.reshape(PACKED_ROWS, PACK).astype(jnp.int32)


def touch_ends(values, key, smallest, high):
    spot = [jax.random.randint(jax.random.fold_in(key, axis), (), 0, length) for axis, length in enumerate(values.shape)]
    main_axis = values.shape.index(max(values.shape))
    next_to = spot[:main_axis] + [(spot[main_axis] + 1) % values.shape[main_axis]] + spot[main_axis + 1:]
    return values.at[tuple(spot)].set(smallest).at[tuple(next_to)].set(high)


def level_of(rng, shape, pieces, low, top_value):
    def one(axis_at, parts):
        draws = jax.random.uniform(jax.random.fold_in(jax.random.fold_in(rng, 6), axis_at), (parts,), jnp.float32, low / len(pieces), top_value / len(pieces))
        return jnp.repeat(jnp.exp(draws), shape[axis_at] // parts).reshape((-1,) + (1,) * (len(shape) - axis_at - 1))

    gain = one(*pieces[0])
    for cut in pieces[1:]:
        gain = gain * one(*cut)
    return gain


def shared_out(own_key, own, number, rows, amount, top, limit, skew):
    sequence = jax.random.permutation(own_key, amount)
    packed, usual = load_shares(amount, rows * top, limit, skew, True), load_shares(amount, rows * top, limit, skew, False)
    places = jnp.arange(amount)

    def named(sizes, turn):
        used = int((sizes > 0).sum())
        fixed = max(1, used // 4)
        shifted = fixed + (places - fixed + turn * (used - fixed)) % max(1, amount - fixed)
        return jnp.zeros((amount,), jnp.int32).at[sequence[jnp.where(places < fixed, places, shifted)]].set(jnp.asarray(sizes, jnp.int32))

    sizes = jnp.where(number % 4 == 0, named(packed, number // 4), named(usual, number - number // 4 - 1))
    mixed = jax.random.permutation(jax.random.fold_in(own, 3), amount)
    source_of, taker = mixed[0:amount // 2 * 2:2], mixed[1:amount // 2 * 2:2]
    room = jnp.minimum(sizes[source_of] - 1, limit - sizes[taker]) // 2
    room = jnp.where((source_of == sequence[0]) | (taker == sequence[0]) | (sizes[taker] == 0), 0, jnp.maximum(room, 0))
    shifted = jax.random.randint(jax.random.fold_in(own, 4), (amount // 2,), 0, 1 << 20) % (room + 1)
    sizes = sizes.at[source_of].add(-shifted).at[taker].add(shifted)
    labels = jnp.searchsorted(jnp.cumsum(sizes), jnp.arange(rows * top), side="right").astype(jnp.int32)
    grid = labels.reshape(top, rows).T
    grid = grid[jax.random.permutation(jax.random.fold_in(own, 1), rows)]
    turn = jax.random.randint(jax.random.fold_in(own, 2), (rows, 1), 0, top)
    return jnp.take_along_axis(grid, (jnp.arange(top)[None, :] + turn) % top, axis=1)


def load_shares(number_of, total, limit, skew, full):
    portions = [(1 << 20) // math.isqrt(standing ** skew) + 1 for standing in range(1, number_of + 1)]
    largest = limit if full else min(limit, max(-(-total // number_of), total * portions[0] // sum(portions)))
    least = 1 if total - largest >= number_of - 1 else 0
    holding, rest = [largest] + [least] * (number_of - 1), total - largest - least * (number_of - 1)
    while rest > 0:
        movable = [i for i in range(1, number_of) if holding[i] < largest] or [i for i in range(1, number_of) if holding[i] < limit]
        pool, left = sum([portions[i] for i in movable]), rest
        for i in movable:
            more = min(limit - holding[i], max(1, left * portions[i] // pool), rest)
            holding[i] = holding[i] + more
            rest = rest - more
    return np.array(holding)


def normal_values(own_key, dims, width, bound, cuts=(), kind=jnp.bfloat16):
    array = width * jax.random.normal(own_key, dims, jnp.float32)
    if cuts:
        array = array * level_of(own_key, dims, cuts, -0.22, 0.18)
    return jnp.clip(array, -bound, bound).astype(kind)


def setup_inputs(seed: int = 0) -> dict:
    key_of = jax.random.split(jax.random.key(seed), 19)
    inputs = normal_values(key_of[0], (PACKED_ROWS, ROW_TOKENS, MODEL_DIMENSION), 1.0, 6.0, ((0, 4), (1, 8)))
    cotangent = normal_values(key_of[1], (PACKED_ROWS, ROW_TOKENS, MODEL_DIMENSION), 1.0, 6.0, ((0, 4), (1, 8)))
    lengths = draw_lengths(jax.random.fold_in(key_of[18], 71), 0)
    rand_owners_keys = jax.random.split(jax.random.fold_in(key_of[3], 1), PACKED_ROWS * ROW_QB // QB_DEV)
    rand_owners_turns = jax.random.permutation(jax.random.fold_in(key_of[3], 3), PACKED_ROWS * ROW_QB // QB_DEV)
    rand_owners = jax.vmap(lambda own, number: shared_out(jax.random.fold_in(key_of[3], 2), own, number, QB_DEV, ITEM_DEVS, RAND, MOST, 2))(rand_owners_keys, rand_owners_turns).reshape((PACKED_ROWS, ROW_QB, RAND))
    rand_offsets = touch_ends(jax.random.randint(key_of[4], (PACKED_ROWS, ROW_QB, RAND), 0, QB_DEV), jax.random.fold_in(key_of[4], 1), 0, QB_DEV - 1).astype(jnp.int32)
    global_ids = touch_ends(jax.random.randint(key_of[5], (PACKED_ROWS, PACK, GLOB), 0, ITEM_QB // 4), jax.random.fold_in(key_of[5], 1), 0, (ITEM_QB // 4) - 1).astype(jnp.int32)
    ln1_gain = jnp.clip(1.0 + 0.1 * jax.random.normal(key_of[6], (MODEL_DIMENSION,), jnp.float32), 0.5, 1.5).astype(jnp.bfloat16)
    ln1_shift = normal_values(key_of[7], (MODEL_DIMENSION,), 0.5, 3.0)
    w_query = normal_values(key_of[8], (MODEL_DIMENSION, MODEL_DIMENSION), MODEL_DIMENSION ** -0.5, 0.1875)
    w_key = normal_values(key_of[9], (MODEL_DIMENSION, MODEL_DIMENSION), MODEL_DIMENSION ** -0.5, 0.1875)
    w_value = normal_values(key_of[10], (MODEL_DIMENSION, MODEL_DIMENSION), MODEL_DIMENSION ** -0.5, 0.1875)
    w_out = normal_values(key_of[11], (MODEL_DIMENSION, MODEL_DIMENSION), (max(MODEL_DIMENSION // 128, 1)) ** -0.5, 2.0)
    ln2_gain = jnp.clip(1.0 + 0.1 * jax.random.normal(key_of[12], (MODEL_DIMENSION,), jnp.float32), 0.5, 1.5).astype(jnp.bfloat16)
    ln2_shift = normal_values(key_of[13], (MODEL_DIMENSION,), 0.5, 3.0)
    w_in = normal_values(key_of[14], (MODEL_DIMENSION, FF), MODEL_DIMENSION ** -0.5, 0.1875)
    b_in = normal_values(key_of[15], (FF,), 0.5, 3.0)
    w_back = normal_values(key_of[16], (FF, MODEL_DIMENSION), FF ** -0.5, 0.09375)
    b_back = normal_values(key_of[17], (MODEL_DIMENSION,), 0.5, 3.0)
    return dict(inputs=inputs, cotangent=cotangent, lengths=lengths, rand_owners=rand_owners, rand_offsets=rand_offsets, global_ids=global_ids, ln1_gain=ln1_gain, ln1_shift=ln1_shift, w_query=w_query, w_key=w_key, w_value=w_value, w_out=w_out, ln2_gain=ln2_gain, ln2_shift=ln2_shift, w_in=w_in, b_in=b_in, w_back=w_back, b_back=b_back)


@jax.custom_vjp
def low(v):
    return lax.optimization_barrier(v.astype(jnp.bfloat16)).astype(jnp.float32)

@jax.custom_vjp
def low_back(v):
    return v

def low_keep(v):
    return (low(v), None)

def low_pass(kept, grad):
    return (grad,)

def back_keep(v):
    return (v, None)

def back_low(kept, grad):
    return (low(grad),)
low.defvjp(low_keep, low_pass)
low_back.defvjp(back_keep, back_low)
highest = lax.Precision.HIGHEST
norm_eps = 1e-05
masked_score = -1e+30

def product(left, right):
    return jnp.dot(left, right, precision=highest, preferred_element_type=jnp.float32)

def layer_norm(values, ln_gain, ln_shift):
    average = lax.optimization_barrier(jnp.mean(values, axis=-1, keepdims=True))
    centered = values - average
    variance = lax.optimization_barrier(jnp.mean(centered * centered, axis=-1, keepdims=True))
    return centered * lax.rsqrt(variance + norm_eps) * ln_gain + ln_shift

def attention(queries, keys, values, length, rand_blocks, global_list):
    keyvals = jnp.concatenate([keys, values], axis=1)
    border = jnp.zeros((BLK, 2 * MODEL_DIMENSION), jnp.float32)
    padded = jnp.concatenate([border, keyvals, border], axis=0)
    kv_blocks = keyvals.reshape(ITEM_QB, BLK, 2 * MODEL_DIMENSION)
    global_kv = jnp.take(kv_blocks, global_list, axis=0)
    scale = HEAD_DIM ** (-0.5)
    inside = jnp.arange(BLK, dtype=jnp.int32)

    def one_group(group):
        first = group * QB_DEV
        query_rows = lax.dynamic_slice_in_dim(queries, first * BLK, QB_DEV * BLK, 0).reshape(QB_DEV, BLK, HEADS, HEAD_DIM)
        window = lax.dynamic_slice_in_dim(padded, first * BLK, (QB_DEV + 2) * BLK, 0).reshape(QB_DEV + 2, BLK, 2 * MODEL_DIMENSION)
        window = jnp.stack([window[:-2], window[1:-1], window[2:]], axis=1)
        chosen = lax.dynamic_slice_in_dim(rand_blocks, first, QB_DEV, 0)
        random_kv = jnp.take(kv_blocks, chosen.reshape(-1), axis=0).reshape(QB_DEV, RAND, BLK, 2 * MODEL_DIMENSION)
        shared = jnp.broadcast_to(global_kv[None], (QB_DEV, GLOB, BLK, 2 * MODEL_DIMENSION))
        gathered = jnp.concatenate([window, random_kv, shared], axis=1).reshape(QB_DEV, KEYS, 2 * MODEL_DIMENSION)
        key_part = gathered[:, :, :MODEL_DIMENSION].reshape(QB_DEV, KEYS, HEADS, HEAD_DIM)
        value_part = gathered[:, :, MODEL_DIMENSION:].reshape(QB_DEV, KEYS, HEADS, HEAD_DIM)
        own_blocks = first + jnp.arange(QB_DEV, dtype=jnp.int32)
        window_ids = own_blocks[:, None] + jnp.arange(WIN, dtype=jnp.int32)[None, :] - WIN // 2
        block_ids = jnp.concatenate([window_ids, chosen, jnp.broadcast_to(global_list[None, :], (QB_DEV, GLOB))], axis=1)
        positions = (block_ids[:, :, None] * BLK + inside).reshape(QB_DEV, KEYS)
        valid = (positions >= 0) & (positions < length)
        score_values = jnp.einsum('bqhd,bkhd->bhqk', query_rows, key_part, precision=highest) * scale
        score_values = low_back(score_values)
        score_values = jnp.where(valid[:, None, None, :], score_values, masked_score)
        top = lax.optimization_barrier(jnp.max(score_values, axis=-1, keepdims=True))
        raised = jnp.exp(score_values - top)
        weights = low(raised / lax.optimization_barrier(jnp.sum(raised, axis=-1, keepdims=True)))
        attended = jnp.einsum('bhqk,bkhd->bqhd', weights, value_part, precision=highest)
        return attended.reshape(QB_DEV * BLK, MODEL_DIMENSION)
    groups_out = lax.map(jax.checkpoint(one_group), jnp.arange(ITEM_DEVS, dtype=jnp.int32))
    return groups_out.reshape(ITEMLEN, MODEL_DIMENSION)

def forward(inputs, params, length, rand_blocks, global_list):
    ln1_gain, ln1_shift, w_query, w_key, w_value, w_out, ln2_gain, ln2_shift, w_in, b_in, w_back, b_back = params
    normed = low(layer_norm(inputs, ln1_gain, ln1_shift))
    queries = low_back(low(product(normed, w_query)))
    keys = low_back(low(product(normed, w_key)))
    values = low_back(low(product(normed, w_value)))
    attended = low_back(low(attention(queries, keys, values, length, rand_blocks, global_list)))
    middle = inputs + low_back(product(attended, w_out))
    normed_two = low(layer_norm(middle, ln2_gain, ln2_shift))
    inner = low_back(product(normed_two, w_in) + b_in)
    activated = low(jax.nn.gelu(inner, approximate=False))
    return middle + low_back(product(activated, w_back) + b_back)

def reference(inputs, cotangent, lengths, rand_owners, rand_offsets, global_ids, ln1_gain, ln1_shift, w_query, w_key, w_value, w_out, ln2_gain, ln2_shift, w_in, b_in, w_back, b_back):
    params = (ln1_gain.astype(jnp.float32), ln1_shift.astype(jnp.float32), w_query.astype(jnp.float32), w_key.astype(jnp.float32), w_value.astype(jnp.float32), w_out.astype(jnp.float32), ln2_gain.astype(jnp.float32), ln2_shift.astype(jnp.float32), w_in.astype(jnp.float32), b_in.astype(jnp.float32), w_back.astype(jnp.float32), b_back.astype(jnp.float32))
    rand_blocks = (rand_owners * QB_DEV + rand_offsets).astype(jnp.int32).reshape(ITEMS, ITEM_QB, RAND)
    item_inputs = inputs.reshape(ITEMS, ITEMLEN, MODEL_DIMENSION)
    item_cotangents = cotangent.reshape(ITEMS, ITEMLEN, MODEL_DIMENSION)
    item_lengths = lengths.reshape(ITEMS).astype(jnp.int32)
    item_globals = global_ids.reshape(ITEMS, GLOB).astype(jnp.int32)

    def per_item(totals, item):
        one_input, one_cotangent, length, blocks, global_list = item

        def run(values, weights):
            return forward(values, weights, length, blocks, global_list)
        result, pull = jax.vjp(run, one_input.astype(jnp.float32), params)
        grad_inputs, grad_params = pull(one_cotangent.astype(jnp.float32))
        totals = jax.tree.map(lambda first, second: first + second, totals, grad_params)
        return (totals, (result.astype(jnp.bfloat16), grad_inputs.astype(jnp.bfloat16)))
    zeros = jax.tree.map(jnp.zeros_like, params)
    totals, (layer_outputs, input_gradients) = lax.scan(per_item, zeros, (item_inputs, item_cotangents, item_lengths, rand_blocks, item_globals))
    layer_outputs = layer_outputs.reshape(PACKED_ROWS, ROW_TOKENS, MODEL_DIMENSION)
    input_gradients = input_gradients.reshape(PACKED_ROWS, ROW_TOKENS, MODEL_DIMENSION)
    return (layer_outputs, input_gradients, totals[0], totals[1], totals[2], totals[3], totals[4], totals[5], totals[6], totals[7], totals[8], totals[9], totals[10], totals[11])
```

```python
import functools

import jax
import jax.numpy as jnp
from jax import lax
from jax.experimental import pallas as pl
from jax.experimental.pallas import tpu as pltpu
from jax.sharding import PartitionSpec as P

HEADS = 16
BLK = 64
RAND = 3

norm_eps = 1e-05
masked_score = -1e30
low = jnp.bfloat16
full = jnp.float32


def matmul(left, right):
    return jnp.dot(left, right, preferred_element_type=full)


def matmul_left(left, right):
    return lax.dot_general(left, right, (((0,), (0,)), ((), ())), preferred_element_type=full)


def matmul_right(left, right):
    return lax.dot_general(left, right, (((1,), (1,)), ((), ())), preferred_element_type=full)


def normalize(values, ln_gain, ln_shift):
    average = jnp.mean(values, axis=-1, keepdims=True)
    centered = values - average
    variance = jnp.mean(centered * centered, axis=-1, keepdims=True)
    inverse = lax.rsqrt(variance + norm_eps)
    scaled = centered * inverse
    return (scaled * ln_gain + ln_shift, scaled, inverse)


def normalize_back(grad_normed, scaled, inverse, ln_gain):
    grad_scaled = grad_normed * ln_gain
    inner_mean = jnp.mean(grad_scaled, axis=-1, keepdims=True)
    along_mean = jnp.mean(grad_scaled * scaled, axis=-1, keepdims=True)
    return inverse * (grad_scaled - inner_mean - scaled * along_mean)


def key_list(step, block_count, total_blocks, lens, owners, offsets, globals_):
    length = lens[0, 0]
    ids = [step - 1, step, step + 1]
    ids += [owners[0, step, r] * block_count + offsets[0, step, r] for r in range(RAND)]
    ids += [globals_[0, 0, g] for g in range(globals_.shape[2])]
    starts, limits = [], []
    for block in ids:
        inside = jnp.logical_and(block >= 0, block < total_blocks)
        clamped = jnp.clip(block, 0, total_blocks - 1)
        starts.append(pl.multiple_of(clamped * BLK, BLK))
        limits.append(jnp.where(inside, length - clamped * BLK, 0))
    return starts, limits


def stack_heads(rows, lanes, head_count):
    if head_count == 1:
        return rows
    zero = jnp.zeros_like(rows)
    return jnp.concatenate([jnp.where(lanes == h, rows, zero) for h in range(head_count)], axis=0)


def merge_heads(stacked, lanes, head_count):
    merged = stacked[:BLK]
    for h in range(1, head_count):
        merged = jnp.where(lanes == h, stacked[h * BLK : (h + 1) * BLK], merged)
    return merged


def masked_scores(keys, query_rows, limits, inner_rows):
    score_values = matmul_right(keys, query_rows)
    parts = [
        jnp.where(inner_rows < limit, score_values[j * BLK : (j + 1) * BLK], masked_score)
        for j, limit in enumerate(limits)
    ]
    return jnp.concatenate(parts, axis=0)


def attend_kernel(
    block_count, head_count, scale, unroll, lens, owners, offsets, globals_, qkv, attended, log_total
):
    total_blocks = qkv.shape[0] // BLK
    width = qkv.shape[1] // 3
    lanes = lax.broadcasted_iota(jnp.int32, (BLK, width), 1) // (width // head_count)
    inner_rows = lax.broadcasted_iota(jnp.int32, (BLK, head_count * BLK), 0)

    def one(step):
        starts, limits = key_list(step, block_count, total_blocks, lens, owners, offsets, globals_)
        row = pl.multiple_of(step * BLK, BLK)
        queries = qkv[pl.ds(row, BLK), 0:width] * jnp.asarray(scale, low)
        query_rows = stack_heads(queries, lanes, head_count)
        keys = jnp.concatenate([qkv[pl.ds(s, BLK), width : 2 * width] for s in starts], axis=0)
        values = jnp.concatenate([qkv[pl.ds(s, BLK), 2 * width :] for s in starts], axis=0)
        score_values = masked_scores(keys, query_rows, limits, inner_rows)
        top = jnp.max(score_values, axis=0, keepdims=True)
        raised = jnp.exp(score_values - top)
        total = jnp.sum(raised, axis=0, keepdims=True)
        weights = (raised * (1.0 / total)).astype(low)
        result = matmul_left(weights, values)
        attended[pl.ds(row, BLK), :] = merge_heads(result, lanes, head_count).astype(low)
        log_total[step] = top + jnp.log(total)

    def body(index, carry):
        for part in range(unroll):
            one(index * unroll + part)
        return carry

    lax.fori_loop(0, total_blocks // unroll, body, 0)


def attend_back_kernel(
    block_count,
    head_count,
    scale,
    unroll,
    lens,
    owners,
    offsets,
    globals_,
    qkv,
    log_total,
    grad_attended,
    grad_qkv,
    key_sum,
    value_sum,
):
    total_blocks = qkv.shape[0] // BLK
    width = qkv.shape[1] // 3
    lanes = lax.broadcasted_iota(jnp.int32, (BLK, width), 1) // (width // head_count)
    inner_rows = lax.broadcasted_iota(jnp.int32, (BLK, head_count * BLK), 0)
    key_sum[...] = jnp.zeros_like(key_sum)
    value_sum[...] = jnp.zeros_like(value_sum)

    def one(step):
        starts, limits = key_list(step, block_count, total_blocks, lens, owners, offsets, globals_)
        row = pl.multiple_of(step * BLK, BLK)
        queries = qkv[pl.ds(row, BLK), 0:width] * jnp.asarray(scale, low)
        query_rows = stack_heads(queries, lanes, head_count)
        grad_rows = stack_heads(grad_attended[pl.ds(row, BLK), :], lanes, head_count)
        keys = jnp.concatenate([qkv[pl.ds(s, BLK), width : 2 * width] for s in starts], axis=0)
        values = jnp.concatenate([qkv[pl.ds(s, BLK), 2 * width :] for s in starts], axis=0)
        score_values = masked_scores(keys, query_rows, limits, inner_rows)
        probs = jnp.exp(score_values - log_total[step])
        grad_probs = matmul_right(values, grad_rows)
        correction = jnp.sum(probs * grad_probs, axis=0, keepdims=True)
        grad_scores = (probs * (grad_probs - correction)).astype(low)
        grad_keys = matmul(grad_scores, query_rows)
        grad_values = matmul(probs.astype(low), grad_rows)
        grad_queries = merge_heads(matmul_left(grad_scores, keys), lanes, head_count) * scale
        grad_qkv[pl.ds(row, BLK), 0:width] = grad_queries.astype(low)
        for j, s in enumerate(starts):
            key_sum[pl.ds(s, BLK), :] += grad_keys[j * BLK : (j + 1) * BLK]
            value_sum[pl.ds(s, BLK), :] += grad_values[j * BLK : (j + 1) * BLK]

    def body(index, carry):
        for part in range(unroll):
            one(index * unroll + part)
        return carry

    lax.fori_loop(0, total_blocks // unroll, body, 0)
    grad_qkv[:, width : 2 * width] = key_sum[...].astype(low)
    grad_qkv[:, 2 * width :] = value_sum[...].astype(low)


smem = pl.BlockSpec(memory_space=pltpu.SMEM)
vmem = pl.BlockSpec(memory_space=pltpu.VMEM)


def attend(tables, qkv, block_count, head_count, scale):
    rows, width = qkv.shape[0], qkv.shape[1] // 3
    total_blocks = rows // BLK
    return pl.pallas_call(
        functools.partial(attend_kernel, block_count, head_count, scale, 3),
        out_shape=(
            jax.ShapeDtypeStruct((rows, width), low),
            jax.ShapeDtypeStruct((total_blocks, 1, head_count * BLK), full),
        ),
        in_specs=[smem] * 4 + [vmem],
        out_specs=(vmem, vmem),
        compiler_params=pltpu.CompilerParams(vmem_limit_bytes=40 * 2**20),
        cost_estimate=pl.CostEstimate(
            flops=total_blocks * 4 * 128 * 128 * 512, bytes_accessed=rows * width * 8, transcendentals=0
        ),
        name="attend",
    )(*tables, qkv)


def attend_back(tables, qkv, log_total, grad_attended, block_count, head_count, scale):
    rows, width = qkv.shape[0], qkv.shape[1] // 3
    total_blocks = rows // BLK
    return pl.pallas_call(
        functools.partial(attend_back_kernel, block_count, head_count, scale, 2),
        out_shape=jax.ShapeDtypeStruct((rows, 3 * width), low),
        in_specs=[smem] * 4 + [vmem] * 3,
        out_specs=vmem,
        scratch_shapes=[pltpu.VMEM((rows, width), full)] * 2,
        compiler_params=pltpu.CompilerParams(vmem_limit_bytes=40 * 2**20),
        cost_estimate=pl.CostEstimate(
            flops=total_blocks * 10 * 128 * 128 * 512, bytes_accessed=rows * width * 16, transcendentals=0
        ),
        name="attend_back",
    )(*tables, qkv, log_total, grad_attended)


def swap(blocks, axes):
    return lax.all_to_all(blocks, axes, split_axis=0, concat_axis=0, tiled=True)


def gather_rows(rows):
    return lax.all_gather(rows, "seq", axis=0, tiled=True)


def shards(
    inputs,
    cotangent,
    lengths,
    rand_owners,
    rand_offsets,
    global_ids,
    ln1_gain,
    ln1_shift,
    w_query,
    w_key,
    w_value,
    w_out,
    ln2_gain,
    ln2_shift,
    w_in,
    b_in,
    w_back,
    b_back,
):
    seq_count = lax.axis_size("seq")
    batch_count = lax.axis_size("batch")
    device_count = seq_count * batch_count
    seq_index = lax.axis_index("seq")
    token_count = inputs.shape[1]
    model_width = inputs.shape[2]
    ff_width = w_in.shape[1]
    block_count = token_count // BLK
    head_dim = model_width // HEADS
    scale = head_dim ** (-0.5)
    total_tokens = seq_count * token_count
    head_groups = min(HEADS, seq_count)
    copies = seq_count // head_groups
    head_count = HEADS // head_groups
    width = head_count * head_dim
    tables = (lengths, rand_owners, rand_offsets, global_ids)

    def to_heads(*parts):
        split = [p.reshape(token_count, head_groups, width).transpose(1, 0, 2) for p in parts]
        joined = jnp.concatenate(split, axis=2)
        if copies > 1:
            joined = jnp.repeat(joined, copies, axis=0)
        received = swap(joined, "seq")
        return received.reshape(total_tokens, len(parts) * width)

    def to_tokens(rows, count):
        received = swap(rows.reshape(seq_count, token_count, count * width), "seq")
        received = received[::copies]
        return [
            received[:, :, i * width : (i + 1) * width].transpose(1, 0, 2).reshape(token_count, model_width)
            for i in range(count)
        ]

    gain_one = ln1_gain.astype(full)
    gain_two = ln2_gain.astype(full)
    grad_out = cotangent[0]
    grad_out_all = gather_rows(grad_out)
    residual_in = inputs[0].astype(full)
    normed, scaled_one, inverse_one = normalize(residual_in, gain_one, ln1_shift.astype(full))
    normed_low = normed.astype(low)
    normed_all = gather_rows(normed_low)
    qkv = to_heads(
        matmul(normed_low, w_query).astype(low),
        matmul(normed_low, w_key).astype(low),
        matmul(normed_low, w_value).astype(low),
    )
    attended_all, log_total = attend(tables, qkv, block_count, head_count, scale)
    (attended,) = to_tokens(attended_all, 1)
    middle = residual_in + matmul(attended, w_out)
    normed_two, scaled_two, inverse_two = normalize(middle, gain_two, ln2_shift.astype(full))
    normed_two_low = normed_two.astype(low)
    normed_two_all = gather_rows(normed_two_low)
    inner = matmul(normed_two_low, w_in) + b_in.astype(full)
    gelu = functools.partial(jax.nn.gelu, approximate=False)
    activated, gelu_pull = jax.vjp(gelu, inner)
    activated = activated.astype(low)
    output = (middle + matmul(activated, w_back) + b_back.astype(full)).astype(low)

    def to_columns(rows):
        columns = rows.shape[1] // seq_count
        split = rows.reshape(token_count, seq_count, columns).transpose(1, 0, 2)
        return swap(split, "seq").reshape(total_tokens, columns)

    activated_all = to_columns(activated)
    grad_w_back = matmul_left(activated_all, grad_out_all).astype(low)
    grad_out_full = grad_out.astype(full)
    grad_b_back = jnp.sum(grad_out_full, axis=0)
    grad_inner = gelu_pull(matmul_right(grad_out, w_back))[0].astype(low)
    grad_inner_all = to_columns(grad_inner)
    grad_w_in = matmul_left(normed_two_all, grad_inner_all).astype(low)
    grad_b_in = jnp.sum(grad_inner.astype(full), axis=0)
    grad_normed_two = matmul_right(grad_inner, w_in)
    grad_ln2_gain = jnp.sum(grad_normed_two * scaled_two, axis=0)
    grad_ln2_shift = jnp.sum(grad_normed_two, axis=0)
    grad_middle = grad_out_full + normalize_back(grad_normed_two, scaled_two, inverse_two, gain_two)
    grad_middle_low = grad_middle.astype(low)
    grad_attended = matmul_right(grad_middle_low, w_out).astype(low)
    grad_middle_all = gather_rows(grad_middle_low)
    out_rows = width // copies
    own_attended = lax.dynamic_slice_in_dim(attended_all, seq_index % copies * out_rows, out_rows, axis=1)
    grad_w_out = matmul_left(own_attended, grad_middle_all).astype(low)
    grad_qkv = attend_back(
        tables, qkv, log_total, to_heads(grad_attended), block_count, head_count, scale
    )
    grad_queries, grad_keys, grad_values = to_tokens(grad_qkv, 3)
    grad_w_qkv = matmul_left(normed_all, grad_qkv).astype(low)
    grad_normed = (
        matmul_right(grad_queries, w_query)
        + matmul_right(grad_keys, w_key)
        + matmul_right(grad_values, w_value)
    )
    grad_ln1_gain = jnp.sum(grad_normed * scaled_one, axis=0)
    grad_ln1_shift = jnp.sum(grad_normed, axis=0)
    input_grad = (
        grad_middle + normalize_back(grad_normed, scaled_one, inverse_one, gain_one)
    ).astype(low)

    both = ("seq", "batch")
    slim = model_width // device_count

    def rows_of(columns, count):
        received = swap(columns.reshape(device_count, slim, columns.shape[1]), both)
        received = received.reshape(seq_count, batch_count, slim, columns.shape[1])
        summed = jnp.sum(received[::count].astype(full), axis=1)
        return summed.transpose(1, 0, 2)

    in_rows = rows_of(grad_w_in, 1).reshape(slim, ff_width)
    qkv_rows = rows_of(grad_w_qkv, copies)
    qkv_rows = [
        qkv_rows[:, :, i * width : (i + 1) * width].reshape(slim, model_width) for i in range(3)
    ]
    back_out = lax.psum_scatter(
        jnp.concatenate(
            [
                grad_w_back.reshape(batch_count, -1, model_width),
                grad_w_out.reshape(batch_count, -1, model_width),
            ],
            axis=1,
        ),
        "batch",
        scatter_dimension=0,
        tiled=False,
    ).astype(full)
    back_rows = ff_width // device_count
    small = [grad_ln1_gain, grad_ln1_shift, grad_ln2_gain, grad_ln2_shift, grad_b_back, grad_b_in]
    packed = jnp.concatenate([v.reshape(device_count, -1) for v in small], axis=1)
    packed = jnp.sum(swap(packed, both), axis=0)
    cuts, at = [], 0
    for v in small:
        size = v.shape[0] // device_count
        cuts.append(packed[at : at + size])
        at += size
    return (
        output[None],
        input_grad[None],
        cuts[0],
        cuts[1],
        qkv_rows[0],
        qkv_rows[1],
        qkv_rows[2],
        back_out[back_rows:],
        cuts[2],
        cuts[3],
        in_rows,
        cuts[5],
        back_out[:back_rows],
        cuts[4],
    )


def solution(mesh):
    rows = P("batch", "seq", None)
    table = P("batch", None, None)
    thin = P(("seq", "batch"))
    wide = P(("seq", "batch"), None)
    return jax.shard_map(
        shards,
        mesh=mesh,
        in_specs=(rows, rows, P("batch", None), table, table, table) + (P(),) * 12,
        out_specs=(rows, rows, thin, thin, wide, wide, wide, wide, thin, thin, wide, thin, wide, thin),
        check_vma=False,
    )
```

```python
import functools

import jax
import jax.numpy as jnp
from jax import lax
from jax.experimental import pallas as pl
from jax.experimental.pallas import tpu as pltpu
from jax.sharding import PartitionSpec as P

HEADS = 16
BLK = 64
RAND = 3

norm_eps = 1e-05
masked_score = -1e30
low = jnp.bfloat16
full = jnp.float32


def matmul(left, right):
    return jnp.dot(left, right, preferred_element_type=full)


def matmul_left(left, right):
    return lax.dot_general(left, right, (((0,), (0,)), ((), ())), preferred_element_type=full)


def matmul_right(left, right):
    return lax.dot_general(left, right, (((1,), (1,)), ((), ())), preferred_element_type=full)


def normalize_back(grad_normed, scaled, inverse, ln_gain):
    grad_scaled = grad_normed * ln_gain
    inner_mean = jnp.mean(grad_scaled, axis=-1, keepdims=True)
    along_mean = jnp.mean(grad_scaled * scaled, axis=-1, keepdims=True)
    return inverse * (grad_scaled - inner_mean - scaled * along_mean)


def key_list(step, block_count, total_blocks, lens, owners, offsets, globals_):
    length = lens[0, 0]
    ids = [step - 1, step, step + 1]
    ids += [owners[0, step, r] * block_count + offsets[0, step, r] for r in range(RAND)]
    ids += [globals_[0, 0, g] for g in range(globals_.shape[2])]
    starts, limits = [], []
    for block in ids:
        inside = jnp.logical_and(block >= 0, block < total_blocks)
        clamped = jnp.clip(block, 0, total_blocks - 1)
        starts.append(pl.multiple_of(clamped * BLK, BLK))
        limits.append(jnp.where(inside, length - clamped * BLK, 0))
    return starts, limits


def stack_heads(rows, lanes, head_count):
    if head_count == 1:
        return rows
    zero = jnp.zeros_like(rows)
    return jnp.concatenate([jnp.where(lanes == h, rows, zero) for h in range(head_count)], axis=0)


def merge_heads(stacked, lanes, head_count):
    merged = stacked[:BLK]
    for h in range(1, head_count):
        merged = jnp.where(lanes == h, stacked[h * BLK : (h + 1) * BLK], merged)
    return merged


def masked_scores(keys, query_rows, limits, inner_rows):
    score_values = matmul_right(keys, query_rows)
    parts = [
        jnp.where(inner_rows < limit, score_values[j * BLK : (j + 1) * BLK], masked_score)
        for j, limit in enumerate(limits)
    ]
    return jnp.concatenate(parts, axis=0)


def attend_kernel(
    block_count, head_count, scale, unroll, lens, owners, offsets, globals_, qkv, attended, log_total
):
    total_blocks = qkv.shape[0] // BLK
    width = qkv.shape[1] // 3
    lanes = lax.broadcasted_iota(jnp.int32, (BLK, width), 1) // (width // head_count)
    inner_rows = lax.broadcasted_iota(jnp.int32, (BLK, head_count * BLK), 0)

    def one(step):
        starts, limits = key_list(step, block_count, total_blocks, lens, owners, offsets, globals_)
        row = pl.multiple_of(step * BLK, BLK)
        queries = qkv[pl.ds(row, BLK), 0:width] * jnp.asarray(scale, low)
        query_rows = stack_heads(queries, lanes, head_count)
        keys = jnp.concatenate([qkv[pl.ds(s, BLK), width : 2 * width] for s in starts], axis=0)
        values = jnp.concatenate([qkv[pl.ds(s, BLK), 2 * width :] for s in starts], axis=0)
        score_values = masked_scores(keys, query_rows, limits, inner_rows)
        top = jnp.max(score_values, axis=0, keepdims=True)
        raised = jnp.exp(score_values - top)
        total = jnp.sum(raised, axis=0, keepdims=True)
        weights = (raised * (1.0 / total)).astype(low)
        result = matmul_left(weights, values)
        attended[pl.ds(row, BLK), :] = merge_heads(result, lanes, head_count).astype(low)
        log_total[step] = top + jnp.log(total)

    def body(index, carry):
        for part in range(unroll):
            one(index * unroll + part)
        return carry

    lax.fori_loop(0, total_blocks // unroll, body, 0)


def attend_back_kernel(
    block_count,
    head_count,
    scale,
    unroll,
    lens,
    owners,
    offsets,
    globals_,
    qkv,
    log_total,
    grad_attended,
    grad_qkv,
    key_sum,
    value_sum,
):
    total_blocks = qkv.shape[0] // BLK
    width = qkv.shape[1] // 3
    lanes = lax.broadcasted_iota(jnp.int32, (BLK, width), 1) // (width // head_count)
    inner_rows = lax.broadcasted_iota(jnp.int32, (BLK, head_count * BLK), 0)
    key_sum[...] = jnp.zeros_like(key_sum)
    value_sum[...] = jnp.zeros_like(value_sum)

    def one(step):
        starts, limits = key_list(step, block_count, total_blocks, lens, owners, offsets, globals_)
        row = pl.multiple_of(step * BLK, BLK)
        queries = qkv[pl.ds(row, BLK), 0:width] * jnp.asarray(scale, low)
        query_rows = stack_heads(queries, lanes, head_count)
        grad_rows = stack_heads(grad_attended[pl.ds(row, BLK), :], lanes, head_count)
        keys = jnp.concatenate([qkv[pl.ds(s, BLK), width : 2 * width] for s in starts], axis=0)
        values = jnp.concatenate([qkv[pl.ds(s, BLK), 2 * width :] for s in starts], axis=0)
        score_values = masked_scores(keys, query_rows, limits, inner_rows)
        probs = jnp.exp(score_values - log_total[step])
        grad_probs = matmul_right(values, grad_rows)
        correction = jnp.sum(probs * grad_probs, axis=0, keepdims=True)
        grad_scores = (probs * (grad_probs - correction)).astype(low)
        grad_keys = matmul(grad_scores, query_rows)
        grad_values = matmul(probs.astype(low), grad_rows)
        grad_queries = merge_heads(matmul_left(grad_scores, keys), lanes, head_count) * scale
        grad_qkv[pl.ds(row, BLK), 0:width] = grad_queries.astype(low)
        for j, s in enumerate(starts):
            key_sum[pl.ds(s, BLK), :] += grad_keys[j * BLK : (j + 1) * BLK]
            value_sum[pl.ds(s, BLK), :] += grad_values[j * BLK : (j + 1) * BLK]

    def body(index, carry):
        for part in range(unroll):
            one(index * unroll + part)
        return carry

    lax.fori_loop(0, total_blocks // unroll, body, 0)
    grad_qkv[:, width : 2 * width] = key_sum[...].astype(low)
    grad_qkv[:, 2 * width :] = value_sum[...].astype(low)


smem = pl.BlockSpec(memory_space=pltpu.SMEM)
vmem = pl.BlockSpec(memory_space=pltpu.VMEM)


def attend(tables, qkv, block_count, head_count, scale):
    rows, width = qkv.shape[0], qkv.shape[1] // 3
    total_blocks = rows // BLK
    return pl.pallas_call(
        functools.partial(attend_kernel, block_count, head_count, scale, 3),
        out_shape=(
            jax.ShapeDtypeStruct((rows, width), low),
            jax.ShapeDtypeStruct((total_blocks, 1, head_count * BLK), full),
        ),
        in_specs=[smem] * 4 + [vmem],
        out_specs=(vmem, vmem),
        compiler_params=pltpu.CompilerParams(vmem_limit_bytes=40 * 2**20),
        cost_estimate=pl.CostEstimate(
            flops=total_blocks * 4 * 128 * 128 * 512, bytes_accessed=rows * width * 8, transcendentals=0
        ),
        name="attend",
    )(*tables, qkv)


def attend_back(tables, qkv, log_total, grad_attended, block_count, head_count, scale):
    rows, width = qkv.shape[0], qkv.shape[1] // 3
    total_blocks = rows // BLK
    return pl.pallas_call(
        functools.partial(attend_back_kernel, block_count, head_count, scale, 2),
        out_shape=jax.ShapeDtypeStruct((rows, 3 * width), low),
        in_specs=[smem] * 4 + [vmem] * 3,
        out_specs=vmem,
        scratch_shapes=[pltpu.VMEM((rows, width), full)] * 2,
        compiler_params=pltpu.CompilerParams(vmem_limit_bytes=40 * 2**20),
        cost_estimate=pl.CostEstimate(
            flops=total_blocks * 10 * 128 * 128 * 512, bytes_accessed=rows * width * 16, transcendentals=0
        ),
        name="attend_back",
    )(*tables, qkv, log_total, grad_attended)


def row_stats(values):
    average = jnp.mean(values, axis=-1, keepdims=True)
    centered = values - average
    variance = jnp.mean(centered * centered, axis=-1, keepdims=True)
    inverse = lax.rsqrt(variance + norm_eps)
    return centered * inverse, inverse


def project_kernel(width, inputs, grad_out, gain, shift, w_query, w_key, w_value, sent, kept):
    model = inputs.shape[1]

    @pl.when(pl.program_id(0) == 0)
    def _():
        scaled, _ = row_stats(inputs[...].astype(full))
        normed = scaled * gain[...].astype(full) + shift[...].astype(full)
        kept[:, :model] = normed.astype(low)
        kept[:, model:] = grad_out[...]

    rows = kept[:, :model]
    for part, weight in enumerate((w_query, w_key, w_value)):
        result = matmul(rows, weight[...]).astype(low)
        for i in range(sent.shape[0]):
            sent[i, :, part * width : (part + 1) * width] = result[:, i * width : (i + 1) * width]


def project(inputs, grad_out, gain, shift, w_query, w_key, w_value, groups, width):
    tokens, model = inputs.shape
    columns = 256
    per_step = columns // width
    weight = pl.BlockSpec((model, columns), lambda j: (0, j))
    row = pl.BlockSpec((1, model), lambda j: (0, 0))
    whole = pl.BlockSpec((tokens, model), lambda j: (0, 0))
    return pl.pallas_call(
        functools.partial(project_kernel, width),
        grid=(model // columns,),
        out_shape=(
            jax.ShapeDtypeStruct((groups, tokens, 3 * width), low),
            jax.ShapeDtypeStruct((tokens, 2 * model), low),
        ),
        in_specs=[whole, whole, row, row, weight, weight, weight],
        out_specs=(
            pl.BlockSpec((per_step, tokens, 3 * width), lambda j: (j, 0, 0)),
            pl.BlockSpec((tokens, 2 * model), lambda j: (0, 0)),
        ),
        compiler_params=pltpu.CompilerParams(vmem_limit_bytes=58 * 2**20),
        cost_estimate=pl.CostEstimate(
            flops=6 * tokens * model * model, bytes_accessed=6 * model * model, transcendentals=0
        ),
        name="project",
    )(inputs, grad_out, gain, shift, w_query, w_key, w_value)


def project_back_kernel(
    width, inputs, gain, grad_middle, received, w_query, w_key, w_value, input_grad, gain_grads, total
):
    step = pl.program_id(0)

    @pl.when(step == 0)
    def _():
        total[...] = jnp.zeros_like(total)

    result = total[...]
    for part, weight in enumerate((w_query, w_key, w_value)):
        pieces = [
            received[i, :, part * width : (part + 1) * width] for i in range(received.shape[0])
        ]
        result += matmul_right(jnp.concatenate(pieces, axis=1), weight[...])
    total[...] = result

    @pl.when(step == pl.num_programs(0) - 1)
    def _():
        grad_normed = total[...]
        scaled, inverse = row_stats(inputs[...].astype(full))
        back = normalize_back(grad_normed, scaled, inverse, gain[...].astype(full))
        input_grad[...] = (grad_middle[...] + back).astype(low)
        gain_grads[0:1, :] = jnp.sum(grad_normed * scaled, axis=0, keepdims=True)
        gain_grads[1:2, :] = jnp.sum(grad_normed, axis=0, keepdims=True)


def project_back(inputs, gain, grad_middle, received, w_query, w_key, w_value):
    tokens, model = inputs.shape
    columns = 256
    width = received.shape[2] // 3
    per_step = columns // width
    weight = pl.BlockSpec((model, columns), lambda j: (0, j))
    row = pl.BlockSpec((1, model), lambda j: (0, 0))
    whole = pl.BlockSpec((tokens, model), lambda j: (0, 0))
    return pl.pallas_call(
        functools.partial(project_back_kernel, width),
        grid=(model // columns,),
        out_shape=(
            jax.ShapeDtypeStruct((tokens, model), low),
            jax.ShapeDtypeStruct((2, model), full),
        ),
        in_specs=[
            whole,
            row,
            whole,
            pl.BlockSpec((per_step, tokens, 3 * width), lambda j: (j, 0, 0)),
            weight,
            weight,
            weight,
        ],
        out_specs=(whole, pl.BlockSpec((2, model), lambda j: (0, 0))),
        scratch_shapes=[pltpu.VMEM((tokens, model), full)],
        compiler_params=pltpu.CompilerParams(vmem_limit_bytes=58 * 2**20),
        cost_estimate=pl.CostEstimate(
            flops=6 * tokens * model * model, bytes_accessed=6 * model * model, transcendentals=0
        ),
        name="project_back",
    )(inputs, gain, grad_middle, received, w_query, w_key, w_value)


def middle_kernel(received, inputs, w_out, gain, shift, middle, normed, attended):
    attended[...] = jnp.concatenate([received[i] for i in range(received.shape[0])], axis=1)
    rows = inputs[...].astype(full) + matmul(attended[...], w_out[...])
    middle[...] = rows
    unit, _ = row_stats(rows)
    normed[...] = (unit * gain[...].astype(full) + shift[...].astype(full)).astype(low)


def attend_out(received, inputs, w_out, gain, shift):
    tokens, model = inputs.shape
    return pl.pallas_call(
        middle_kernel,
        out_shape=(
            jax.ShapeDtypeStruct((tokens, model), full),
            jax.ShapeDtypeStruct((tokens, model), low),
            jax.ShapeDtypeStruct((tokens, model), low),
        ),
        in_specs=[vmem] * 5,
        out_specs=(vmem, vmem, vmem),
        compiler_params=pltpu.CompilerParams(vmem_limit_bytes=24 * 2**20),
        cost_estimate=pl.CostEstimate(
            flops=2 * tokens * model * model, bytes_accessed=2 * model * model, transcendentals=0
        ),
        name="attend_out",
    )(received, inputs, w_out, gain, shift)


def hidden(normed, grad_out, w_in, b_in, w_back):
    inner = matmul(normed, w_in) + b_in.astype(full)
    share = 0.5 * (1.0 + lax.erf(inner * 0.7071067811865476))
    density = jnp.exp(inner * inner * -0.5) * 0.3989422804014327
    grad_active = matmul_right(grad_out, w_back)
    grads = (grad_active * (share + inner * density)).astype(low)
    return (inner * share).astype(low), grads


def feed_kernel(
    normed,
    middle,
    grad_out,
    w_out,
    gain,
    b_back,
    w_in,
    b_in,
    w_back,
    output,
    grad_middle,
    grad_middle_low,
    grad_attended,
    gain_grads,
    b_in_grad,
    out_total,
    grad_total,
):
    step = pl.program_id(0)
    groups, _, width = grad_attended.shape

    @pl.when(step == 0)
    def _():
        out_total[...] = middle[...] + b_back[...].astype(full)
        grad_total[...] = jnp.zeros_like(grad_total)

    active, grads = hidden(normed[...], grad_out[...], w_in[...], b_in[...], w_back[...])
    b_in_grad[...] = jnp.sum(grads.astype(full), axis=0, keepdims=True)
    out_total[...] += matmul(active, w_back[...])
    grad_total[...] += matmul_right(grads, w_in[...])

    @pl.when(step == pl.num_programs(0) - 1)
    def _():
        output[...] = out_total[...].astype(low)
        grad_normed = grad_total[...]
        unit, rate = row_stats(middle[...])
        grad_full = grad_out[...].astype(full)
        back = normalize_back(grad_normed, unit, rate, gain[...].astype(full))
        grads_middle = grad_full + back
        grad_middle[...] = grads_middle
        grads_low = grads_middle.astype(low)
        grad_middle_low[...] = grads_low
        result = matmul_right(grads_low, w_out[...]).astype(low)
        for i in range(groups):
            grad_attended[i] = result[:, i * width : (i + 1) * width]
        gain_grads[0:1, :] = jnp.sum(grad_normed * unit, axis=0, keepdims=True)
        gain_grads[1:2, :] = jnp.sum(grad_normed, axis=0, keepdims=True)
        gain_grads[2:3, :] = jnp.sum(grad_full, axis=0, keepdims=True)


def feed(normed, middle, grad_out, w_out, gain, b_back, w_in, b_in, w_back, groups, width):
    tokens, model = normed.shape
    ff = w_in.shape[1]
    columns = 512
    row = pl.BlockSpec((1, model), lambda j: (0, 0))
    whole = pl.BlockSpec((tokens, model), lambda j: (0, 0))
    heads = pl.BlockSpec((groups, tokens, width), lambda j: (0, 0, 0))
    return pl.pallas_call(
        feed_kernel,
        grid=(ff // columns,),
        out_shape=(
            jax.ShapeDtypeStruct((tokens, model), low),
            jax.ShapeDtypeStruct((tokens, model), full),
            jax.ShapeDtypeStruct((tokens, model), low),
            jax.ShapeDtypeStruct((groups, tokens, width), low),
            jax.ShapeDtypeStruct((3, model), full),
            jax.ShapeDtypeStruct((1, ff), full),
        ),
        in_specs=[
            whole,
            whole,
            whole,
            pl.BlockSpec((model, model), lambda j: (0, 0), pipeline_mode=pl.Buffered(1)),
            row,
            row,
            pl.BlockSpec((model, columns), lambda j: (0, j)),
            pl.BlockSpec((1, columns), lambda j: (0, j)),
            pl.BlockSpec((columns, model), lambda j: (j, 0)),
        ],
        out_specs=(
            whole,
            whole,
            whole,
            heads,
            pl.BlockSpec((3, model), lambda j: (0, 0)),
            pl.BlockSpec((1, columns), lambda j: (0, j)),
        ),
        scratch_shapes=[pltpu.VMEM((tokens, model), full)] * 2,
        compiler_params=pltpu.CompilerParams(vmem_limit_bytes=48 * 2**20),
        cost_estimate=pl.CostEstimate(
            flops=8 * tokens * model * ff, bytes_accessed=4 * model * ff, transcendentals=0
        ),
        name="feed",
    )(normed, middle, grad_out, w_out, gain, b_back, w_in, b_in, w_back)


def pick_blocks(index, total, sent, own, other):
    def block(distance):
        return total[:, pl.ds(index ^ distance, 1)][:, 0].astype(low)

    sent[0] = block(1)
    sent[1] = block(3)
    own[...] = block(0)
    other[...] = block(2)


def picked_shapes(outer, rows, columns):
    shape = (outer, rows, columns)
    return [jax.ShapeDtypeStruct((2,) + shape, low)] + [jax.ShapeDtypeStruct(shape, low)] * 2


def picked_specs(outer, rows, columns):
    whole = pl.BlockSpec((outer, rows, columns), lambda j, places: (0, 0, 0))
    return [pl.BlockSpec((2, outer, rows, columns), lambda j, places: (0, 0, 0, 0)), whole, whole]


def product_kernel(places, left, right, sent, own, other, total):
    step = pl.program_id(0)

    @pl.when(step == 0)
    def _():
        total[...] = jnp.zeros_like(total)

    total[...] += matmul_left(left[...], right[...]).reshape(total.shape)

    @pl.when(step == pl.num_programs(0) - 1)
    def _():
        pick_blocks(places[1], total, sent, own, other)


def product(places, left, left_columns, right, outer, name):
    tokens, columns = right.shape
    chunk = min(512, tokens)
    rows = left_columns // (4 * outer)
    return pl.pallas_call(
        product_kernel,
        grid_spec=pltpu.PrefetchScalarGridSpec(
            num_scalar_prefetch=1,
            grid=(tokens // chunk,),
            in_specs=[
                pl.BlockSpec((chunk, left_columns), lambda j, places: (j, 0)),
                pl.BlockSpec((chunk, columns), lambda j, places: (j, 0)),
            ],
            out_specs=picked_specs(outer, rows, columns),
            scratch_shapes=[pltpu.VMEM((outer, 4, rows, columns), full)],
        ),
        out_shape=picked_shapes(outer, rows, columns),
        compiler_params=pltpu.CompilerParams(vmem_limit_bytes=40 * 2**20),
        cost_estimate=pl.CostEstimate(
            flops=2 * tokens * left_columns * columns,
            bytes_accessed=2 * tokens * (left_columns + columns),
            transcendentals=0,
        ),
        name=name,
    )(places, left, right)


def feed_products_kernel(
    places,
    normed,
    grad_out,
    w_in,
    b_in,
    w_back,
    in_sent,
    in_own,
    in_other,
    back_sent,
    back_own,
    back_other,
    in_total,
    back_total,
):
    step = pl.program_id(0)

    @pl.when(step == 0)
    def _():
        in_total[...] = jnp.zeros_like(in_total)
        back_total[...] = jnp.zeros_like(back_total)

    active, grads = hidden(normed[...], grad_out[...], w_in[...], b_in[...], w_back[...])
    in_total[...] += matmul_left(normed[...], grads).reshape(in_total.shape)
    back_total[...] += matmul_left(active, grad_out[...]).reshape(back_total.shape)

    @pl.when(step == pl.num_programs(0) - 1)
    def _():
        pick_blocks(places[1], in_total, in_sent, in_own, in_other)
        pick_blocks(places[1], back_total, back_sent, back_own, back_other)


def feed_products(places, normed, kept, w_in, b_in, w_back, seq_count):
    tokens, model = normed.shape
    columns = w_in.shape[1] // seq_count
    chunk = 512
    slim = model // (4 * seq_count)
    back_slim = columns // 4
    return pl.pallas_call(
        feed_products_kernel,
        grid_spec=pltpu.PrefetchScalarGridSpec(
            num_scalar_prefetch=1,
            grid=(tokens // chunk,),
            in_specs=[
                pl.BlockSpec((chunk, model), lambda j, places: (j, 0)),
                pl.BlockSpec((chunk, model), lambda j, places: (j, 1)),
                pl.BlockSpec((model, columns), lambda j, places: (0, places[0])),
                pl.BlockSpec((1, columns), lambda j, places: (0, places[0])),
                pl.BlockSpec((columns, model), lambda j, places: (places[0], 0)),
            ],
            out_specs=picked_specs(seq_count, slim, columns) + picked_specs(1, back_slim, model),
            scratch_shapes=[
                pltpu.VMEM((seq_count, 4, slim, columns), full),
                pltpu.VMEM((1, 4, back_slim, model), full),
            ],
        ),
        out_shape=picked_shapes(seq_count, slim, columns) + picked_shapes(1, back_slim, model),
        compiler_params=pltpu.CompilerParams(vmem_limit_bytes=48 * 2**20),
        cost_estimate=pl.CostEstimate(
            flops=8 * tokens * model * columns,
            bytes_accessed=4 * tokens * model + 4 * model * columns,
            transcendentals=0,
        ),
        name="feed_products",
    )(places, normed, kept, w_in, b_in, w_back)


def swap(blocks, axes):
    return lax.all_to_all(blocks, axes, split_axis=0, concat_axis=0, tiled=True)


def gather_rows(rows, axis):
    return lax.all_gather(rows, axis, axis=0, tiled=True)


def trade(block, distance):
    return lax.ppermute(block, "batch", [(i, i ^ distance) for i in range(4)])


def first_sum(got, own, other):
    own = own.astype(full) + got[0].astype(full)
    other = (other.astype(full) + got[1].astype(full)).astype(low)
    return own, other


def together(*values):
    return lax.optimization_barrier(values)


def shards(
    inputs,
    cotangent,
    lengths,
    rand_owners,
    rand_offsets,
    global_ids,
    ln1_gain,
    ln1_shift,
    w_query,
    w_key,
    w_value,
    w_out,
    ln2_gain,
    ln2_shift,
    w_in,
    b_in,
    w_back,
    b_back,
):
    seq_count = lax.axis_size("seq")
    batch_count = lax.axis_size("batch")
    device_count = seq_count * batch_count
    token_count = inputs.shape[1]
    model_width = inputs.shape[2]
    ff_width = w_in.shape[1]
    block_count = token_count // BLK
    head_dim = model_width // HEADS
    scale = head_dim ** (-0.5)
    total_tokens = seq_count * token_count
    head_groups = min(HEADS, seq_count)
    copies = seq_count // head_groups
    head_count = HEADS // head_groups
    width = head_count * head_dim
    tables = (lengths, rand_owners, rand_offsets, global_ids)

    def to_heads(sent):
        if copies > 1:
            sent = jnp.repeat(sent, copies, axis=0)
        return swap(sent, "seq").reshape(total_tokens, -1)

    def to_tokens(rows):
        return swap(rows.reshape(seq_count, token_count, -1), "seq")[::copies]

    def one_row(vector):
        return vector.reshape(1, -1)

    rows_in, grad_out = inputs[0], cotangent[0]
    gain_one, gain_two = one_row(ln1_gain), one_row(ln2_gain)
    places = jnp.stack([lax.axis_index("seq"), lax.axis_index("batch")]).astype(jnp.int32)
    sent, kept = project(
        rows_in, grad_out, gain_one, one_row(ln1_shift), w_query, w_key, w_value, head_groups, width
    )
    qkv, kept = together(to_heads(sent), kept)
    kept_all = gather_rows(kept, "seq")
    attended_all, log_total = attend(tables, qkv, block_count, head_count, scale)
    middle, normed_two, attended = attend_out(
        to_tokens(attended_all), rows_in, w_out, gain_two, one_row(ln2_shift)
    )
    normed_two_all = gather_rows(normed_two, "seq")
    output, grad_middle, grad_middle_low, grad_attended, gain_two_grads, grad_b_in = feed(
        normed_two,
        middle,
        grad_out,
        w_out,
        gain_two,
        one_row(b_back),
        w_in,
        one_row(b_in),
        w_back,
        head_groups,
        width,
    )
    out_blocks = product(places, attended, model_width, grad_middle_low, seq_count, "out_product")
    grad_rows, out_blocks = together(to_heads(grad_attended), out_blocks)
    out_got = trade(out_blocks[0], 1)
    grad_qkv = attend_back(tables, qkv, log_total, grad_rows, block_count, head_count, scale)
    out_own, out_other = first_sum(out_got, *out_blocks[1:])
    out_last = trade(out_other, 2)
    grad_qkv_near = to_tokens(grad_qkv)

    slim = model_width // device_count
    inner_columns = ff_width // seq_count
    qkv_blocks = product(places, kept_all, model_width, grad_qkv, seq_count, "qkv_product")
    qkv_got = trade(qkv_blocks[0], 1)
    in_sent, in_own, in_other, back_sent, back_own, back_other = feed_products(
        places, normed_two_all, kept_all, w_in, one_row(b_in), w_back, seq_count
    )
    qkv_got, grad_qkv_near, in_sent, back_sent, out_last = together(
        qkv_got, grad_qkv_near, in_sent, back_sent, out_last
    )
    qkv_own, qkv_other = first_sum(qkv_got, *qkv_blocks[1:])
    qkv_last = trade(qkv_other, 2)
    in_got = trade(in_sent, 1)
    back_got = trade(back_sent, 1)
    input_grad, gain_one_grads = project_back(
        rows_in, gain_one, grad_middle, grad_qkv_near, w_query, w_key, w_value
    )
    in_got, back_got, qkv_last, gain_one_grads = together(in_got, back_got, qkv_last, gain_one_grads)
    in_own, in_other = first_sum(in_got, in_own, in_other)
    in_last = trade(in_other, 2)
    back_own, back_other = first_sum(back_got, back_own, back_other)
    back_rows = (back_own + trade(back_other, 2).astype(full))[0]

    mixed = [
        (own + last.astype(full)).astype(low)
        for own, last in ((in_own, in_last), (qkv_own, qkv_last), (out_own, out_last))
    ]
    mixed = swap(jnp.concatenate(mixed, axis=2), "seq")
    at = inner_columns + 3 * width
    in_rows = mixed[:, :, :inner_columns].transpose(1, 0, 2).reshape(slim, ff_width).astype(full)
    qkv_rows = mixed[::copies, :, inner_columns:at].transpose(1, 0, 2).astype(full)
    qkv_rows = [
        qkv_rows[:, :, i * width : (i + 1) * width].reshape(slim, model_width) for i in range(3)
    ]
    out_rows = jnp.sum(mixed[:, :, at:].astype(full), axis=0)
    small = [gain_one_grads[0], gain_one_grads[1], *gain_two_grads, grad_b_in[0]]
    packed = jnp.concatenate([v.reshape(device_count, -1) for v in small], axis=1)
    packed = jnp.sum(swap(packed, ("seq", "batch")), axis=0)
    cuts, at = [], 0
    for v in small:
        size = v.shape[0] // device_count
        cuts.append(packed[at : at + size])
        at += size
    return (
        output[None],
        input_grad[None],
        cuts[0],
        cuts[1],
        qkv_rows[0],
        qkv_rows[1],
        qkv_rows[2],
        out_rows,
        cuts[2],
        cuts[3],
        in_rows,
        cuts[5],
        back_rows,
        cuts[4],
    )


def solution(mesh):
    rows = P("batch", "seq", None)
    table = P("batch", None, None)
    thin = P(("seq", "batch"))
    wide = P(("seq", "batch"), None)
    return jax.shard_map(
        shards,
        mesh=mesh,
        in_specs=(rows, rows, P("batch", None), table, table, table) + (P(),) * 12,
        out_specs=(rows, rows, thin, thin, wide, wide, wide, wide, thin, thin, wide, thin, wide, thin),
        check_vma=False,
    )
```

```python
import functools

import jax
import jax.numpy as jnp
from jax import lax
from jax.experimental import pallas as pl
from jax.experimental.pallas import tpu as pltpu
from jax.sharding import PartitionSpec as P

HEADS = 16
BLK = 64
RAND = 3

norm_eps = 1e-05
masked_score = -1e30
vmem_limit = 60 * 2**20
low = jnp.bfloat16
full = jnp.float32


def matmul(left, right):
    return jnp.dot(left, right, preferred_element_type=full)


def matmul_left(left, right):
    return lax.dot_general(left, right, (((0,), (0,)), ((), ())), preferred_element_type=full)


def matmul_right(left, right):
    return lax.dot_general(left, right, (((1,), (1,)), ((), ())), preferred_element_type=full)


def normalize_back(grad_normed, scaled, inverse, ln_gain):
    grad_scaled = grad_normed * ln_gain
    inner_mean = jnp.mean(grad_scaled, axis=-1, keepdims=True)
    along_mean = jnp.mean(grad_scaled * scaled, axis=-1, keepdims=True)
    return inverse * (grad_scaled - inner_mean - scaled * along_mean)


def key_list(step, block_count, total_blocks, lens, owners, offsets, globals_):
    length = lens[0, 0]
    ids = [step - 1, step, step + 1]
    ids += [owners[0, step, r] * block_count + offsets[0, step, r] for r in range(RAND)]
    ids += [globals_[0, 0, g] for g in range(globals_.shape[2])]
    starts, limits = [], []
    for block in ids:
        inside = jnp.logical_and(block >= 0, block < total_blocks)
        clamped = jnp.clip(block, 0, total_blocks - 1)
        starts.append(pl.multiple_of(clamped * BLK, BLK))
        limits.append(jnp.where(inside, length - clamped * BLK, 0))
    return starts, limits


def stack_heads(rows, lanes, head_count):
    if head_count == 1:
        return rows
    zero = jnp.zeros_like(rows)
    return jnp.concatenate([jnp.where(lanes == h, rows, zero) for h in range(head_count)], axis=0)


def merge_heads(stacked, lanes, head_count):
    merged = stacked[:BLK]
    for h in range(1, head_count):
        merged = jnp.where(lanes == h, stacked[h * BLK : (h + 1) * BLK], merged)
    return merged


def masked_scores(keys, query_rows, limits, inner_rows):
    score_values = matmul_right(keys, query_rows)
    parts = [
        jnp.where(inner_rows < limit, score_values[j * BLK : (j + 1) * BLK], masked_score)
        for j, limit in enumerate(limits)
    ]
    return jnp.concatenate(parts, axis=0)


def attend_kernel(
    block_count, head_count, scale, unroll, lens, owners, offsets, globals_, qkv, attended, log_total
):
    total_blocks = qkv.shape[0] // BLK
    width = qkv.shape[1] // 3
    lanes = lax.broadcasted_iota(jnp.int32, (BLK, width), 1) // (width // head_count)
    inner_rows = lax.broadcasted_iota(jnp.int32, (BLK, head_count * BLK), 0)

    def one(step):
        starts, limits = key_list(step, block_count, total_blocks, lens, owners, offsets, globals_)
        row = pl.multiple_of(step * BLK, BLK)
        queries = qkv[pl.ds(row, BLK), 0:width] * jnp.asarray(scale, low)
        query_rows = stack_heads(queries, lanes, head_count)
        keys = jnp.concatenate([qkv[pl.ds(s, BLK), width : 2 * width] for s in starts], axis=0)
        values = jnp.concatenate([qkv[pl.ds(s, BLK), 2 * width :] for s in starts], axis=0)
        score_values = masked_scores(keys, query_rows, limits, inner_rows)
        top = jnp.max(score_values, axis=0, keepdims=True)
        raised = jnp.exp(score_values - top)
        total = jnp.sum(raised, axis=0, keepdims=True)
        weights = (raised * (1.0 / total)).astype(low)
        result = matmul_left(weights, values)
        attended[pl.ds(row, BLK), :] = merge_heads(result, lanes, head_count).astype(low)
        log_total[step] = top + jnp.log(total)

    def body(index, carry):
        for part in range(unroll):
            one(index * unroll + part)
        return carry

    lax.fori_loop(0, total_blocks // unroll, body, 0)


def attend_back_kernel(
    block_count,
    head_count,
    scale,
    unroll,
    lens,
    owners,
    offsets,
    globals_,
    qkv,
    log_total,
    grad_attended,
    grad_qkv,
    key_sum,
    value_sum,
):
    total_blocks = qkv.shape[0] // BLK
    width = qkv.shape[1] // 3
    lanes = lax.broadcasted_iota(jnp.int32, (BLK, width), 1) // (width // head_count)
    inner_rows = lax.broadcasted_iota(jnp.int32, (BLK, head_count * BLK), 0)
    key_sum[...] = jnp.zeros_like(key_sum)
    value_sum[...] = jnp.zeros_like(value_sum)

    def one(step):
        starts, limits = key_list(step, block_count, total_blocks, lens, owners, offsets, globals_)
        row = pl.multiple_of(step * BLK, BLK)
        queries = qkv[pl.ds(row, BLK), 0:width] * jnp.asarray(scale, low)
        query_rows = stack_heads(queries, lanes, head_count)
        grad_rows = stack_heads(grad_attended[pl.ds(row, BLK), :], lanes, head_count)
        keys = jnp.concatenate([qkv[pl.ds(s, BLK), width : 2 * width] for s in starts], axis=0)
        values = jnp.concatenate([qkv[pl.ds(s, BLK), 2 * width :] for s in starts], axis=0)
        score_values = masked_scores(keys, query_rows, limits, inner_rows)
        probs = jnp.exp(score_values - log_total[step])
        grad_probs = matmul_right(values, grad_rows)
        correction = jnp.sum(probs * grad_probs, axis=0, keepdims=True)
        grad_scores = (probs * (grad_probs - correction)).astype(low)
        grad_keys = matmul(grad_scores, query_rows)
        grad_values = matmul(probs.astype(low), grad_rows)
        grad_queries = merge_heads(matmul_left(grad_scores, keys), lanes, head_count) * scale
        grad_qkv[pl.ds(row, BLK), 0:width] = grad_queries.astype(low)
        for j, s in enumerate(starts):
            key_sum[pl.ds(s, BLK), :] += grad_keys[j * BLK : (j + 1) * BLK]
            value_sum[pl.ds(s, BLK), :] += grad_values[j * BLK : (j + 1) * BLK]

    def body(index, carry):
        for part in range(unroll):
            one(index * unroll + part)
        return carry

    lax.fori_loop(0, total_blocks // unroll, body, 0)
    grad_qkv[:, width : 2 * width] = key_sum[...].astype(low)
    grad_qkv[:, 2 * width :] = value_sum[...].astype(low)


smem = pl.BlockSpec(memory_space=pltpu.SMEM)
vmem = pl.BlockSpec(memory_space=pltpu.VMEM)


def attend(tables, qkv, block_count, head_count, scale):
    rows, width = qkv.shape[0], qkv.shape[1] // 3
    total_blocks = rows // BLK
    return pl.pallas_call(
        functools.partial(attend_kernel, block_count, head_count, scale, 3),
        out_shape=(
            jax.ShapeDtypeStruct((rows, width), low),
            jax.ShapeDtypeStruct((total_blocks, 1, head_count * BLK), full),
        ),
        in_specs=[smem] * 4 + [vmem],
        out_specs=(vmem, vmem),
        compiler_params=pltpu.CompilerParams(vmem_limit_bytes=40 * 2**20),
        cost_estimate=pl.CostEstimate(
            flops=total_blocks * 4 * 128 * 128 * 512, bytes_accessed=rows * width * 8, transcendentals=0
        ),
        name="attend",
    )(*tables, qkv)


def attend_back(tables, qkv, log_total, grad_attended, block_count, head_count, scale):
    rows, width = qkv.shape[0], qkv.shape[1] // 3
    total_blocks = rows // BLK
    return pl.pallas_call(
        functools.partial(attend_back_kernel, block_count, head_count, scale, 2),
        out_shape=jax.ShapeDtypeStruct((rows, 3 * width), low),
        in_specs=[smem] * 4 + [vmem] * 3,
        out_specs=vmem,
        scratch_shapes=[pltpu.VMEM((rows, width), full)] * 2,
        compiler_params=pltpu.CompilerParams(vmem_limit_bytes=40 * 2**20),
        cost_estimate=pl.CostEstimate(
            flops=total_blocks * 10 * 128 * 128 * 512, bytes_accessed=rows * width * 16, transcendentals=0
        ),
        name="attend_back",
    )(*tables, qkv, log_total, grad_attended)


def as_row(vector):
    return vector[...].astype(full).reshape(1, -1)


def row_stats(values):
    average = jnp.mean(values, axis=-1, keepdims=True)
    centered = values - average
    variance = jnp.mean(centered * centered, axis=-1, keepdims=True)
    inverse = lax.rsqrt(variance + norm_eps)
    return centered * inverse, inverse


def project_kernel(count, places, *refs):
    parts, (gain, shift, w_query, w_key, w_value, qkv, normed) = refs[:count], refs[count:]
    tokens = parts[0].shape[0]
    weights = jnp.concatenate([w_query[...], w_key[...], w_value[...]], axis=1)
    for distance, part in enumerate(parts):
        scaled, _ = row_stats(part[...].astype(full))
        rows = (scaled * as_row(gain) + as_row(shift)).astype(low)
        at = pl.ds(pl.multiple_of((places[0] ^ distance) * tokens, tokens), tokens)
        normed[at, :] = rows
        qkv[at, :] = matmul(rows, weights).astype(low)


def project(places, parts, gain, shift, w_query, w_key, w_value, width, copies):
    count = len(parts)
    tokens, model = parts[0].shape
    whole = pl.BlockSpec((tokens, model), lambda j, places: (0, 0))
    row = pl.BlockSpec((model,), lambda j, places: (0,))
    if width % 128:
        weights = [
            lax.dynamic_slice_in_dim(w, places[0] // copies * width, width, axis=1)
            for w in (w_query, w_key, w_value)
        ]
        weight = pl.BlockSpec((model, width), lambda j, places: (0, 0))
    else:
        weights = [w_query, w_key, w_value]
        weight = pl.BlockSpec((model, width), lambda j, places: (0, places[0] // copies))
    return pl.pallas_call(
        functools.partial(project_kernel, count),
        grid_spec=pltpu.PrefetchScalarGridSpec(
            num_scalar_prefetch=1,
            grid=(1,),
            in_specs=[whole] * count + [row, row] + [weight] * 3,
            out_specs=(
                pl.BlockSpec((count * tokens, 3 * width), lambda j, places: (0, 0)),
                pl.BlockSpec((count * tokens, model), lambda j, places: (0, 0)),
            ),
        ),
        out_shape=(
            jax.ShapeDtypeStruct((count * tokens, 3 * width), low),
            jax.ShapeDtypeStruct((count * tokens, model), low),
        ),
        compiler_params=pltpu.CompilerParams(vmem_limit_bytes=vmem_limit),
        cost_estimate=pl.CostEstimate(
            flops=6 * count * tokens * model * width,
            bytes_accessed=4 * count * tokens * model,
            transcendentals=0,
        ),
        name="project",
    )(places, *parts, gain, shift, *weights)


def project_back_kernel(
    width, inputs, gain, grad_middle, received, w_query, w_key, w_value, input_grad, gain_grads, total
):
    step = pl.program_id(0)

    @pl.when(step == 0)
    def _():
        total[...] = jnp.zeros_like(total)

    result = total[...]
    for part, weight in enumerate((w_query, w_key, w_value)):
        pieces = [
            received[i, :, part * width : (part + 1) * width] for i in range(received.shape[0])
        ]
        result += matmul_right(jnp.concatenate(pieces, axis=1), weight[...])
    total[...] = result

    @pl.when(step == pl.num_programs(0) - 1)
    def _():
        grad_normed = total[...]
        scaled, inverse = row_stats(inputs[...].astype(full))
        back = normalize_back(grad_normed, scaled, inverse, as_row(gain))
        input_grad[...] = (grad_middle[...] + back).astype(low)
        gain_grads[0:1, :] = jnp.sum(grad_normed * scaled, axis=0, keepdims=True)
        gain_grads[1:2, :] = jnp.sum(grad_normed, axis=0, keepdims=True)


def project_back(inputs, gain, grad_middle, received, w_query, w_key, w_value):
    tokens, model = inputs.shape
    columns = 256
    width = received.shape[2] // 3
    per_step = columns // width
    weight = pl.BlockSpec((model, columns), lambda j: (0, j))
    row = pl.BlockSpec((model,), lambda j: (0,))
    whole = pl.BlockSpec((tokens, model), lambda j: (0, 0))
    return pl.pallas_call(
        functools.partial(project_back_kernel, width),
        grid=(model // columns,),
        out_shape=(
            jax.ShapeDtypeStruct((tokens, model), low),
            jax.ShapeDtypeStruct((2, model), full),
        ),
        in_specs=[
            whole,
            row,
            whole,
            pl.BlockSpec((per_step, tokens, 3 * width), lambda j: (j, 0, 0)),
            weight,
            weight,
            weight,
        ],
        out_specs=(whole, pl.BlockSpec((2, model), lambda j: (0, 0))),
        scratch_shapes=[pltpu.VMEM((tokens, model), full)],
        compiler_params=pltpu.CompilerParams(vmem_limit_bytes=vmem_limit),
        cost_estimate=pl.CostEstimate(
            flops=6 * tokens * model * model, bytes_accessed=6 * model * model, transcendentals=0
        ),
        name="project_back",
    )(inputs, gain, grad_middle, received, w_query, w_key, w_value)


def middle_kernel(received, inputs, w_out, gain, shift, middle, normed):
    attended = jnp.concatenate([received[i] for i in range(received.shape[0])], axis=1)
    rows = inputs[...].astype(full) + matmul(attended, w_out[...])
    middle[...] = rows
    unit, _ = row_stats(rows)
    normed[...] = (unit * as_row(gain) + as_row(shift)).astype(low)


def attend_out(received, inputs, w_out, gain, shift):
    tokens, model = inputs.shape
    return pl.pallas_call(
        middle_kernel,
        out_shape=(
            jax.ShapeDtypeStruct((tokens, model), full),
            jax.ShapeDtypeStruct((tokens, model), low),
        ),
        in_specs=[vmem] * 5,
        out_specs=(vmem, vmem),
        compiler_params=pltpu.CompilerParams(vmem_limit_bytes=vmem_limit),
        cost_estimate=pl.CostEstimate(
            flops=2 * tokens * model * model, bytes_accessed=2 * model * model, transcendentals=0
        ),
        name="attend_out",
    )(received, inputs, w_out, gain, shift)


def hidden(normed, grad_out, w_in, b_in, w_back):
    inner = matmul(normed, w_in) + as_row(b_in)
    share = 0.5 * (1.0 + lax.erf(inner * 0.7071067811865476))
    density = jnp.exp(inner * inner * -0.5) * 0.3989422804014327
    grad_active = matmul_right(grad_out, w_back)
    grads = (grad_active * (share + inner * density)).astype(low)
    return (inner * share).astype(low), grads


def feed_kernel(
    normed,
    middle,
    grad_out,
    w_out,
    gain,
    b_back,
    w_in,
    b_in,
    w_back,
    output,
    grad_middle,
    grad_middle_low,
    grad_attended,
    gain_grads,
    b_in_grad,
    out_total,
    grad_total,
):
    step = pl.program_id(0)
    groups, _, width = grad_attended.shape

    @pl.when(step == 0)
    def _():
        out_total[...] = middle[...] + as_row(b_back)
        grad_total[...] = jnp.zeros_like(grad_total)

    active, grads = hidden(normed[...], grad_out[...], w_in[...], b_in, w_back[...])
    b_in_grad[...] = jnp.sum(grads.astype(full), axis=0, keepdims=True)
    out_total[...] += matmul(active, w_back[...])
    grad_total[...] += matmul_right(grads, w_in[...])

    @pl.when(step == pl.num_programs(0) - 1)
    def _():
        output[...] = out_total[...].astype(low)
        grad_normed = grad_total[...]
        unit, rate = row_stats(middle[...])
        grad_full = grad_out[...].astype(full)
        back = normalize_back(grad_normed, unit, rate, as_row(gain))
        grads_middle = grad_full + back
        grad_middle[...] = grads_middle
        grads_low = grads_middle.astype(low)
        grad_middle_low[...] = grads_low
        result = matmul_right(grads_low, w_out[...]).astype(low)
        for i in range(groups):
            grad_attended[i] = result[:, i * width : (i + 1) * width]
        gain_grads[0:1, :] = jnp.sum(grad_normed * unit, axis=0, keepdims=True)
        gain_grads[1:2, :] = jnp.sum(grad_normed, axis=0, keepdims=True)
        gain_grads[2:3, :] = jnp.sum(grad_full, axis=0, keepdims=True)


def feed(normed, middle, grad_out, w_out, gain, b_back, w_in, b_in, w_back, groups, width):
    tokens, model = normed.shape
    ff = w_in.shape[1]
    columns = 512
    row = pl.BlockSpec((model,), lambda j: (0,))
    whole = pl.BlockSpec((tokens, model), lambda j: (0, 0))
    heads = pl.BlockSpec((groups, tokens, width), lambda j: (0, 0, 0))
    return pl.pallas_call(
        feed_kernel,
        grid=(ff // columns,),
        out_shape=(
            jax.ShapeDtypeStruct((tokens, model), low),
            jax.ShapeDtypeStruct((tokens, model), full),
            jax.ShapeDtypeStruct((tokens, model), low),
            jax.ShapeDtypeStruct((groups, tokens, width), low),
            jax.ShapeDtypeStruct((3, model), full),
            jax.ShapeDtypeStruct((1, ff), full),
        ),
        in_specs=[
            whole,
            whole,
            whole,
            pl.BlockSpec((model, model), lambda j: (0, 0), pipeline_mode=pl.Buffered(1)),
            row,
            row,
            pl.BlockSpec((model, columns), lambda j: (0, j)),
            pl.BlockSpec((columns,), lambda j: (j,)),
            pl.BlockSpec((columns, model), lambda j: (j, 0)),
        ],
        out_specs=(
            whole,
            whole,
            whole,
            heads,
            pl.BlockSpec((3, model), lambda j: (0, 0)),
            pl.BlockSpec((1, columns), lambda j: (0, j)),
        ),
        scratch_shapes=[pltpu.VMEM((tokens, model), full)] * 2,
        compiler_params=pltpu.CompilerParams(vmem_limit_bytes=vmem_limit),
        cost_estimate=pl.CostEstimate(
            flops=8 * tokens * model * ff, bytes_accessed=4 * model * ff, transcendentals=0
        ),
        name="feed",
    )(normed, middle, grad_out, w_out, gain, b_back, w_in, b_in, w_back)


def pick_blocks(index, total, sent, own, other):
    def block(distance):
        return total[:, pl.ds(index ^ distance, 1)][:, 0].astype(low)

    sent[0] = block(1)
    sent[1] = block(3)
    own[...] = block(0)
    other[...] = block(2)


def picked_shapes(outer, rows, columns):
    shape = (outer, rows, columns)
    return [jax.ShapeDtypeStruct((2,) + shape, low)] + [jax.ShapeDtypeStruct(shape, low)] * 2


def picked_specs(outer, rows, columns):
    whole = pl.BlockSpec((outer, rows, columns), lambda j, places: (0, 0, 0))
    return [pl.BlockSpec((2, outer, rows, columns), lambda j, places: (0, 0, 0, 0)), whole, whole]


def accumulate(total, value):
    @pl.when(pl.program_id(0) == 0)
    def _():
        total[...] = value.reshape(total.shape)

    @pl.when(pl.program_id(0) > 0)
    def _():
        total[...] += value.reshape(total.shape)


def product_kernel(places, left, right, sent, own, other, total):
    accumulate(total, matmul_left(left[...], right[...]))

    @pl.when(pl.program_id(0) == pl.num_programs(0) - 1)
    def _():
        pick_blocks(places[1], total, sent, own, other)


def product(places, left, left_columns, right, outer, name):
    tokens, columns = right.shape
    chunk = min(512, tokens)
    rows = left_columns // (4 * outer)
    return pl.pallas_call(
        product_kernel,
        grid_spec=pltpu.PrefetchScalarGridSpec(
            num_scalar_prefetch=1,
            grid=(tokens // chunk,),
            in_specs=[
                pl.BlockSpec((chunk, left_columns), lambda j, places: (j, 0)),
                pl.BlockSpec((chunk, columns), lambda j, places: (j, 0)),
            ],
            out_specs=picked_specs(outer, rows, columns),
            scratch_shapes=[pltpu.VMEM((outer, 4, rows, columns), full)],
        ),
        out_shape=picked_shapes(outer, rows, columns),
        compiler_params=pltpu.CompilerParams(vmem_limit_bytes=vmem_limit),
        cost_estimate=pl.CostEstimate(
            flops=2 * tokens * left_columns * columns,
            bytes_accessed=2 * tokens * (left_columns + columns),
            transcendentals=0,
        ),
        name=name,
    )(places, left, right)


def feed_products_kernel(
    places,
    normed,
    grad_out,
    w_in,
    b_in,
    w_back,
    in_sent,
    in_own,
    in_other,
    back_sent,
    back_own,
    back_other,
    in_total,
    back_total,
):
    active, grads = hidden(normed[...], grad_out[...], w_in[...], b_in, w_back[...])
    accumulate(in_total, matmul_left(normed[...], grads))
    accumulate(back_total, matmul_left(active, grad_out[...]))

    @pl.when(pl.program_id(0) == pl.num_programs(0) - 1)
    def _():
        pick_blocks(places[1], in_total, in_sent, in_own, in_other)
        pick_blocks(places[1], back_total, back_sent, back_own, back_other)


def feed_products(places, normed, kept, w_in, b_in, w_back, seq_count):
    tokens, model = normed.shape
    columns = w_in.shape[1] // seq_count
    chunk = 512
    slim = model // (4 * seq_count)
    back_slim = columns // 4
    return pl.pallas_call(
        feed_products_kernel,
        grid_spec=pltpu.PrefetchScalarGridSpec(
            num_scalar_prefetch=1,
            grid=(tokens // chunk,),
            in_specs=[
                pl.BlockSpec((chunk, model), lambda j, places: (j, 0)),
                pl.BlockSpec((chunk, model), lambda j, places: (j, 0)),
                pl.BlockSpec((model, columns), lambda j, places: (0, places[0])),
                pl.BlockSpec((1, columns), lambda j, places: (0, places[0])),
                pl.BlockSpec((columns, model), lambda j, places: (places[0], 0)),
            ],
            out_specs=picked_specs(seq_count, slim, columns) + picked_specs(1, back_slim, model),
            scratch_shapes=[
                pltpu.VMEM((seq_count, 4, slim, columns), full),
                pltpu.VMEM((1, 4, back_slim, model), full),
            ],
        ),
        out_shape=picked_shapes(seq_count, slim, columns) + picked_shapes(1, back_slim, model),
        compiler_params=pltpu.CompilerParams(vmem_limit_bytes=vmem_limit),
        cost_estimate=pl.CostEstimate(
            flops=8 * tokens * model * columns,
            bytes_accessed=4 * tokens * model + 4 * model * columns,
            transcendentals=0,
        ),
        name="feed_products",
    )(places, normed, kept, w_in, b_in.reshape(1, -1), w_back)


def swap(blocks, axes):
    return lax.all_to_all(blocks, axes, split_axis=0, concat_axis=0, tiled=True)


def gather_rows(rows):
    return lax.all_gather(rows, "seq", axis=0, tiled=True)


def gather_parts(rows):
    count = lax.axis_size("seq")

    def move(block, distance):
        return lax.ppermute(block, "seq", [(i, i ^ distance) for i in range(count)])

    parts = [rows, None] + [None] * (count - 2)
    for distance in range(2, count, 2):
        parts[distance] = move(rows, distance)
    for distance in range(0, count, 2):
        parts[distance + 1] = move(parts[distance], 1)
    return parts


def trade(block, distance):
    return lax.ppermute(block, "batch", [(i, i ^ distance) for i in range(4)])


def first_sum(got, own, other):
    own = own.astype(full) + got[0].astype(full)
    other = (other.astype(full) + got[1].astype(full)).astype(low)
    return own, other


def together(*values):
    return lax.optimization_barrier(values)


def shards(
    inputs,
    cotangent,
    lengths,
    rand_owners,
    rand_offsets,
    global_ids,
    ln1_gain,
    ln1_shift,
    w_query,
    w_key,
    w_value,
    w_out,
    ln2_gain,
    ln2_shift,
    w_in,
    b_in,
    w_back,
    b_back,
):
    seq_count = lax.axis_size("seq")
    batch_count = lax.axis_size("batch")
    device_count = seq_count * batch_count
    token_count = inputs.shape[1]
    model_width = inputs.shape[2]
    ff_width = w_in.shape[1]
    block_count = token_count // BLK
    head_dim = model_width // HEADS
    scale = head_dim ** (-0.5)
    total_tokens = seq_count * token_count
    head_groups = min(HEADS, seq_count)
    copies = seq_count // head_groups
    head_count = HEADS // head_groups
    width = head_count * head_dim
    tables = (lengths, rand_owners, rand_offsets, global_ids)

    def to_heads(sent):
        if copies > 1:
            sent = jnp.repeat(sent, copies, axis=0)
        return swap(sent, "seq").reshape(total_tokens, -1)

    def to_tokens(rows):
        return swap(rows.reshape(seq_count, token_count, -1), "seq")[::copies]

    rows_in, grad_out = inputs[0], cotangent[0]
    gain_one, gain_two = ln1_gain, ln2_gain
    places = jnp.stack([lax.axis_index("seq"), lax.axis_index("batch")]).astype(jnp.int32)
    parts = gather_parts(rows_in)
    qkv, normed_all = project(
        places, parts, gain_one, ln1_shift, w_query, w_key, w_value, width, copies
    )
    late_grad_out, qkv = together(grad_out, qkv)
    grad_out_all = gather_rows(late_grad_out)
    attended_all, log_total = attend(tables, qkv, block_count, head_count, scale)
    middle, normed_two = attend_out(
        to_tokens(attended_all), rows_in, w_out, gain_two, ln2_shift
    )
    normed_two_all = gather_rows(normed_two)
    output, grad_middle, grad_middle_low, grad_attended, gain_two_grads, grad_b_in = feed(
        normed_two,
        middle,
        grad_out,
        w_out,
        gain_two,
        b_back,
        w_in,
        b_in,
        w_back,
        head_groups,
        width,
    )
    grad_middle_all = gather_rows(grad_middle_low)
    grad_rows, grad_out_all = together(to_heads(grad_attended), grad_out_all)
    grad_qkv = attend_back(tables, qkv, log_total, grad_rows, block_count, head_count, scale)
    grad_qkv_near = to_tokens(grad_qkv)

    slim = model_width // device_count
    inner_columns = ff_width // seq_count
    qkv_sent, qkv_own, qkv_other = product(
        places, normed_all, model_width, grad_qkv, seq_count, "qkv_product"
    )
    qkv_got = trade(qkv_sent, 1)
    normed_two_all, qkv_own = together(normed_two_all, qkv_own)
    in_sent, in_own, in_other, back_sent, back_own, back_other = feed_products(
        places, normed_two_all, grad_out_all, w_in, b_in, w_back, seq_count
    )
    in_got = trade(in_sent, 1)
    qkv_got, in_own = together(qkv_got, in_own)
    qkv_own, qkv_other = first_sum(qkv_got, qkv_own, qkv_other)
    grad_qkv_near, qkv_other = together(grad_qkv_near, qkv_other)
    qkv_last = trade(qkv_other, 2)
    input_grad, gain_one_grads = project_back(
        rows_in, gain_one, grad_middle, grad_qkv_near, w_query, w_key, w_value
    )
    in_got, qkv_last, back_sent, input_grad, gain_one_grads = together(
        in_got, qkv_last, back_sent, input_grad, gain_one_grads
    )
    in_own, in_other = first_sum(in_got, in_own, in_other)
    in_last = trade(in_other, 2)
    back_got = trade(back_sent, 1)
    own_rows = width // copies
    own_attended, in_own = together(attended_all, in_own)
    if copies > 1:
        at = lax.axis_index("seq") % copies * own_rows
        own_attended = lax.dynamic_slice_in_dim(own_attended, at, own_rows, axis=1)
    out_sent, out_own, out_other = product(
        places, own_attended, own_rows, grad_middle_all, 1, "out_product"
    )
    in_last, back_got, out_sent, gain_one_grads = together(in_last, back_got, out_sent, gain_one_grads)
    out_got = trade(out_sent, 1)
    back_own, back_other = first_sum(back_got, back_own, back_other)
    back_rows = (back_own + trade(back_other, 2).astype(full))[0]
    out_own, out_other = first_sum(out_got, out_own, out_other)
    out_rows = (out_own + trade(out_other, 2).astype(full))[0]

    mixed = [
        (own + last.astype(full)).astype(low)
        for own, last in ((in_own, in_last), (qkv_own, qkv_last))
    ]
    mixed = swap(jnp.concatenate(mixed, axis=2), "seq")
    in_rows = mixed[:, :, :inner_columns].transpose(1, 0, 2).reshape(slim, ff_width).astype(full)
    qkv_rows = mixed[::copies, :, inner_columns:].transpose(1, 0, 2).astype(full)
    qkv_rows = [
        qkv_rows[:, :, i * width : (i + 1) * width].reshape(slim, model_width) for i in range(3)
    ]
    small = [gain_one_grads[0], gain_one_grads[1], *gain_two_grads, grad_b_in[0]]
    packed = jnp.concatenate([v.reshape(device_count, -1) for v in small], axis=1)
    packed = jnp.sum(swap(packed, ("seq", "batch")), axis=0)
    cuts, at = [], 0
    for v in small:
        size = v.shape[0] // device_count
        cuts.append(packed[at : at + size])
        at += size
    return (
        output[None],
        input_grad[None],
        cuts[0],
        cuts[1],
        qkv_rows[0],
        qkv_rows[1],
        qkv_rows[2],
        out_rows,
        cuts[2],
        cuts[3],
        in_rows,
        cuts[5],
        back_rows,
        cuts[4],
    )


def solution(mesh):
    rows = P("batch", "seq", None)
    table = P("batch", None, None)
    thin = P(("seq", "batch"))
    wide = P(("seq", "batch"), None)
    return jax.shard_map(
        shards,
        mesh=mesh,
        in_specs=(rows, rows, P("batch", None), table, table, table) + (P(),) * 12,
        out_specs=(rows, rows, thin, thin, wide, wide, wide, wide, thin, thin, wide, thin, wide, thin),
        check_vma=False,
    )
```

```python
import functools

import jax
import jax.numpy as jnp
from jax import lax
from jax.experimental import pallas as pl
from jax.experimental.pallas import tpu as pltpu
from jax.sharding import PartitionSpec as P

HEADS = 16
BLK = 64
RAND = 3
KEY_BLOCKS = 3 + RAND + 2

norm_eps = 1e-05
masked_score = -1e30
vmem_limit = 60 * 2**20
low = jnp.bfloat16
full = jnp.float32


def matmul(left, right):
    return jnp.dot(left, right, preferred_element_type=full)


def matmul_left(left, right):
    return lax.dot_general(left, right, (((0,), (0,)), ((), ())), preferred_element_type=full)


def matmul_right(left, right):
    return lax.dot_general(left, right, (((1,), (1,)), ((), ())), preferred_element_type=full)


def normalize_back(grad_normed, scaled, inverse, ln_gain):
    grad_scaled = grad_normed * ln_gain
    inner_mean = jnp.mean(grad_scaled, axis=-1, keepdims=True)
    along_mean = jnp.mean(grad_scaled * scaled, axis=-1, keepdims=True)
    return inverse * (grad_scaled - inner_mean - scaled * along_mean)


def key_list(step, block_count, total_blocks, lens, owners, offsets, globals_):
    length = lens[0, 0]
    ids = [step - 1, step, step + 1]
    ids += [owners[0, step, r] * block_count + offsets[0, step, r] for r in range(RAND)]
    ids += [globals_[0, 0, g] for g in range(globals_.shape[2])]
    starts, limits = [], []
    for block in ids:
        inside = jnp.logical_and(block >= 0, block < total_blocks)
        clamped = jnp.clip(block, 0, total_blocks - 1)
        starts.append(pl.multiple_of(clamped * BLK, BLK))
        limits.append(jnp.where(inside, length - clamped * BLK, 0))
    return starts, limits


def stack_heads(rows, lanes, head_count):
    if head_count == 1:
        return rows
    zero = jnp.zeros_like(rows)
    return jnp.concatenate([jnp.where(lanes == h, rows, zero) for h in range(head_count)], axis=0)


def merge_heads(stacked, lanes, head_count):
    merged = stacked[:BLK]
    for h in range(1, head_count):
        merged = jnp.where(lanes == h, stacked[h * BLK : (h + 1) * BLK], merged)
    return merged


def masked(score_values, limits, inner_rows):
    parts = [
        jnp.where(inner_rows < limit, score_values[j * BLK : (j + 1) * BLK], masked_score)
        for j, limit in enumerate(limits)
    ]
    return jnp.concatenate(parts, axis=0)


def attend_kernel(
    block_count, head_count, scale, unroll, lens, owners, offsets, globals_, qkv, attended, log_total
):
    total_blocks = qkv.shape[0] // BLK
    width = qkv.shape[1] // 3
    lanes = lax.broadcasted_iota(jnp.int32, (BLK, width), 1) // (width // head_count)
    inner_rows = lax.broadcasted_iota(jnp.int32, (BLK, head_count * BLK), 0)

    def one(step):
        starts, limits = key_list(step, block_count, total_blocks, lens, owners, offsets, globals_)
        row = pl.multiple_of(step * BLK, BLK)
        queries = qkv[pl.ds(row, BLK), 0:width] * jnp.asarray(scale, low)
        query_rows = stack_heads(queries, lanes, head_count)
        keys = jnp.concatenate([qkv[pl.ds(s, BLK), width : 2 * width] for s in starts], axis=0)
        values = jnp.concatenate([qkv[pl.ds(s, BLK), 2 * width :] for s in starts], axis=0)
        score_values = masked(matmul_right(keys, query_rows), limits, inner_rows)
        top = jnp.max(score_values, axis=0, keepdims=True)
        raised = jnp.exp(score_values - top)
        total = jnp.sum(raised, axis=0, keepdims=True)
        weights = (raised * (1.0 / total)).astype(low)
        result = matmul_left(weights, values)
        attended[pl.ds(row, BLK), :] = merge_heads(result, lanes, head_count).astype(low)
        log_total[step] = top + jnp.log(total)

    def body(index, carry):
        for part in range(unroll):
            one(index * unroll + part)
        return carry

    lax.fori_loop(0, total_blocks // unroll, body, 0)


def attend_back_kernel(
    block_count,
    head_count,
    scale,
    unroll,
    lens,
    owners,
    offsets,
    globals_,
    qkv,
    log_total,
    grad_attended,
    grad_qkv,
    sums,
    parts,
):
    total_blocks = qkv.shape[0] // BLK
    width = qkv.shape[1] // 3
    lanes = lax.broadcasted_iota(jnp.int32, (BLK, width), 1) // (width // head_count)
    inner_rows = lax.broadcasted_iota(jnp.int32, (BLK, head_count * BLK), 0)
    sums[...] = jnp.zeros_like(sums)

    def one(step, part):
        starts, limits = key_list(step, block_count, total_blocks, lens, owners, offsets, globals_)
        row = pl.multiple_of(step * BLK, BLK)
        queries = qkv[pl.ds(row, BLK), 0:width] * jnp.asarray(scale, low)
        query_rows = stack_heads(queries, lanes, head_count)
        grad_rows = stack_heads(grad_attended[pl.ds(row, BLK), :], lanes, head_count)
        keys = jnp.concatenate([qkv[pl.ds(s, BLK), width : 2 * width] for s in starts], axis=0)
        values = jnp.concatenate([qkv[pl.ds(s, BLK), 2 * width :] for s in starts], axis=0)
        score_values = masked(matmul_right(keys, query_rows), limits, inner_rows)
        probs = jnp.exp(score_values - log_total[step])
        grad_probs = matmul_right(values, grad_rows)
        correction = jnp.sum(probs * grad_probs, axis=0, keepdims=True)
        grad_scores = (probs * (grad_probs - correction)).astype(low)
        parts[part, :, :width] = matmul(grad_scores, query_rows)
        parts[part, :, width:] = matmul(probs.astype(low), grad_rows)
        grad_queries = merge_heads(matmul_left(grad_scores, keys), lanes, head_count) * scale
        grad_qkv[pl.ds(row, BLK), 0:width] = grad_queries.astype(low)
        return starts

    def body(index, carry):
        lists = [one(index * unroll + part, part) for part in range(unroll)]
        for part, starts in enumerate(lists):
            for j, s in enumerate(starts):
                sums[pl.ds(s, BLK), :] += parts[part, j * BLK : (j + 1) * BLK]
        return carry

    lax.fori_loop(0, total_blocks // unroll, body, 0)
    grad_qkv[:, width:] = sums[...].astype(low)


def unroll_of(steps, most):
    return max(u for u in range(1, most + 1) if steps % u == 0)


smem = pl.BlockSpec(memory_space=pltpu.SMEM)
vmem = pl.BlockSpec(memory_space=pltpu.VMEM)


def attend(tables, qkv, block_count, head_count, scale):
    rows, width = qkv.shape[0], qkv.shape[1] // 3
    total_blocks = rows // BLK
    return pl.pallas_call(
        functools.partial(attend_kernel, block_count, head_count, scale, unroll_of(total_blocks, 8)),
        out_shape=(
            jax.ShapeDtypeStruct((rows, width), low),
            jax.ShapeDtypeStruct((total_blocks, 1, head_count * BLK), full),
        ),
        in_specs=[smem] * 4 + [vmem],
        out_specs=(vmem, vmem),
        compiler_params=pltpu.CompilerParams(vmem_limit_bytes=40 * 2**20),
        cost_estimate=pl.CostEstimate(
            flops=total_blocks * 4 * 128 * 128 * 512, bytes_accessed=rows * width * 8, transcendentals=0
        ),
        name="attend",
    )(*tables, qkv)


def attend_back(tables, qkv, log_total, grad_attended, block_count, head_count, scale):
    rows, width = qkv.shape[0], qkv.shape[1] // 3
    total_blocks = rows // BLK
    return pl.pallas_call(
        functools.partial(attend_back_kernel, block_count, head_count, scale, unroll_of(total_blocks, 8)),
        out_shape=jax.ShapeDtypeStruct((rows, 3 * width), low),
        in_specs=[smem] * 4 + [vmem] * 3,
        out_specs=vmem,
        scratch_shapes=[
            pltpu.VMEM((rows, 2 * width), full),
            pltpu.VMEM((unroll_of(total_blocks, 8), KEY_BLOCKS * BLK, 2 * width), full),
        ],
        compiler_params=pltpu.CompilerParams(vmem_limit_bytes=40 * 2**20),
        cost_estimate=pl.CostEstimate(
            flops=total_blocks * 10 * 128 * 128 * 512, bytes_accessed=rows * width * 16, transcendentals=0
        ),
        name="attend_back",
    )(*tables, qkv, log_total, grad_attended)


def as_row(vector):
    return vector[...].astype(full).reshape(1, -1)


def row_stats(values):
    average = jnp.mean(values, axis=-1, keepdims=True)
    centered = values - average
    variance = jnp.mean(centered * centered, axis=-1, keepdims=True)
    inverse = lax.rsqrt(variance + norm_eps)
    return centered * inverse, inverse


def project_kernel(count, rows, column, *refs):
    parts, (gain, shift, w_query, w_key, w_value) = refs[:count], refs[count : count + 5]
    qkv, normed = refs[-2:]
    weights = jnp.concatenate([w_query[...], w_key[...], w_value[...]], axis=1)
    for i, part in enumerate(parts):
        at = pl.ds(pl.multiple_of(rows[i] * part.shape[0], part.shape[0]), part.shape[0])
        scaled, _ = row_stats(part[...].astype(full))
        result = (scaled * as_row(gain) + as_row(shift)).astype(low)
        normed[at, :] = result
        qkv[at, :] = matmul(result, weights).astype(low)


def project(rows, column, parts, gain, shift, weights, width):
    count = len(parts)
    tokens, model = parts[0].shape
    whole = pl.BlockSpec((tokens, model), lambda j, rows, column: (0, 0))
    row = pl.BlockSpec((model,), lambda j, rows, column: (0,))
    weight = pl.BlockSpec((model, width), lambda j, rows, column: (0, column[0]))
    return pl.pallas_call(
        functools.partial(project_kernel, count),
        grid_spec=pltpu.PrefetchScalarGridSpec(
            num_scalar_prefetch=2,
            grid=(1,),
            in_specs=[whole] * count + [row, row] + [weight] * 3,
            out_specs=(
                pl.BlockSpec((count * tokens, 3 * width), lambda j, rows, column: (0, 0)),
                pl.BlockSpec((count * tokens, model), lambda j, rows, column: (0, 0)),
            ),
        ),
        out_shape=(
            jax.ShapeDtypeStruct((count * tokens, 3 * width), low),
            jax.ShapeDtypeStruct((count * tokens, model), low),
        ),
        compiler_params=pltpu.CompilerParams(vmem_limit_bytes=vmem_limit),
        cost_estimate=pl.CostEstimate(
            flops=6 * count * tokens * model * width,
            bytes_accessed=4 * count * tokens * model,
            transcendentals=0,
        ),
        name="project",
    )(rows, column, *parts, gain, shift, *weights)


def project_back_kernel(
    width, inputs, gain, grad_middle, received, w_query, w_key, w_value, input_grad, gain_grads, total
):
    step = pl.program_id(0)

    @pl.when(step == 0)
    def _():
        total[...] = jnp.zeros_like(total)

    result = total[...]
    for part, weight in enumerate((w_query, w_key, w_value)):
        pieces = [
            received[i, :, part * width : (part + 1) * width] for i in range(received.shape[0])
        ]
        result += matmul_right(jnp.concatenate(pieces, axis=1), weight[...])
    total[...] = result

    @pl.when(step == pl.num_programs(0) - 1)
    def _():
        grad_normed = total[...]
        scaled, inverse = row_stats(inputs[...].astype(full))
        back = normalize_back(grad_normed, scaled, inverse, as_row(gain))
        input_grad[...] = (grad_middle[...] + back).astype(low)
        gain_grads[0:1, :] = jnp.sum(grad_normed * scaled, axis=0, keepdims=True)
        gain_grads[1:2, :] = jnp.sum(grad_normed, axis=0, keepdims=True)


def project_back(inputs, gain, grad_middle, received, w_query, w_key, w_value):
    tokens, model = inputs.shape
    columns = 256
    width = received.shape[2] // 3
    per_step = columns // width
    weight = pl.BlockSpec((model, columns), lambda j: (0, j))
    row = pl.BlockSpec((model,), lambda j: (0,))
    whole = pl.BlockSpec((tokens, model), lambda j: (0, 0))
    return pl.pallas_call(
        functools.partial(project_back_kernel, width),
        grid=(model // columns,),
        out_shape=(
            jax.ShapeDtypeStruct((tokens, model), low),
            jax.ShapeDtypeStruct((2, model), full),
        ),
        in_specs=[
            whole,
            row,
            whole,
            pl.BlockSpec((per_step, tokens, 3 * width), lambda j: (j, 0, 0)),
            weight,
            weight,
            weight,
        ],
        out_specs=(whole, pl.BlockSpec((2, model), lambda j: (0, 0))),
        scratch_shapes=[pltpu.VMEM((tokens, model), full)],
        compiler_params=pltpu.CompilerParams(vmem_limit_bytes=vmem_limit),
        cost_estimate=pl.CostEstimate(
            flops=6 * tokens * model * model, bytes_accessed=6 * model * model, transcendentals=0
        ),
        name="project_back",
    )(inputs, gain, grad_middle, received, w_query, w_key, w_value)


def middle_kernel(received, inputs, w_out, gain, shift, middle, normed):
    attended = jnp.concatenate([received[i] for i in range(received.shape[0])], axis=1)
    rows = inputs[...].astype(full) + matmul(attended, w_out[...])
    middle[...] = rows
    unit, _ = row_stats(rows)
    normed[...] = (unit * as_row(gain) + as_row(shift)).astype(low)


def attend_out(received, inputs, w_out, gain, shift):
    tokens, model = inputs.shape
    return pl.pallas_call(
        middle_kernel,
        out_shape=(
            jax.ShapeDtypeStruct((tokens, model), full),
            jax.ShapeDtypeStruct((tokens, model), low),
        ),
        in_specs=[vmem] * 5,
        out_specs=(vmem, vmem),
        compiler_params=pltpu.CompilerParams(vmem_limit_bytes=vmem_limit),
        cost_estimate=pl.CostEstimate(
            flops=2 * tokens * model * model, bytes_accessed=2 * model * model, transcendentals=0
        ),
        name="attend_out",
    )(received, inputs, w_out, gain, shift)


def hidden(normed, grad_out, w_in, b_in, w_back):
    inner = matmul(normed, w_in) + as_row(b_in)
    share = 0.5 * (1.0 + lax.erf(inner * 0.7071067811865476))
    density = jnp.exp(inner * inner * -0.5) * 0.3989422804014327
    grad_active = matmul_right(grad_out, w_back)
    grads = (grad_active * (share + inner * density)).astype(low)
    return (inner * share).astype(low), grads


def feed_kernel(
    normed,
    middle,
    grad_out,
    w_out,
    gain,
    b_back,
    w_in,
    b_in,
    w_back,
    output,
    grad_middle,
    grad_middle_low,
    grad_attended,
    gain_grads,
    b_in_grad,
    out_total,
    grad_total,
):
    step = pl.program_id(0)
    groups, _, width = grad_attended.shape

    @pl.when(step == 0)
    def _():
        out_total[...] = middle[...] + as_row(b_back)
        grad_total[...] = jnp.zeros_like(grad_total)

    active, grads = hidden(normed[...], grad_out[...], w_in[...], b_in, w_back[...])
    b_in_grad[...] = jnp.sum(grads.astype(full), axis=0, keepdims=True)
    out_total[...] += matmul(active, w_back[...])
    grad_total[...] += matmul_right(grads, w_in[...])

    @pl.when(step == pl.num_programs(0) - 1)
    def _():
        output[...] = out_total[...].astype(low)
        grad_normed = grad_total[...]
        unit, rate = row_stats(middle[...])
        grad_full = grad_out[...].astype(full)
        back = normalize_back(grad_normed, unit, rate, as_row(gain))
        grads_middle = grad_full + back
        grad_middle[...] = grads_middle
        grads_low = grads_middle.astype(low)
        grad_middle_low[...] = grads_low
        result = matmul_right(grads_low, w_out[...]).astype(low)
        for i in range(groups):
            grad_attended[i] = result[:, i * width : (i + 1) * width]
        gain_grads[0:1, :] = jnp.sum(grad_normed * unit, axis=0, keepdims=True)
        gain_grads[1:2, :] = jnp.sum(grad_normed, axis=0, keepdims=True)
        gain_grads[2:3, :] = jnp.sum(grad_full, axis=0, keepdims=True)


def feed(normed, middle, grad_out, w_out, gain, b_back, w_in, b_in, w_back, groups, width):
    tokens, model = normed.shape
    ff = w_in.shape[1]
    columns = 1024
    row = pl.BlockSpec((model,), lambda j: (0,))
    whole = pl.BlockSpec((tokens, model), lambda j: (0, 0))
    heads = pl.BlockSpec((groups, tokens, width), lambda j: (0, 0, 0))
    return pl.pallas_call(
        feed_kernel,
        grid=(ff // columns,),
        out_shape=(
            jax.ShapeDtypeStruct((tokens, model), low),
            jax.ShapeDtypeStruct((tokens, model), full),
            jax.ShapeDtypeStruct((tokens, model), low),
            jax.ShapeDtypeStruct((groups, tokens, width), low),
            jax.ShapeDtypeStruct((3, model), full),
            jax.ShapeDtypeStruct((1, ff), full),
        ),
        in_specs=[
            whole,
            whole,
            whole,
            pl.BlockSpec((model, model), lambda j: (0, 0), pipeline_mode=pl.Buffered(1)),
            row,
            row,
            pl.BlockSpec((model, columns), lambda j: (0, j)),
            pl.BlockSpec((columns,), lambda j: (j,)),
            pl.BlockSpec((columns, model), lambda j: (j, 0)),
        ],
        out_specs=(
            whole,
            whole,
            whole,
            heads,
            pl.BlockSpec((3, model), lambda j: (0, 0)),
            pl.BlockSpec((1, columns), lambda j: (0, j)),
        ),
        scratch_shapes=[pltpu.VMEM((tokens, model), full)] * 2,
        compiler_params=pltpu.CompilerParams(vmem_limit_bytes=vmem_limit),
        cost_estimate=pl.CostEstimate(
            flops=8 * tokens * model * ff, bytes_accessed=4 * model * ff, transcendentals=0
        ),
        name="feed",
    )(normed, middle, grad_out, w_out, gain, b_back, w_in, b_in, w_back)


def pick_blocks(index, total, sent, own, other):
    def block(distance):
        return total[:, pl.ds(index ^ distance, 1)][:, 0].astype(low)

    sent[0] = block(1)
    sent[1] = block(3)
    own[...] = block(0)
    other[...] = block(2)


def picked_shapes(outer, rows, columns):
    shape = (outer, rows, columns)
    return [jax.ShapeDtypeStruct((2,) + shape, low)] + [jax.ShapeDtypeStruct(shape, low)] * 2


def picked_specs(outer, rows, columns):
    whole = pl.BlockSpec((outer, rows, columns), lambda j, places: (0, 0, 0))
    return [pl.BlockSpec((2, outer, rows, columns), lambda j, places: (0, 0, 0, 0)), whole, whole]


def accumulate(total, value):
    @pl.when(pl.program_id(0) == 0)
    def _():
        total[...] = value.reshape(total.shape)

    @pl.when(pl.program_id(0) > 0)
    def _():
        total[...] += value.reshape(total.shape)


def product_kernel(places, left, right, sent, own, other, total):
    accumulate(total, matmul_left(left[...], right[...]))

    @pl.when(pl.program_id(0) == pl.num_programs(0) - 1)
    def _():
        pick_blocks(places[1], total, sent, own, other)


def product(places, left, left_columns, right, outer, name):
    tokens, columns = right.shape
    chunk = 768
    rows = left_columns // (4 * outer)
    return pl.pallas_call(
        product_kernel,
        grid_spec=pltpu.PrefetchScalarGridSpec(
            num_scalar_prefetch=1,
            grid=(tokens // chunk,),
            in_specs=[
                pl.BlockSpec((chunk, left_columns), lambda j, places: (j, 0)),
                pl.BlockSpec((chunk, columns), lambda j, places: (j, 0)),
            ],
            out_specs=picked_specs(outer, rows, columns),
            scratch_shapes=[pltpu.VMEM((outer, 4, rows, columns), full)],
        ),
        out_shape=picked_shapes(outer, rows, columns),
        compiler_params=pltpu.CompilerParams(vmem_limit_bytes=vmem_limit),
        cost_estimate=pl.CostEstimate(
            flops=2 * tokens * left_columns * columns,
            bytes_accessed=2 * tokens * (left_columns + columns),
            transcendentals=0,
        ),
        name=name,
    )(places, left, right)


def feed_products_kernel(
    places,
    normed,
    grad_out,
    w_in,
    b_in,
    w_back,
    in_sent,
    in_own,
    in_other,
    back_sent,
    back_own,
    back_other,
    in_total,
    back_total,
):
    active, grads = hidden(normed[...], grad_out[...], w_in[...], b_in, w_back[...])
    accumulate(in_total, matmul_left(normed[...], grads))
    accumulate(back_total, matmul_left(active, grad_out[...]))

    @pl.when(pl.program_id(0) == pl.num_programs(0) - 1)
    def _():
        pick_blocks(places[1], in_total, in_sent, in_own, in_other)
        pick_blocks(places[1], back_total, back_sent, back_own, back_other)


def feed_products(places, normed, kept, w_in, b_in, w_back, seq_count):
    tokens, model = normed.shape
    columns = w_in.shape[1] // seq_count
    chunk = 768
    slim = model // (4 * seq_count)
    back_slim = columns // 4
    return pl.pallas_call(
        feed_products_kernel,
        grid_spec=pltpu.PrefetchScalarGridSpec(
            num_scalar_prefetch=1,
            grid=(tokens // chunk,),
            in_specs=[
                pl.BlockSpec((chunk, model), lambda j, places: (j, 0)),
                pl.BlockSpec((chunk, model), lambda j, places: (j, 0)),
                pl.BlockSpec((model, columns), lambda j, places: (0, places[0])),
                pl.BlockSpec((1, columns), lambda j, places: (0, places[0])),
                pl.BlockSpec((columns, model), lambda j, places: (places[0], 0)),
            ],
            out_specs=picked_specs(seq_count, slim, columns) + picked_specs(1, back_slim, model),
            scratch_shapes=[
                pltpu.VMEM((seq_count, 4, slim, columns), full),
                pltpu.VMEM((1, 4, back_slim, model), full),
            ],
        ),
        out_shape=picked_shapes(seq_count, slim, columns) + picked_shapes(1, back_slim, model),
        compiler_params=pltpu.CompilerParams(vmem_limit_bytes=vmem_limit),
        cost_estimate=pl.CostEstimate(
            flops=8 * tokens * model * columns,
            bytes_accessed=4 * tokens * model + 4 * model * columns,
            transcendentals=0,
        ),
        name="feed_products",
    )(places, normed, kept, w_in, b_in.reshape(1, -1), w_back)


def swap(blocks, axes):
    return lax.all_to_all(blocks, axes, split_axis=0, concat_axis=0, tiled=True)


def gather_rows(rows):
    return lax.all_gather(rows, "seq", axis=0, tiled=True)


def gather_parts(rows):
    count = lax.axis_size("seq")

    def move(block, distance):
        return lax.ppermute(block, "seq", [(i, i ^ distance) for i in range(count)])

    parts = [rows, None] + [None] * (count - 2)
    for distance in range(2, count, 2):
        parts[distance] = move(rows, distance)
    for distance in range(0, count, 2):
        parts[distance + 1] = move(parts[distance], 1)
    return parts


def trade(block, distance):
    return lax.ppermute(block, "batch", [(i, i ^ distance) for i in range(4)])


def first_sum(got, own, other):
    own = own.astype(full) + got[0].astype(full)
    other = (other.astype(full) + got[1].astype(full)).astype(low)
    return own, other


def together(*values):
    return lax.optimization_barrier(values)


def shards(
    inputs,
    cotangent,
    lengths,
    rand_owners,
    rand_offsets,
    global_ids,
    ln1_gain,
    ln1_shift,
    w_query,
    w_key,
    w_value,
    w_out,
    ln2_gain,
    ln2_shift,
    w_in,
    b_in,
    w_back,
    b_back,
):
    seq_count = lax.axis_size("seq")
    batch_count = lax.axis_size("batch")
    device_count = seq_count * batch_count
    token_count = inputs.shape[1]
    model_width = inputs.shape[2]
    ff_width = w_in.shape[1]
    block_count = token_count // BLK
    head_dim = model_width // HEADS
    scale = head_dim ** (-0.5)
    total_tokens = seq_count * token_count
    head_groups = min(HEADS, seq_count)
    copies = seq_count // head_groups
    head_count = HEADS // head_groups
    width = head_count * head_dim
    tables = (lengths, rand_owners, rand_offsets, global_ids)

    def to_heads(sent):
        if copies > 1:
            sent = jnp.repeat(sent, copies, axis=0)
        return swap(sent, "seq").reshape(total_tokens, -1)

    def to_tokens(rows):
        return swap(rows.reshape(seq_count, token_count, -1), "seq")[::copies]

    rows_in, grad_out = inputs[0], cotangent[0]
    gain_one, gain_two = ln1_gain, ln2_gain
    places = jnp.stack([lax.axis_index("seq"), lax.axis_index("batch")]).astype(jnp.int32)
    parts = gather_parts(rows_in)
    place = lax.axis_index("seq").astype(jnp.int32)
    column = (place // copies).reshape(1)
    weights = [w_query, w_key, w_value]
    if width % 128:
        weights = [
            lax.dynamic_slice_in_dim(w, place // copies * width, width, axis=1) for w in weights
        ]
        column = jnp.zeros_like(column)
    qkv, normed_all = project(
        place ^ jnp.arange(seq_count, dtype=jnp.int32),
        column,
        parts,
        gain_one,
        ln1_shift,
        weights,
        width,
    )
    late_grad_out, qkv = together(grad_out, qkv)
    grad_out_all = gather_rows(late_grad_out)
    attended_all, log_total = attend(tables, qkv, block_count, head_count, scale)
    middle, normed_two = attend_out(
        to_tokens(attended_all), rows_in, w_out, gain_two, ln2_shift
    )
    normed_two_all = gather_rows(normed_two)
    output, grad_middle, grad_middle_low, grad_attended, gain_two_grads, grad_b_in = feed(
        normed_two,
        middle,
        grad_out,
        w_out,
        gain_two,
        b_back,
        w_in,
        b_in,
        w_back,
        head_groups,
        width,
    )
    grad_middle_all = gather_rows(grad_middle_low)
    grad_rows, grad_out_all = together(to_heads(grad_attended), grad_out_all)
    grad_qkv = attend_back(tables, qkv, log_total, grad_rows, block_count, head_count, scale)
    grad_qkv_near = to_tokens(grad_qkv)

    slim = model_width // device_count
    inner_columns = ff_width // seq_count
    qkv_sent, qkv_own, qkv_other = product(
        places, normed_all, model_width, grad_qkv, seq_count, "qkv_product"
    )
    qkv_got = trade(qkv_sent, 1)
    normed_two_all, qkv_own = together(normed_two_all, qkv_own)
    in_sent, in_own, in_other, back_sent, back_own, back_other = feed_products(
        places, normed_two_all, grad_out_all, w_in, b_in, w_back, seq_count
    )
    in_got = trade(in_sent, 1)
    qkv_got, in_own = together(qkv_got, in_own)
    qkv_own, qkv_other = first_sum(qkv_got, qkv_own, qkv_other)
    grad_qkv_near, qkv_other = together(grad_qkv_near, qkv_other)
    qkv_last = trade(qkv_other, 2)
    input_grad, gain_one_grads = project_back(
        rows_in, gain_one, grad_middle, grad_qkv_near, w_query, w_key, w_value
    )
    small = [gain_one_grads[0], gain_one_grads[1], *gain_two_grads, grad_b_in[0]]
    packed = jnp.concatenate([v.reshape(device_count, -1) for v in small], axis=1)
    packed = swap(packed, ("seq", "batch"))
    input_grad, back_sent = together(input_grad, back_sent)
    back_got = trade(back_sent, 1)
    in_got, qkv_last, packed = together(in_got, qkv_last, packed)
    in_own, in_other = first_sum(in_got, in_own, in_other)
    in_last = trade(in_other, 2)
    own_rows = width // copies
    own_attended, in_own = together(attended_all, in_own)
    if copies > 1:
        at = lax.axis_index("seq") % copies * own_rows
        own_attended = lax.dynamic_slice_in_dim(own_attended, at, own_rows, axis=1)
    out_sent, out_own, out_other = product(
        places, own_attended, own_rows, grad_middle_all, 1, "out_product"
    )
    out_got = trade(out_sent, 1)
    in_last, out_got = together(in_last, out_got)
    mixed = [
        (own + last.astype(full)).astype(low)
        for own, last in ((in_own, in_last), (qkv_own, qkv_last))
    ]
    mixed = swap(jnp.concatenate(mixed, axis=2), "seq")
    out_own, out_other = first_sum(out_got, out_own, out_other)
    out_last = trade(out_other, 2)
    back_own, out_last = together(back_own, out_last)
    back_own, back_other = first_sum(back_got, back_own, back_other)
    back_rows = (back_own + trade(back_other, 2).astype(full))[0]
    out_rows = (out_own + out_last.astype(full))[0]
    in_rows = mixed[:, :, :inner_columns].transpose(1, 0, 2).reshape(slim, ff_width).astype(full)
    qkv_rows = mixed[::copies, :, inner_columns:].transpose(1, 0, 2).astype(full)
    qkv_rows = [
        qkv_rows[:, :, i * width : (i + 1) * width].reshape(slim, model_width) for i in range(3)
    ]
    packed = jnp.sum(packed, axis=0)
    cuts, at = [], 0
    for v in small:
        size = v.shape[0] // device_count
        cuts.append(packed[at : at + size])
        at += size
    return (
        output[None],
        input_grad[None],
        cuts[0],
        cuts[1],
        qkv_rows[0],
        qkv_rows[1],
        qkv_rows[2],
        out_rows,
        cuts[2],
        cuts[3],
        in_rows,
        cuts[5],
        back_rows,
        cuts[4],
    )


def solution(mesh):
    rows = P("batch", "seq", None)
    table = P("batch", None, None)
    thin = P(("seq", "batch"))
    wide = P(("seq", "batch"), None)
    return jax.shard_map(
        shards,
        mesh=mesh,
        in_specs=(rows, rows, P("batch", None), table, table, table) + (P(),) * 12,
        out_specs=(rows, rows, thin, thin, wide, wide, wide, wide, thin, thin, wide, thin, wide, thin),
        check_vma=False,
    )
```

```python
import functools

import jax
import jax.numpy as jnp
from jax import lax
from jax.experimental import pallas as pl
from jax.experimental.pallas import tpu as pltpu
from jax.sharding import PartitionSpec as P

HEADS = 16
BLK = 64
RAND = 3
KEY_BLOCKS = 3 + RAND + 2

norm_eps = 1e-05
masked_score = -1e30
vmem_limit = 60 * 2**20
low = jnp.bfloat16
full = jnp.float32


def matmul(left, right):
    return jnp.dot(left, right, preferred_element_type=full)


def matmul_left(left, right):
    return lax.dot_general(left, right, (((0,), (0,)), ((), ())), preferred_element_type=full)


def matmul_right(left, right):
    return lax.dot_general(left, right, (((1,), (1,)), ((), ())), preferred_element_type=full)


def normalize_back(grad_normed, scaled, inverse, ln_gain):
    grad_scaled = grad_normed * ln_gain
    inner_mean = jnp.mean(grad_scaled, axis=-1, keepdims=True)
    along_mean = jnp.mean(grad_scaled * scaled, axis=-1, keepdims=True)
    return inverse * (grad_scaled - inner_mean - scaled * along_mean)


def key_list(step, block_count, total_blocks, lens, owners, offsets, globals_):
    length = lens[0, 0]
    ids = [step - 1, step, step + 1]
    ids += [owners[0, step, r] * block_count + offsets[0, step, r] for r in range(RAND)]
    ids += [globals_[0, 0, g] for g in range(globals_.shape[2])]
    starts, limits = [], []
    for block in ids:
        inside = jnp.logical_and(block >= 0, block < total_blocks)
        clamped = jnp.clip(block, 0, total_blocks - 1)
        starts.append(pl.multiple_of(clamped * BLK, BLK))
        limits.append(jnp.where(inside, length - clamped * BLK, 0))
    return starts, limits


def stack_heads(rows, lanes, head_count):
    if head_count == 1:
        return rows
    zero = jnp.zeros_like(rows)
    return jnp.concatenate([jnp.where(lanes == h, rows, zero) for h in range(head_count)], axis=0)


def merge_heads(stacked, lanes, head_count):
    merged = stacked[:BLK]
    for h in range(1, head_count):
        merged = jnp.where(lanes == h, stacked[h * BLK : (h + 1) * BLK], merged)
    return merged


def masked(score_values, limits, inner_rows):
    parts = [
        jnp.where(inner_rows < limit, score_values[j * BLK : (j + 1) * BLK], masked_score)
        for j, limit in enumerate(limits)
    ]
    return jnp.concatenate(parts, axis=0)


def attend_kernel(
    block_count, head_count, scale, unroll, lens, owners, offsets, globals_, qkv, attended, log_total
):
    total_blocks = qkv.shape[0] // BLK
    width = qkv.shape[1] // 3
    lanes = lax.broadcasted_iota(jnp.int32, (BLK, width), 1) // (width // head_count)
    inner_rows = lax.broadcasted_iota(jnp.int32, (BLK, head_count * BLK), 0)

    def one(step):
        starts, limits = key_list(step, block_count, total_blocks, lens, owners, offsets, globals_)
        row = pl.multiple_of(step * BLK, BLK)
        queries = qkv[pl.ds(row, BLK), 0:width] * jnp.asarray(scale, low)
        query_rows = stack_heads(queries, lanes, head_count)
        keys = jnp.concatenate([qkv[pl.ds(s, BLK), width : 2 * width] for s in starts], axis=0)
        values = jnp.concatenate([qkv[pl.ds(s, BLK), 2 * width :] for s in starts], axis=0)
        score_values = masked(matmul_right(keys, query_rows), limits, inner_rows)
        top = jnp.max(score_values, axis=0, keepdims=True)
        raised = jnp.exp(score_values - top)
        total = jnp.sum(raised, axis=0, keepdims=True)
        weights = (raised * (1.0 / total)).astype(low)
        result = matmul_left(weights, values)
        attended[pl.ds(row, BLK), :] = merge_heads(result, lanes, head_count).astype(low)
        log_total[step] = top + jnp.log(total)

    def body(index, carry):
        for part in range(unroll):
            one(index * unroll + part)
        return carry

    lax.fori_loop(0, total_blocks // unroll, body, 0)


def attend_back_kernel(
    block_count,
    head_count,
    scale,
    unroll,
    lens,
    owners,
    offsets,
    globals_,
    qkv,
    log_total,
    grad_attended,
    grad_qkv,
    sums,
    parts,
):
    total_blocks = qkv.shape[0] // BLK
    width = qkv.shape[1] // 3
    lanes = lax.broadcasted_iota(jnp.int32, (BLK, width), 1) // (width // head_count)
    inner_rows = lax.broadcasted_iota(jnp.int32, (BLK, head_count * BLK), 0)
    sums[...] = jnp.zeros_like(sums)

    def one(step, part):
        starts, limits = key_list(step, block_count, total_blocks, lens, owners, offsets, globals_)
        row = pl.multiple_of(step * BLK, BLK)
        queries = qkv[pl.ds(row, BLK), 0:width] * jnp.asarray(scale, low)
        query_rows = stack_heads(queries, lanes, head_count)
        grad_rows = stack_heads(grad_attended[pl.ds(row, BLK), :], lanes, head_count)
        keys = jnp.concatenate([qkv[pl.ds(s, BLK), width : 2 * width] for s in starts], axis=0)
        values = jnp.concatenate([qkv[pl.ds(s, BLK), 2 * width :] for s in starts], axis=0)
        score_values = masked(matmul_right(keys, query_rows), limits, inner_rows)
        probs = jnp.exp(score_values - log_total[step])
        grad_probs = matmul_right(values, grad_rows)
        correction = jnp.sum(probs * grad_probs, axis=0, keepdims=True)
        grad_scores = (probs * (grad_probs - correction)).astype(low)
        parts[part, :, :width] = matmul(grad_scores, query_rows)
        parts[part, :, width:] = matmul(probs.astype(low), grad_rows)
        grad_queries = merge_heads(matmul_left(grad_scores, keys), lanes, head_count) * scale
        grad_qkv[pl.ds(row, BLK), 0:width] = grad_queries.astype(low)
        return starts

    def body(index, carry):
        lists = [one(index * unroll + part, part) for part in range(unroll)]
        for part, starts in enumerate(lists):
            for j, s in enumerate(starts):
                sums[pl.ds(s, BLK), :] += parts[part, j * BLK : (j + 1) * BLK]
        return carry

    lax.fori_loop(0, total_blocks // unroll, body, 0)
    grad_qkv[:, width:] = sums[...].astype(low)


def unroll_of(steps, most):
    return max(u for u in range(1, most + 1) if steps % u == 0)


smem = pl.BlockSpec(memory_space=pltpu.SMEM)
vmem = pl.BlockSpec(memory_space=pltpu.VMEM)


def attend(tables, qkv, block_count, head_count, scale):
    rows, width = qkv.shape[0], qkv.shape[1] // 3
    total_blocks = rows // BLK
    return pl.pallas_call(
        functools.partial(attend_kernel, block_count, head_count, scale, unroll_of(total_blocks, 8)),
        out_shape=(
            jax.ShapeDtypeStruct((rows, width), low),
            jax.ShapeDtypeStruct((total_blocks, 1, head_count * BLK), full),
        ),
        in_specs=[smem] * 4 + [vmem],
        out_specs=(vmem, vmem),
        compiler_params=pltpu.CompilerParams(vmem_limit_bytes=40 * 2**20),
        cost_estimate=pl.CostEstimate(
            flops=total_blocks * 4 * 128 * 128 * 512, bytes_accessed=rows * width * 8, transcendentals=0
        ),
        name="attend",
    )(*tables, qkv)


def attend_back(tables, qkv, log_total, grad_attended, block_count, head_count, scale):
    rows, width = qkv.shape[0], qkv.shape[1] // 3
    total_blocks = rows // BLK
    return pl.pallas_call(
        functools.partial(attend_back_kernel, block_count, head_count, scale, unroll_of(total_blocks, 8)),
        out_shape=jax.ShapeDtypeStruct((rows, 3 * width), low),
        in_specs=[smem] * 4 + [vmem] * 3,
        out_specs=vmem,
        scratch_shapes=[
            pltpu.VMEM((rows, 2 * width), full),
            pltpu.VMEM((unroll_of(total_blocks, 8), KEY_BLOCKS * BLK, 2 * width), full),
        ],
        compiler_params=pltpu.CompilerParams(vmem_limit_bytes=40 * 2**20),
        cost_estimate=pl.CostEstimate(
            flops=total_blocks * 10 * 128 * 128 * 512, bytes_accessed=rows * width * 16, transcendentals=0
        ),
        name="attend_back",
    )(*tables, qkv, log_total, grad_attended)


def as_row(vector):
    return vector[...].astype(full).reshape(1, -1)


def row_stats(values):
    average = jnp.mean(values, axis=-1, keepdims=True)
    centered = values - average
    variance = jnp.mean(centered * centered, axis=-1, keepdims=True)
    inverse = lax.rsqrt(variance + norm_eps)
    return centered * inverse, inverse


def project_kernel(count, rows, column, *refs):
    parts, (gain, shift, w_query, w_key, w_value) = refs[:count], refs[count : count + 5]
    qkv, normed = refs[-2:]
    weights = jnp.concatenate([w_query[...], w_key[...], w_value[...]], axis=1)
    for i, part in enumerate(parts):
        at = pl.ds(pl.multiple_of(rows[i] * part.shape[0], part.shape[0]), part.shape[0])
        scaled, _ = row_stats(part[...].astype(full))
        result = (scaled * as_row(gain) + as_row(shift)).astype(low)
        normed[at, :] = result
        qkv[at, :] = matmul(result, weights).astype(low)


def project(rows, column, parts, gain, shift, weights, width):
    count = len(parts)
    tokens, model = parts[0].shape
    whole = pl.BlockSpec((tokens, model), lambda j, rows, column: (0, 0))
    row = pl.BlockSpec((model,), lambda j, rows, column: (0,))
    weight = pl.BlockSpec((model, width), lambda j, rows, column: (0, column[0]))
    return pl.pallas_call(
        functools.partial(project_kernel, count),
        grid_spec=pltpu.PrefetchScalarGridSpec(
            num_scalar_prefetch=2,
            grid=(1,),
            in_specs=[whole] * count + [row, row] + [weight] * 3,
            out_specs=(
                pl.BlockSpec((count * tokens, 3 * width), lambda j, rows, column: (0, 0)),
                pl.BlockSpec((count * tokens, model), lambda j, rows, column: (0, 0)),
            ),
        ),
        out_shape=(
            jax.ShapeDtypeStruct((count * tokens, 3 * width), low),
            jax.ShapeDtypeStruct((count * tokens, model), low),
        ),
        compiler_params=pltpu.CompilerParams(vmem_limit_bytes=vmem_limit),
        cost_estimate=pl.CostEstimate(
            flops=6 * count * tokens * model * width,
            bytes_accessed=4 * count * tokens * model,
            transcendentals=0,
        ),
        name="project",
    )(rows, column, *parts, gain, shift, *weights)


def project_back_kernel(
    width, inputs, gain, grad_middle, received, w_query, w_key, w_value, input_grad, gain_grads, total
):
    step = pl.program_id(0)

    @pl.when(step == 0)
    def _():
        total[...] = jnp.zeros_like(total)

    result = total[...]
    for part, weight in enumerate((w_query, w_key, w_value)):
        pieces = [
            received[i, :, part * width : (part + 1) * width] for i in range(received.shape[0])
        ]
        result += matmul_right(jnp.concatenate(pieces, axis=1), weight[...])
    total[...] = result

    @pl.when(step == pl.num_programs(0) - 1)
    def _():
        grad_normed = total[...]
        scaled, inverse = row_stats(inputs[...].astype(full))
        back = normalize_back(grad_normed, scaled, inverse, as_row(gain))
        input_grad[...] = (grad_middle[...] + back).astype(low)
        gain_grads[0:1, :] = jnp.sum(grad_normed * scaled, axis=0, keepdims=True)
        gain_grads[1:2, :] = jnp.sum(grad_normed, axis=0, keepdims=True)


def project_back(inputs, gain, grad_middle, received, w_query, w_key, w_value):
    tokens, model = inputs.shape
    columns = 256
    width = received.shape[2] // 3
    per_step = columns // width
    weight = pl.BlockSpec((model, columns), lambda j: (0, j))
    row = pl.BlockSpec((model,), lambda j: (0,))
    whole = pl.BlockSpec((tokens, model), lambda j: (0, 0))
    return pl.pallas_call(
        functools.partial(project_back_kernel, width),
        grid=(model // columns,),
        out_shape=(
            jax.ShapeDtypeStruct((tokens, model), low),
            jax.ShapeDtypeStruct((2, model), full),
        ),
        in_specs=[
            whole,
            row,
            whole,
            pl.BlockSpec((per_step, tokens, 3 * width), lambda j: (j, 0, 0)),
            weight,
            weight,
            weight,
        ],
        out_specs=(whole, pl.BlockSpec((2, model), lambda j: (0, 0))),
        scratch_shapes=[pltpu.VMEM((tokens, model), full)],
        compiler_params=pltpu.CompilerParams(vmem_limit_bytes=vmem_limit),
        cost_estimate=pl.CostEstimate(
            flops=6 * tokens * model * model, bytes_accessed=6 * model * model, transcendentals=0
        ),
        name="project_back",
    )(inputs, gain, grad_middle, received, w_query, w_key, w_value)


def hidden(normed, grad_out, w_in, b_in, w_back):
    inner = matmul(normed, w_in) + as_row(b_in)
    share = 0.5 * (1.0 + lax.erf(inner * 0.7071067811865476))
    density = jnp.exp(inner * inner * -0.5) * 0.3989422804014327
    grad_active = matmul_right(grad_out, w_back)
    grads = (grad_active * (share + inner * density)).astype(low)
    return (inner * share).astype(low), grads


def feed_kernel(
    received,
    inputs,
    grad_out,
    w_out,
    gain,
    shift,
    b_back,
    w_in,
    b_in,
    w_back,
    output,
    normed,
    grad_middle,
    grad_middle_low,
    grad_attended,
    gain_grads,
    b_in_grad,
    held_out,
    held_in,
    held_back,
    scaled,
    out_total,
    grad_total,
    arrived,
):
    groups, _, width = received.shape
    pieces, _, columns = held_in.shape
    first = pltpu.make_async_copy(w_out, held_out, arrived.at[2, 0])
    loads = []
    for i in range(pieces):
        at = pl.ds(i * columns, columns)
        loads.append(
            (
                pltpu.make_async_copy(w_in.at[:, at], held_in.at[i], arrived.at[0, i]),
                pltpu.make_async_copy(w_back.at[at, :], held_back.at[i], arrived.at[1, i]),
            )
        )
    first.start()
    for pair in loads:
        for load in pair:
            load.start()
    first.wait()
    attended = jnp.concatenate([received[i] for i in range(groups)], axis=1)
    rows = inputs[...].astype(full) + matmul(attended, held_out[...])
    unit, rate = row_stats(rows)
    scaled[...] = unit
    normed[...] = (unit * as_row(gain) + as_row(shift)).astype(low)
    out_total[...] = rows + as_row(b_back)
    for i, pair in enumerate(loads):
        at = slice(i * columns, (i + 1) * columns)
        for load in pair:
            load.wait()
        active, grads = hidden(
            normed[...], grad_out[...], held_in[i], b_in[at], held_back[i]
        )
        b_in_grad[:, at] = jnp.sum(grads.astype(full), axis=0, keepdims=True)
        out_total[...] += matmul(active, held_back[i])
        back = matmul_right(grads, held_in[i])
        if i:
            back += grad_total[...]
        grad_total[...] = back
    output[...] = out_total[...].astype(low)
    grad_normed = grad_total[...]
    unit = scaled[...]
    grad_full = grad_out[...].astype(full)
    grads_middle = grad_full + normalize_back(grad_normed, unit, rate, as_row(gain))
    grad_middle[...] = grads_middle
    grads_low = grads_middle.astype(low)
    grad_middle_low[...] = grads_low
    result = matmul_right(grads_low, held_out[...]).astype(low)
    for i in range(groups):
        grad_attended[i] = result[:, i * width : (i + 1) * width]
    gain_grads[0:1, :] = jnp.sum(grad_normed * unit, axis=0, keepdims=True)
    gain_grads[1:2, :] = jnp.sum(grad_normed, axis=0, keepdims=True)
    gain_grads[2:3, :] = jnp.sum(grad_full, axis=0, keepdims=True)


def feed(received, inputs, grad_out, w_out, gain, shift, b_back, w_in, b_in, w_back):
    tokens, model = inputs.shape
    ff = w_in.shape[1]
    groups, _, width = received.shape
    columns = 1024
    pieces = ff // columns
    anywhere = pl.BlockSpec(memory_space=pl.ANY)
    return pl.pallas_call(
        feed_kernel,
        out_shape=(
            jax.ShapeDtypeStruct((tokens, model), low),
            jax.ShapeDtypeStruct((tokens, model), low),
            jax.ShapeDtypeStruct((tokens, model), full),
            jax.ShapeDtypeStruct((tokens, model), low),
            jax.ShapeDtypeStruct((groups, tokens, width), low),
            jax.ShapeDtypeStruct((3, model), full),
            jax.ShapeDtypeStruct((1, ff), full),
        ),
        in_specs=[vmem, vmem, vmem, anywhere, vmem, vmem, vmem, anywhere, vmem, anywhere],
        out_specs=(vmem,) * 7,
        scratch_shapes=[
            pltpu.VMEM((model, model), low),
            pltpu.VMEM((pieces, model, columns), low),
            pltpu.VMEM((pieces, columns, model), low),
            pltpu.VMEM((tokens, model), full),
            pltpu.VMEM((tokens, model), full),
            pltpu.VMEM((tokens, model), full),
            pltpu.SemaphoreType.DMA((3, pieces)),
        ],
        compiler_params=pltpu.CompilerParams(vmem_limit_bytes=vmem_limit),
        cost_estimate=pl.CostEstimate(
            flops=8 * tokens * model * ff, bytes_accessed=4 * model * ff, transcendentals=0
        ),
        name="feed",
    )(received, inputs, grad_out, w_out, gain, shift, b_back, w_in, b_in, w_back)


def pick_blocks(index, total, sent, own, other):
    def block(distance):
        return total[:, pl.ds(index ^ distance, 1)][:, 0].astype(low)

    sent[0] = block(1)
    sent[1] = block(3)
    own[...] = block(0)
    other[...] = block(2)


def picked_shapes(outer, rows, columns):
    shape = (outer, rows, columns)
    return [jax.ShapeDtypeStruct((2,) + shape, low)] + [jax.ShapeDtypeStruct(shape, low)] * 2


def picked_specs(outer, rows, columns):
    whole = pl.BlockSpec((outer, rows, columns), lambda j, places: (0, 0, 0))
    return [pl.BlockSpec((2, outer, rows, columns), lambda j, places: (0, 0, 0, 0)), whole, whole]


def accumulate(total, value):
    @pl.when(pl.program_id(0) == 0)
    def _():
        total[...] = value.reshape(total.shape)

    @pl.when(pl.program_id(0) > 0)
    def _():
        total[...] += value.reshape(total.shape)


def product_kernel(places, left, right, sent, own, other, total):
    accumulate(total, matmul_left(left[...], right[...]))

    @pl.when(pl.program_id(0) == pl.num_programs(0) - 1)
    def _():
        pick_blocks(places[1], total, sent, own, other)


def product(places, left, left_columns, right, outer, name):
    tokens, columns = right.shape
    chunk = 768
    rows = left_columns // (4 * outer)
    return pl.pallas_call(
        product_kernel,
        grid_spec=pltpu.PrefetchScalarGridSpec(
            num_scalar_prefetch=1,
            grid=(tokens // chunk,),
            in_specs=[
                pl.BlockSpec((chunk, left_columns), lambda j, places: (j, 0)),
                pl.BlockSpec((chunk, columns), lambda j, places: (j, 0)),
            ],
            out_specs=picked_specs(outer, rows, columns),
            scratch_shapes=[pltpu.VMEM((outer, 4, rows, columns), full)],
        ),
        out_shape=picked_shapes(outer, rows, columns),
        compiler_params=pltpu.CompilerParams(vmem_limit_bytes=vmem_limit),
        cost_estimate=pl.CostEstimate(
            flops=2 * tokens * left_columns * columns,
            bytes_accessed=2 * tokens * (left_columns + columns),
            transcendentals=0,
        ),
        name=name,
    )(places, left, right)


def feed_products_kernel(
    places,
    normed,
    grad_out,
    w_in,
    b_in,
    w_back,
    in_sent,
    in_own,
    in_other,
    back_sent,
    back_own,
    back_other,
    in_total,
    back_total,
):
    active, grads = hidden(normed[...], grad_out[...], w_in[...], b_in, w_back[...])
    accumulate(in_total, matmul_left(normed[...], grads))
    accumulate(back_total, matmul_left(active, grad_out[...]))

    @pl.when(pl.program_id(0) == pl.num_programs(0) - 1)
    def _():
        pick_blocks(places[1], in_total, in_sent, in_own, in_other)
        pick_blocks(places[1], back_total, back_sent, back_own, back_other)


def feed_products(places, normed, kept, w_in, b_in, w_back, seq_count):
    tokens, model = normed.shape
    columns = w_in.shape[1] // seq_count
    chunk = 768
    slim = model // (4 * seq_count)
    back_slim = columns // 4
    return pl.pallas_call(
        feed_products_kernel,
        grid_spec=pltpu.PrefetchScalarGridSpec(
            num_scalar_prefetch=1,
            grid=(tokens // chunk,),
            in_specs=[
                pl.BlockSpec((chunk, model), lambda j, places: (j, 0)),
                pl.BlockSpec((chunk, model), lambda j, places: (j, 0)),
                pl.BlockSpec((model, columns), lambda j, places: (0, places[0])),
                pl.BlockSpec((1, columns), lambda j, places: (0, places[0])),
                pl.BlockSpec((columns, model), lambda j, places: (places[0], 0)),
            ],
            out_specs=picked_specs(seq_count, slim, columns) + picked_specs(1, back_slim, model),
            scratch_shapes=[
                pltpu.VMEM((seq_count, 4, slim, columns), full),
                pltpu.VMEM((1, 4, back_slim, model), full),
            ],
        ),
        out_shape=picked_shapes(seq_count, slim, columns) + picked_shapes(1, back_slim, model),
        compiler_params=pltpu.CompilerParams(vmem_limit_bytes=vmem_limit),
        cost_estimate=pl.CostEstimate(
            flops=8 * tokens * model * columns,
            bytes_accessed=4 * tokens * model + 4 * model * columns,
            transcendentals=0,
        ),
        name="feed_products",
    )(places, normed, kept, w_in, b_in.reshape(1, -1), w_back)


def swap(blocks, axes):
    return lax.all_to_all(blocks, axes, split_axis=0, concat_axis=0, tiled=True)


def gather_rows(rows):
    return lax.all_gather(rows, "seq", axis=0, tiled=True)


def gather_parts(rows):
    count = lax.axis_size("seq")

    def move(block, distance):
        return lax.ppermute(block, "seq", [(i, i ^ distance) for i in range(count)])

    parts = [rows, None] + [None] * (count - 2)
    for distance in range(2, count, 2):
        parts[distance] = move(rows, distance)
    for distance in range(0, count, 2):
        parts[distance + 1] = move(parts[distance], 1)
    return parts


def trade(block, distance):
    return lax.ppermute(block, "batch", [(i, i ^ distance) for i in range(4)])


def first_sum(got, own, other):
    own = own.astype(full) + got[0].astype(full)
    other = (other.astype(full) + got[1].astype(full)).astype(low)
    return own, other


def together(*values):
    return lax.optimization_barrier(values)


def shards(
    inputs,
    cotangent,
    lengths,
    rand_owners,
    rand_offsets,
    global_ids,
    ln1_gain,
    ln1_shift,
    w_query,
    w_key,
    w_value,
    w_out,
    ln2_gain,
    ln2_shift,
    w_in,
    b_in,
    w_back,
    b_back,
):
    seq_count = lax.axis_size("seq")
    batch_count = lax.axis_size("batch")
    device_count = seq_count * batch_count
    token_count = inputs.shape[1]
    model_width = inputs.shape[2]
    ff_width = w_in.shape[1]
    block_count = token_count // BLK
    head_dim = model_width // HEADS
    scale = head_dim ** (-0.5)
    total_tokens = seq_count * token_count
    head_groups = min(HEADS, seq_count)
    copies = seq_count // head_groups
    head_count = HEADS // head_groups
    width = head_count * head_dim
    tables = (lengths, rand_owners, rand_offsets, global_ids)

    def to_heads(sent):
        if copies > 1:
            sent = jnp.repeat(sent, copies, axis=0)
        return swap(sent, "seq").reshape(total_tokens, -1)

    def to_tokens(rows):
        return swap(rows.reshape(seq_count, token_count, -1), "seq")[::copies]

    rows_in, grad_out = inputs[0], cotangent[0]
    gain_one, gain_two = ln1_gain, ln2_gain
    places = jnp.stack([lax.axis_index("seq"), lax.axis_index("batch")]).astype(jnp.int32)
    parts = gather_parts(rows_in)
    place = lax.axis_index("seq").astype(jnp.int32)
    column = (place // copies).reshape(1)
    weights = [w_query, w_key, w_value]
    if width % 128:
        weights = [
            lax.dynamic_slice_in_dim(w, place // copies * width, width, axis=1) for w in weights
        ]
        column = jnp.zeros_like(column)
    qkv, normed_all = project(
        place ^ jnp.arange(seq_count, dtype=jnp.int32),
        column,
        parts,
        gain_one,
        ln1_shift,
        weights,
        width,
    )
    late_grad_out, qkv = together(grad_out, qkv)
    grad_out_all = gather_rows(late_grad_out)
    attended_all, log_total = attend(tables, qkv, block_count, head_count, scale)
    output, normed_two, grad_middle, grad_middle_low, grad_attended, gain_two_grads, grad_b_in = feed(
        to_tokens(attended_all),
        rows_in,
        grad_out,
        w_out,
        gain_two,
        ln2_shift,
        b_back,
        w_in,
        b_in,
        w_back,
    )
    normed_two_all = gather_rows(normed_two)
    grad_middle_all = gather_rows(grad_middle_low)
    grad_rows, grad_out_all = together(to_heads(grad_attended), grad_out_all)
    grad_qkv = attend_back(tables, qkv, log_total, grad_rows, block_count, head_count, scale)
    grad_qkv_near = to_tokens(grad_qkv)

    slim = model_width // device_count
    inner_columns = ff_width // seq_count
    qkv_sent, qkv_own, qkv_other = product(
        places, normed_all, model_width, grad_qkv, seq_count, "qkv_product"
    )
    qkv_got = trade(qkv_sent, 1)
    normed_two_all, qkv_own = together(normed_two_all, qkv_own)
    in_sent, in_own, in_other, back_sent, back_own, back_other = feed_products(
        places, normed_two_all, grad_out_all, w_in, b_in, w_back, seq_count
    )
    in_got = trade(in_sent, 1)
    qkv_got, in_own = together(qkv_got, in_own)
    qkv_own, qkv_other = first_sum(qkv_got, qkv_own, qkv_other)
    grad_qkv_near, qkv_other = together(grad_qkv_near, qkv_other)
    qkv_last = trade(qkv_other, 2)
    input_grad, gain_one_grads = project_back(
        rows_in, gain_one, grad_middle, grad_qkv_near, w_query, w_key, w_value
    )
    small = [gain_one_grads[0], gain_one_grads[1], *gain_two_grads, grad_b_in[0]]
    packed = jnp.concatenate([v.reshape(device_count, -1) for v in small], axis=1)
    packed = swap(packed, ("seq", "batch"))
    input_grad, back_sent = together(input_grad, back_sent)
    back_got = trade(back_sent, 1)
    in_got, qkv_last, packed = together(in_got, qkv_last, packed)
    in_own, in_other = first_sum(in_got, in_own, in_other)
    in_last = trade(in_other, 2)
    own_rows = width // copies
    own_attended, in_own = together(attended_all, in_own)
    if copies > 1:
        at = lax.axis_index("seq") % copies * own_rows
        own_attended = lax.dynamic_slice_in_dim(own_attended, at, own_rows, axis=1)
    out_sent, out_own, out_other = product(
        places, own_attended, own_rows, grad_middle_all, 1, "out_product"
    )
    out_got = trade(out_sent, 1)
    in_last, out_got = together(in_last, out_got)
    mixed = [
        (own + last.astype(full)).astype(low)
        for own, last in ((in_own, in_last), (qkv_own, qkv_last))
    ]
    mixed = swap(jnp.concatenate(mixed, axis=2), "seq")
    out_own, out_other = first_sum(out_got, out_own, out_other)
    out_last = trade(out_other, 2)
    back_own, out_last = together(back_own, out_last)
    back_own, back_other = first_sum(back_got, back_own, back_other)
    back_rows = (back_own + trade(back_other, 2).astype(full))[0]
    out_rows = (out_own + out_last.astype(full))[0]
    in_rows = mixed[:, :, :inner_columns].transpose(1, 0, 2).reshape(slim, ff_width).astype(full)
    qkv_rows = mixed[::copies, :, inner_columns:].transpose(1, 0, 2).astype(full)
    qkv_rows = [
        qkv_rows[:, :, i * width : (i + 1) * width].reshape(slim, model_width) for i in range(3)
    ]
    packed = jnp.sum(packed, axis=0)
    cuts, at = [], 0
    for v in small:
        size = v.shape[0] // device_count
        cuts.append(packed[at : at + size])
        at += size
    return (
        output[None],
        input_grad[None],
        cuts[0],
        cuts[1],
        qkv_rows[0],
        qkv_rows[1],
        qkv_rows[2],
        out_rows,
        cuts[2],
        cuts[3],
        in_rows,
        cuts[5],
        back_rows,
        cuts[4],
    )


def solution(mesh):
    rows = P("batch", "seq", None)
    table = P("batch", None, None)
    thin = P(("seq", "batch"))
    wide = P(("seq", "batch"), None)
    return jax.shard_map(
        shards,
        mesh=mesh,
        in_specs=(rows, rows, P("batch", None), table, table, table) + (P(),) * 12,
        out_specs=(rows, rows, thin, thin, wide, wide, wide, wide, thin, thin, wide, thin, wide, thin),
        check_vma=False,
    )
```

```python
import functools

import jax
import jax.numpy as jnp
from jax import lax
from jax.experimental import pallas as pl
from jax.experimental.pallas import tpu as pltpu
from jax.sharding import PartitionSpec as P

HEADS = 16
BLK = 64
RAND = 3
KEY_BLOCKS = 3 + RAND + 2

norm_eps = 1e-05
masked_score = -1e30
vmem_limit = 60 * 2**20
low = jnp.bfloat16
full = jnp.float32


def matmul(left, right):
    return jnp.dot(left, right, preferred_element_type=full)


def matmul_left(left, right):
    return lax.dot_general(left, right, (((0,), (0,)), ((), ())), preferred_element_type=full)


def matmul_right(left, right):
    return lax.dot_general(left, right, (((1,), (1,)), ((), ())), preferred_element_type=full)


def normalize_back(grad_normed, scaled, inverse, ln_gain):
    grad_scaled = grad_normed * ln_gain
    inner_mean = jnp.mean(grad_scaled, axis=-1, keepdims=True)
    along_mean = jnp.mean(grad_scaled * scaled, axis=-1, keepdims=True)
    return inverse * (grad_scaled - inner_mean - scaled * along_mean)


def key_list(step, block_count, total_blocks, lens, owners, offsets, globals_):
    length = lens[0, 0]
    ids = [step - 1, step, step + 1]
    ids += [owners[0, step, r] * block_count + offsets[0, step, r] for r in range(RAND)]
    ids += [globals_[0, 0, g] for g in range(globals_.shape[2])]
    starts, limits = [], []
    for block in ids:
        inside = jnp.logical_and(block >= 0, block < total_blocks)
        clamped = jnp.clip(block, 0, total_blocks - 1)
        starts.append(pl.multiple_of(clamped * BLK, BLK))
        limits.append(jnp.where(inside, length - clamped * BLK, 0))
    return starts, limits


def stack_heads(rows, lanes, head_count):
    if head_count == 1:
        return rows
    zero = jnp.zeros_like(rows)
    return jnp.concatenate([jnp.where(lanes == h, rows, zero) for h in range(head_count)], axis=0)


def merge_heads(stacked, lanes, head_count):
    merged = stacked[:BLK]
    for h in range(1, head_count):
        merged = jnp.where(lanes == h, stacked[h * BLK : (h + 1) * BLK], merged)
    return merged


def masked(score_values, limits, inner_rows):
    parts = [
        jnp.where(inner_rows < limit, score_values[j * BLK : (j + 1) * BLK], masked_score)
        for j, limit in enumerate(limits)
    ]
    return jnp.concatenate(parts, axis=0)


def attend_kernel(
    block_count, head_count, scale, unroll, lens, owners, offsets, globals_, qkv, attended, log_total
):
    total_blocks = qkv.shape[0] // BLK
    width = qkv.shape[1] // 3
    lanes = lax.broadcasted_iota(jnp.int32, (BLK, width), 1) // (width // head_count)
    inner_rows = lax.broadcasted_iota(jnp.int32, (BLK, head_count * BLK), 0)

    def one(step):
        starts, limits = key_list(step, block_count, total_blocks, lens, owners, offsets, globals_)
        row = pl.multiple_of(step * BLK, BLK)
        queries = qkv[pl.ds(row, BLK), 0:width] * jnp.asarray(scale, low)
        query_rows = stack_heads(queries, lanes, head_count)
        keys = jnp.concatenate([qkv[pl.ds(s, BLK), width : 2 * width] for s in starts], axis=0)
        values = jnp.concatenate([qkv[pl.ds(s, BLK), 2 * width :] for s in starts], axis=0)
        score_values = masked(matmul_right(keys, query_rows), limits, inner_rows)
        top = jnp.max(score_values, axis=0, keepdims=True)
        raised = jnp.exp(score_values - top)
        total = jnp.sum(raised, axis=0, keepdims=True)
        weights = (raised * (1.0 / total)).astype(low)
        result = matmul_left(weights, values)
        attended[pl.ds(row, BLK), :] = merge_heads(result, lanes, head_count).astype(low)
        log_total[step] = top + jnp.log(total)

    def body(index, carry):
        for part in range(unroll):
            one(index * unroll + part)
        return carry

    lax.fori_loop(0, total_blocks // unroll, body, 0)


def attend_back_kernel(
    block_count,
    head_count,
    scale,
    unroll,
    lens,
    owners,
    offsets,
    globals_,
    qkv,
    log_total,
    grad_attended,
    grad_qkv,
    sums,
    parts,
):
    total_blocks = qkv.shape[0] // BLK
    width = qkv.shape[1] // 3
    lanes = lax.broadcasted_iota(jnp.int32, (BLK, width), 1) // (width // head_count)
    inner_rows = lax.broadcasted_iota(jnp.int32, (BLK, head_count * BLK), 0)
    sums[...] = jnp.zeros_like(sums)

    def one(step, part):
        starts, limits = key_list(step, block_count, total_blocks, lens, owners, offsets, globals_)
        row = pl.multiple_of(step * BLK, BLK)
        queries = qkv[pl.ds(row, BLK), 0:width] * jnp.asarray(scale, low)
        query_rows = stack_heads(queries, lanes, head_count)
        grad_rows = stack_heads(grad_attended[pl.ds(row, BLK), :], lanes, head_count)
        keys = jnp.concatenate([qkv[pl.ds(s, BLK), width : 2 * width] for s in starts], axis=0)
        values = jnp.concatenate([qkv[pl.ds(s, BLK), 2 * width :] for s in starts], axis=0)
        score_values = masked(matmul_right(keys, query_rows), limits, inner_rows)
        probs = jnp.exp(score_values - log_total[step])
        grad_probs = matmul_right(values, grad_rows)
        correction = jnp.sum(probs * grad_probs, axis=0, keepdims=True)
        grad_scores = (probs * (grad_probs - correction)).astype(low)
        parts[part, :, :width] = matmul(grad_scores, query_rows)
        parts[part, :, width:] = matmul(probs.astype(low), grad_rows)
        grad_queries = merge_heads(matmul_left(grad_scores, keys), lanes, head_count) * scale
        grad_qkv[pl.ds(row, BLK), 0:width] = grad_queries.astype(low)
        return starts

    def body(index, carry):
        lists = [one(index * unroll + part, part) for part in range(unroll)]
        for part, starts in enumerate(lists):
            for j, s in enumerate(starts):
                sums[pl.ds(s, BLK), :] += parts[part, j * BLK : (j + 1) * BLK]
        return carry

    lax.fori_loop(0, total_blocks // unroll, body, 0)
    grad_qkv[:, width:] = sums[...].astype(low)


def unroll_of(steps, most):
    return max(u for u in range(1, most + 1) if steps % u == 0)


smem = pl.BlockSpec(memory_space=pltpu.SMEM)
vmem = pl.BlockSpec(memory_space=pltpu.VMEM)


def attend(tables, qkv, block_count, head_count, scale):
    rows, width = qkv.shape[0], qkv.shape[1] // 3
    total_blocks = rows // BLK
    return pl.pallas_call(
        functools.partial(attend_kernel, block_count, head_count, scale, unroll_of(total_blocks, 8)),
        out_shape=(
            jax.ShapeDtypeStruct((rows, width), low),
            jax.ShapeDtypeStruct((total_blocks, 1, head_count * BLK), full),
        ),
        in_specs=[smem] * 4 + [vmem],
        out_specs=(vmem, vmem),
        compiler_params=pltpu.CompilerParams(vmem_limit_bytes=40 * 2**20),
        cost_estimate=pl.CostEstimate(
            flops=total_blocks * 4 * 128 * 128 * 512, bytes_accessed=rows * width * 8, transcendentals=0
        ),
        name="attend",
    )(*tables, qkv)


def attend_back(tables, qkv, log_total, grad_attended, block_count, head_count, scale):
    rows, width = qkv.shape[0], qkv.shape[1] // 3
    total_blocks = rows // BLK
    return pl.pallas_call(
        functools.partial(attend_back_kernel, block_count, head_count, scale, unroll_of(total_blocks, 8)),
        out_shape=jax.ShapeDtypeStruct((rows, 3 * width), low),
        in_specs=[smem] * 4 + [vmem] * 3,
        out_specs=vmem,
        scratch_shapes=[
            pltpu.VMEM((rows, 2 * width), full),
            pltpu.VMEM((unroll_of(total_blocks, 8), KEY_BLOCKS * BLK, 2 * width), full),
        ],
        compiler_params=pltpu.CompilerParams(vmem_limit_bytes=40 * 2**20),
        cost_estimate=pl.CostEstimate(
            flops=total_blocks * 10 * 128 * 128 * 512, bytes_accessed=rows * width * 16, transcendentals=0
        ),
        name="attend_back",
    )(*tables, qkv, log_total, grad_attended)


def as_row(vector):
    return vector[...].astype(full).reshape(1, -1)


def row_stats(values):
    average = jnp.mean(values, axis=-1, keepdims=True)
    centered = values - average
    variance = jnp.mean(centered * centered, axis=-1, keepdims=True)
    inverse = lax.rsqrt(variance + norm_eps)
    return centered * inverse, inverse


def project_kernel(count, rows, column, *refs):
    parts, (gain, shift, w_query, w_key, w_value) = refs[:count], refs[count : count + 5]
    qkv, normed = refs[-2:]
    weights = jnp.concatenate([w_query[...], w_key[...], w_value[...]], axis=1)
    for i, part in enumerate(parts):
        at = pl.ds(pl.multiple_of(rows[i] * part.shape[0], part.shape[0]), part.shape[0])
        scaled, _ = row_stats(part[...].astype(full))
        result = (scaled * as_row(gain) + as_row(shift)).astype(low)
        normed[at, :] = result
        qkv[at, :] = matmul(result, weights).astype(low)


def project(rows, column, parts, gain, shift, weights, width):
    count = len(parts)
    tokens, model = parts[0].shape
    whole = pl.BlockSpec((tokens, model), lambda j, rows, column: (0, 0))
    row = pl.BlockSpec((model,), lambda j, rows, column: (0,))
    weight = pl.BlockSpec((model, width), lambda j, rows, column: (0, column[0]))
    return pl.pallas_call(
        functools.partial(project_kernel, count),
        grid_spec=pltpu.PrefetchScalarGridSpec(
            num_scalar_prefetch=2,
            grid=(1,),
            in_specs=[whole] * count + [row, row] + [weight] * 3,
            out_specs=(
                pl.BlockSpec((count * tokens, 3 * width), lambda j, rows, column: (0, 0)),
                pl.BlockSpec((count * tokens, model), lambda j, rows, column: (0, 0)),
            ),
        ),
        out_shape=(
            jax.ShapeDtypeStruct((count * tokens, 3 * width), low),
            jax.ShapeDtypeStruct((count * tokens, model), low),
        ),
        compiler_params=pltpu.CompilerParams(vmem_limit_bytes=vmem_limit),
        cost_estimate=pl.CostEstimate(
            flops=6 * count * tokens * model * width,
            bytes_accessed=4 * count * tokens * model,
            transcendentals=0,
        ),
        name="project",
    )(rows, column, *parts, gain, shift, *weights)


def project_back_kernel(
    width, inputs, gain, grad_middle, received, w_query, w_key, w_value, input_grad, gain_grads, total
):
    step = pl.program_id(0)

    @pl.when(step == 0)
    def _():
        total[...] = jnp.zeros_like(total)

    result = total[...]
    for part, weight in enumerate((w_query, w_key, w_value)):
        pieces = [
            received[i, :, part * width : (part + 1) * width] for i in range(received.shape[0])
        ]
        result += matmul_right(jnp.concatenate(pieces, axis=1), weight[...])
    total[...] = result

    @pl.when(step == pl.num_programs(0) - 1)
    def _():
        grad_normed = total[...]
        scaled, inverse = row_stats(inputs[...].astype(full))
        back = normalize_back(grad_normed, scaled, inverse, as_row(gain))
        input_grad[...] = (grad_middle[...] + back).astype(low)
        gain_grads[0:1, :] = jnp.sum(grad_normed * scaled, axis=0, keepdims=True)
        gain_grads[1:2, :] = jnp.sum(grad_normed, axis=0, keepdims=True)


def project_back(inputs, gain, grad_middle, received, w_query, w_key, w_value):
    tokens, model = inputs.shape
    columns = 256
    width = received.shape[2] // 3
    per_step = columns // width
    weight = pl.BlockSpec((model, columns), lambda j: (0, j))
    row = pl.BlockSpec((model,), lambda j: (0,))
    whole = pl.BlockSpec((tokens, model), lambda j: (0, 0))
    return pl.pallas_call(
        functools.partial(project_back_kernel, width),
        grid=(model // columns,),
        out_shape=(
            jax.ShapeDtypeStruct((tokens, model), low),
            jax.ShapeDtypeStruct((2, model), full),
        ),
        in_specs=[
            whole,
            row,
            whole,
            pl.BlockSpec((per_step, tokens, 3 * width), lambda j: (j, 0, 0)),
            weight,
            weight,
            weight,
        ],
        out_specs=(whole, pl.BlockSpec((2, model), lambda j: (0, 0))),
        scratch_shapes=[pltpu.VMEM((tokens, model), full)],
        compiler_params=pltpu.CompilerParams(vmem_limit_bytes=vmem_limit),
        cost_estimate=pl.CostEstimate(
            flops=6 * tokens * model * model, bytes_accessed=6 * model * model, transcendentals=0
        ),
        name="project_back",
    )(inputs, gain, grad_middle, received, w_query, w_key, w_value)


def hidden(normed, grad_out, w_in, b_in, w_back):
    inner = matmul(normed, w_in) + as_row(b_in)
    share = 0.5 * (1.0 + lax.erf(inner * 0.7071067811865476))
    density = jnp.exp(inner * inner * -0.5) * 0.3989422804014327
    grad_active = matmul_right(grad_out, w_back)
    grads = (grad_active * (share + inner * density)).astype(low)
    return (inner * share).astype(low), grads


def feed_kernel(
    received,
    inputs,
    grad_out,
    w_out,
    gain,
    shift,
    b_back,
    w_in,
    b_in,
    w_back,
    output,
    normed,
    grad_middle,
    grad_middle_low,
    grad_attended,
    gain_grads,
    b_in_grad,
    held_out,
    held_in,
    held_back,
    scaled,
    out_total,
    grad_total,
    arrived,
):
    groups, _, width = received.shape
    pieces, _, columns = held_in.shape
    first = pltpu.make_async_copy(w_out, held_out, arrived.at[2, 0])
    loads = []
    for i in range(pieces):
        at = pl.ds(i * columns, columns)
        loads.append(
            (
                pltpu.make_async_copy(w_in.at[:, at], held_in.at[i], arrived.at[0, i]),
                pltpu.make_async_copy(w_back.at[at, :], held_back.at[i], arrived.at[1, i]),
            )
        )
    first.start()
    for pair in loads:
        for load in pair:
            load.start()
    first.wait()
    attended = jnp.concatenate([received[i] for i in range(groups)], axis=1)
    rows = inputs[...].astype(full) + matmul(attended, held_out[...])
    unit, rate = row_stats(rows)
    scaled[...] = unit
    normed[...] = (unit * as_row(gain) + as_row(shift)).astype(low)
    out_total[...] = rows + as_row(b_back)
    for i, pair in enumerate(loads):
        at = slice(i * columns, (i + 1) * columns)
        for load in pair:
            load.wait()
        active, grads = hidden(
            normed[...], grad_out[...], held_in[i], b_in[at], held_back[i]
        )
        b_in_grad[:, at] = jnp.sum(grads.astype(full), axis=0, keepdims=True)
        out_total[...] += matmul(active, held_back[i])
        back = matmul_right(grads, held_in[i])
        if i:
            back += grad_total[...]
        grad_total[...] = back
    output[...] = out_total[...].astype(low)
    grad_normed = grad_total[...]
    unit = scaled[...]
    grad_full = grad_out[...].astype(full)
    grads_middle = grad_full + normalize_back(grad_normed, unit, rate, as_row(gain))
    grad_middle[...] = grads_middle
    grads_low = grads_middle.astype(low)
    grad_middle_low[...] = grads_low
    result = matmul_right(grads_low, held_out[...]).astype(low)
    for i in range(groups):
        grad_attended[i] = result[:, i * width : (i + 1) * width]
    gain_grads[0:1, :] = jnp.sum(grad_normed * unit, axis=0, keepdims=True)
    gain_grads[1:2, :] = jnp.sum(grad_normed, axis=0, keepdims=True)
    gain_grads[2:3, :] = jnp.sum(grad_full, axis=0, keepdims=True)


def feed(received, inputs, grad_out, w_out, gain, shift, b_back, w_in, b_in, w_back):
    tokens, model = inputs.shape
    ff = w_in.shape[1]
    groups, _, width = received.shape
    columns = 1024
    pieces = ff // columns
    anywhere = pl.BlockSpec(memory_space=pl.ANY)
    return pl.pallas_call(
        feed_kernel,
        out_shape=(
            jax.ShapeDtypeStruct((tokens, model), low),
            jax.ShapeDtypeStruct((tokens, model), low),
            jax.ShapeDtypeStruct((tokens, model), full),
            jax.ShapeDtypeStruct((tokens, model), low),
            jax.ShapeDtypeStruct((groups, tokens, width), low),
            jax.ShapeDtypeStruct((3, model), full),
            jax.ShapeDtypeStruct((1, ff), full),
        ),
        in_specs=[vmem, vmem, vmem, anywhere, vmem, vmem, vmem, anywhere, vmem, anywhere],
        out_specs=(vmem,) * 7,
        scratch_shapes=[
            pltpu.VMEM((model, model), low),
            pltpu.VMEM((pieces, model, columns), low),
            pltpu.VMEM((pieces, columns, model), low),
            pltpu.VMEM((tokens, model), full),
            pltpu.VMEM((tokens, model), full),
            pltpu.VMEM((tokens, model), full),
            pltpu.SemaphoreType.DMA((3, pieces)),
        ],
        compiler_params=pltpu.CompilerParams(vmem_limit_bytes=vmem_limit),
        cost_estimate=pl.CostEstimate(
            flops=8 * tokens * model * ff, bytes_accessed=4 * model * ff, transcendentals=0
        ),
        name="feed",
    )(received, inputs, grad_out, w_out, gain, shift, b_back, w_in, b_in, w_back)


def pick_blocks(index, total, sent, own, other):
    def block(distance):
        return total[:, pl.ds(index ^ distance, 1)][:, 0].astype(low)

    sent[0] = block(1)
    sent[1] = block(3)
    own[...] = block(0)
    other[...] = block(2)


def picked_shapes(outer, rows, columns):
    shape = (outer, rows, columns)
    return [jax.ShapeDtypeStruct((2,) + shape, low)] + [jax.ShapeDtypeStruct(shape, low)] * 2


def picked_specs(outer, rows, columns):
    whole = pl.BlockSpec((outer, rows, columns), lambda j, places: (0, 0, 0))
    return [pl.BlockSpec((2, outer, rows, columns), lambda j, places: (0, 0, 0, 0)), whole, whole]


def accumulate(total, value):
    @pl.when(pl.program_id(0) == 0)
    def _():
        total[...] = value.reshape(total.shape)

    @pl.when(pl.program_id(0) > 0)
    def _():
        total[...] += value.reshape(total.shape)


def product_kernel(places, left, right, sent, own, other, total):
    accumulate(total, matmul_left(left[...], right[...]))

    @pl.when(pl.program_id(0) == pl.num_programs(0) - 1)
    def _():
        pick_blocks(places[1], total, sent, own, other)


def product(places, left, left_columns, right, outer, name):
    tokens, columns = right.shape
    chunk = 768
    rows = left_columns // (4 * outer)
    return pl.pallas_call(
        product_kernel,
        grid_spec=pltpu.PrefetchScalarGridSpec(
            num_scalar_prefetch=1,
            grid=(tokens // chunk,),
            in_specs=[
                pl.BlockSpec((chunk, left_columns), lambda j, places: (j, 0)),
                pl.BlockSpec((chunk, columns), lambda j, places: (j, 0)),
            ],
            out_specs=picked_specs(outer, rows, columns),
            scratch_shapes=[pltpu.VMEM((outer, 4, rows, columns), full)],
        ),
        out_shape=picked_shapes(outer, rows, columns),
        compiler_params=pltpu.CompilerParams(vmem_limit_bytes=vmem_limit),
        cost_estimate=pl.CostEstimate(
            flops=2 * tokens * left_columns * columns,
            bytes_accessed=2 * tokens * (left_columns + columns),
            transcendentals=0,
        ),
        name=name,
    )(places, left, right)


def whole_product_kernel(left, right, result, total):
    accumulate(total, matmul_left(left[...], right[...]))

    @pl.when(pl.program_id(0) == pl.num_programs(0) - 1)
    def _():
        result[...] = total[...].astype(low)


def whole_product(left, right, name):
    tokens, columns = right.shape
    rows = left.shape[1]
    chunk = 768
    return pl.pallas_call(
        whole_product_kernel,
        grid=(tokens // chunk,),
        in_specs=[
            pl.BlockSpec((chunk, rows), lambda j: (j, 0)),
            pl.BlockSpec((chunk, columns), lambda j: (j, 0)),
        ],
        out_specs=pl.BlockSpec((rows, columns), lambda j: (0, 0)),
        out_shape=jax.ShapeDtypeStruct((rows, columns), low),
        scratch_shapes=[pltpu.VMEM((rows, columns), full)],
        compiler_params=pltpu.CompilerParams(vmem_limit_bytes=vmem_limit),
        cost_estimate=pl.CostEstimate(
            flops=2 * tokens * rows * columns,
            bytes_accessed=2 * tokens * (rows + columns),
            transcendentals=0,
        ),
        name=name,
    )(left, right)


def feed_products_kernel(
    places,
    normed,
    grad_out,
    w_in,
    b_in,
    w_back,
    in_sent,
    in_own,
    in_other,
    back_sent,
    back_own,
    back_other,
    in_total,
    back_total,
):
    active, grads = hidden(normed[...], grad_out[...], w_in[...], b_in, w_back[...])
    accumulate(in_total, matmul_left(normed[...], grads))
    accumulate(back_total, matmul_left(active, grad_out[...]))

    @pl.when(pl.program_id(0) == pl.num_programs(0) - 1)
    def _():
        pick_blocks(places[1], in_total, in_sent, in_own, in_other)
        pick_blocks(places[1], back_total, back_sent, back_own, back_other)


def feed_products(places, normed, kept, w_in, b_in, w_back, seq_count):
    tokens, model = normed.shape
    columns = w_in.shape[1] // seq_count
    chunk = 768
    slim = model // (4 * seq_count)
    back_slim = columns // 4
    return pl.pallas_call(
        feed_products_kernel,
        grid_spec=pltpu.PrefetchScalarGridSpec(
            num_scalar_prefetch=1,
            grid=(tokens // chunk,),
            in_specs=[
                pl.BlockSpec((chunk, model), lambda j, places: (j, 0)),
                pl.BlockSpec((chunk, model), lambda j, places: (j, 0)),
                pl.BlockSpec((model, columns), lambda j, places: (0, places[0])),
                pl.BlockSpec((1, columns), lambda j, places: (0, places[0])),
                pl.BlockSpec((columns, model), lambda j, places: (places[0], 0)),
            ],
            out_specs=picked_specs(seq_count, slim, columns) + picked_specs(1, back_slim, model),
            scratch_shapes=[
                pltpu.VMEM((seq_count, 4, slim, columns), full),
                pltpu.VMEM((1, 4, back_slim, model), full),
            ],
        ),
        out_shape=picked_shapes(seq_count, slim, columns) + picked_shapes(1, back_slim, model),
        compiler_params=pltpu.CompilerParams(vmem_limit_bytes=vmem_limit),
        cost_estimate=pl.CostEstimate(
            flops=8 * tokens * model * columns,
            bytes_accessed=4 * tokens * model + 4 * model * columns,
            transcendentals=0,
        ),
        name="feed_products",
    )(places, normed, kept, w_in, b_in.reshape(1, -1), w_back)


def swap(blocks, axes):
    return lax.all_to_all(blocks, axes, split_axis=0, concat_axis=0, tiled=True)


def gather_rows(rows):
    return lax.all_gather(rows, "seq", axis=0, tiled=True)


def gather_parts(rows):
    count = lax.axis_size("seq")

    def move(block, distance):
        return lax.ppermute(block, "seq", [(i, i ^ distance) for i in range(count)])

    parts = [rows, None] + [None] * (count - 2)
    for distance in range(2, count, 2):
        parts[distance] = move(rows, distance)
    for distance in range(0, count, 2):
        parts[distance + 1] = move(parts[distance], 1)
    return parts


def trade(block, distance):
    return lax.ppermute(block, "batch", [(i, i ^ distance) for i in range(4)])


def first_sum(got, own, other):
    own = own.astype(full) + got[0].astype(full)
    other = (other.astype(full) + got[1].astype(full)).astype(low)
    return own, other


def together(*values):
    return lax.optimization_barrier(values)


def shards(
    inputs,
    cotangent,
    lengths,
    rand_owners,
    rand_offsets,
    global_ids,
    ln1_gain,
    ln1_shift,
    w_query,
    w_key,
    w_value,
    w_out,
    ln2_gain,
    ln2_shift,
    w_in,
    b_in,
    w_back,
    b_back,
):
    seq_count = lax.axis_size("seq")
    batch_count = lax.axis_size("batch")
    device_count = seq_count * batch_count
    token_count = inputs.shape[1]
    model_width = inputs.shape[2]
    ff_width = w_in.shape[1]
    block_count = token_count // BLK
    head_dim = model_width // HEADS
    scale = head_dim ** (-0.5)
    total_tokens = seq_count * token_count
    head_groups = min(HEADS, seq_count)
    copies = seq_count // head_groups
    head_count = HEADS // head_groups
    width = head_count * head_dim
    tables = (lengths, rand_owners, rand_offsets, global_ids)

    def to_heads(sent):
        if copies > 1:
            sent = jnp.repeat(sent, copies, axis=0)
        return swap(sent, "seq").reshape(total_tokens, -1)

    def to_tokens(rows):
        return swap(rows.reshape(seq_count, token_count, -1), "seq")[::copies]

    rows_in, grad_out = inputs[0], cotangent[0]
    gain_one, gain_two = ln1_gain, ln2_gain
    places = jnp.stack([lax.axis_index("seq"), lax.axis_index("batch")]).astype(jnp.int32)
    parts = gather_parts(rows_in)
    place = lax.axis_index("seq").astype(jnp.int32)
    column = (place // copies).reshape(1)
    weights = [w_query, w_key, w_value]
    if width % 128:
        weights = [
            lax.dynamic_slice_in_dim(w, place // copies * width, width, axis=1) for w in weights
        ]
        column = jnp.zeros_like(column)
    qkv, normed_all = project(
        place ^ jnp.arange(seq_count, dtype=jnp.int32),
        column,
        parts,
        gain_one,
        ln1_shift,
        weights,
        width,
    )
    late_grad_out, qkv = together(grad_out, qkv)
    grad_out_all = gather_rows(late_grad_out)
    attended_all, log_total = attend(tables, qkv, block_count, head_count, scale)
    output, normed_two, grad_middle, grad_middle_low, grad_attended, gain_two_grads, grad_b_in = feed(
        to_tokens(attended_all),
        rows_in,
        grad_out,
        w_out,
        gain_two,
        ln2_shift,
        b_back,
        w_in,
        b_in,
        w_back,
    )
    normed_two_all = gather_rows(normed_two)
    grad_middle_all = gather_rows(grad_middle_low)
    grad_rows, grad_out_all = together(to_heads(grad_attended), grad_out_all)
    grad_qkv = attend_back(tables, qkv, log_total, grad_rows, block_count, head_count, scale)
    grad_qkv_near = to_tokens(grad_qkv)

    slim = model_width // device_count
    inner_columns = ff_width // seq_count
    qkv_sent, qkv_own, qkv_other = product(
        places, normed_all, model_width, grad_qkv, seq_count, "qkv_product"
    )
    qkv_got = trade(qkv_sent, 1)
    normed_two_all, qkv_own = together(normed_two_all, qkv_own)
    in_sent, in_own, in_other, back_sent, back_own, back_other = feed_products(
        places, normed_two_all, grad_out_all, w_in, b_in, w_back, seq_count
    )
    in_got = trade(in_sent, 1)
    qkv_got, in_own = together(qkv_got, in_own)
    qkv_own, qkv_other = first_sum(qkv_got, qkv_own, qkv_other)
    grad_qkv_near, qkv_other = together(grad_qkv_near, qkv_other)
    qkv_last = trade(qkv_other, 2)
    input_grad, gain_one_grads = project_back(
        rows_in, gain_one, grad_middle, grad_qkv_near, w_query, w_key, w_value
    )
    small = [gain_one_grads[0], gain_one_grads[1], *gain_two_grads, grad_b_in[0]]
    packed = jnp.concatenate([v.reshape(device_count, -1) for v in small], axis=1)
    packed = swap(packed, ("seq", "batch"))
    input_grad, back_sent = together(input_grad, back_sent)
    back_got = trade(back_sent, 1)
    in_got, qkv_last, packed = together(in_got, qkv_last, packed)
    in_own, in_other = first_sum(in_got, in_own, in_other)
    in_last = trade(in_other, 2)
    own_rows = width // copies
    back_own, back_other = first_sum(back_got, back_own, back_other)
    own_attended, in_own = together(attended_all, in_own)
    if copies > 1:
        at = lax.axis_index("seq") % copies * own_rows
        own_attended = lax.dynamic_slice_in_dim(own_attended, at, own_rows, axis=1)
    out_partial = whole_product(own_attended, grad_middle_all, "out_product")
    out_rows = lax.psum_scatter(out_partial, "batch", scatter_dimension=0, tiled=True).astype(full)
    in_last, back_other = together(in_last, back_other)
    mixed = [
        (own + last.astype(full)).astype(low)
        for own, last in ((in_own, in_last), (qkv_own, qkv_last))
    ]
    mixed = swap(jnp.concatenate(mixed, axis=2), "seq")
    back_rows = (back_own + trade(back_other, 2).astype(full))[0]
    in_rows = mixed[:, :, :inner_columns].transpose(1, 0, 2).reshape(slim, ff_width).astype(full)
    qkv_rows = mixed[::copies, :, inner_columns:].transpose(1, 0, 2).astype(full)
    qkv_rows = [
        qkv_rows[:, :, i * width : (i + 1) * width].reshape(slim, model_width) for i in range(3)
    ]
    packed = jnp.sum(packed, axis=0)
    cuts, at = [], 0
    for v in small:
        size = v.shape[0] // device_count
        cuts.append(packed[at : at + size])
        at += size
    return (
        output[None],
        input_grad[None],
        cuts[0],
        cuts[1],
        qkv_rows[0],
        qkv_rows[1],
        qkv_rows[2],
        out_rows,
        cuts[2],
        cuts[3],
        in_rows,
        cuts[5],
        back_rows,
        cuts[4],
    )


def solution(mesh):
    rows = P("batch", "seq", None)
    table = P("batch", None, None)
    thin = P(("seq", "batch"))
    wide = P(("seq", "batch"), None)
    return jax.shard_map(
        shards,
        mesh=mesh,
        in_specs=(rows, rows, P("batch", None), table, table, table) + (P(),) * 12,
        out_specs=(rows, rows, thin, thin, wide, wide, wide, wide, thin, thin, wide, thin, wide, thin),
        check_vma=False,
    )
```

```python
import functools

import jax
import jax.numpy as jnp
from jax import lax
from jax.experimental import pallas as pl
from jax.experimental.pallas import tpu as pltpu
from jax.sharding import PartitionSpec as P

HEADS = 16
BLK = 64
RAND = 3
KEY_BLOCKS = 3 + RAND + 2

norm_eps = 1e-05
masked_score = -1e30
vmem_limit = 60 * 2**20
low = jnp.bfloat16
full = jnp.float32


def matmul(left, right):
    return jnp.dot(left, right, preferred_element_type=full)


def matmul_left(left, right):
    return lax.dot_general(left, right, (((0,), (0,)), ((), ())), preferred_element_type=full)


def matmul_right(left, right):
    return lax.dot_general(left, right, (((1,), (1,)), ((), ())), preferred_element_type=full)


def normalize_back(grad_normed, scaled, inverse, ln_gain):
    grad_scaled = grad_normed * ln_gain
    inner_mean = jnp.mean(grad_scaled, axis=-1, keepdims=True)
    along_mean = jnp.mean(grad_scaled * scaled, axis=-1, keepdims=True)
    return inverse * (grad_scaled - inner_mean - scaled * along_mean)


def key_list(step, block_count, total_blocks, lens, owners, offsets, globals_):
    length = lens[0, 0]
    ids = [step - 1, step, step + 1]
    ids += [owners[0, step, r] * block_count + offsets[0, step, r] for r in range(RAND)]
    ids += [globals_[0, 0, g] for g in range(globals_.shape[2])]
    starts, limits = [], []
    for block in ids:
        inside = jnp.logical_and(block >= 0, block < total_blocks)
        clamped = jnp.clip(block, 0, total_blocks - 1)
        starts.append(pl.multiple_of(clamped * BLK, BLK))
        limits.append(jnp.where(inside, length - clamped * BLK, 0))
    return starts, limits


def stack_heads(rows, lanes, head_count):
    if head_count == 1:
        return rows
    zero = jnp.zeros_like(rows)
    return jnp.concatenate([jnp.where(lanes == h, rows, zero) for h in range(head_count)], axis=0)


def merge_heads(stacked, lanes, head_count):
    merged = stacked[:BLK]
    for h in range(1, head_count):
        merged = jnp.where(lanes == h, stacked[h * BLK : (h + 1) * BLK], merged)
    return merged


def masked(score_values, limits, inner_rows):
    parts = [
        jnp.where(inner_rows < limit, score_values[j * BLK : (j + 1) * BLK], masked_score)
        for j, limit in enumerate(limits)
    ]
    return jnp.concatenate(parts, axis=0)


def attend_kernel(
    block_count, head_count, scale, unroll, lens, owners, offsets, globals_, qkv, attended, log_total
):
    total_blocks = qkv.shape[0] // BLK
    width = qkv.shape[1] // 3
    lanes = lax.broadcasted_iota(jnp.int32, (BLK, width), 1) // (width // head_count)
    inner_rows = lax.broadcasted_iota(jnp.int32, (BLK, head_count * BLK), 0)

    def one(step):
        starts, limits = key_list(step, block_count, total_blocks, lens, owners, offsets, globals_)
        row = pl.multiple_of(step * BLK, BLK)
        queries = qkv[pl.ds(row, BLK), 0:width] * jnp.asarray(scale, low)
        query_rows = stack_heads(queries, lanes, head_count)
        keys = jnp.concatenate([qkv[pl.ds(s, BLK), width : 2 * width] for s in starts], axis=0)
        values = jnp.concatenate([qkv[pl.ds(s, BLK), 2 * width :] for s in starts], axis=0)
        score_values = masked(matmul_right(keys, query_rows), limits, inner_rows)
        top = jnp.max(score_values, axis=0, keepdims=True)
        raised = jnp.exp(score_values - top)
        total = jnp.sum(raised, axis=0, keepdims=True)
        weights = (raised * (1.0 / total)).astype(low)
        result = matmul_left(weights, values)
        attended[pl.ds(row, BLK), :] = merge_heads(result, lanes, head_count).astype(low)
        log_total[step] = top + jnp.log(total)

    def body(index, carry):
        for part in range(unroll):
            one(index * unroll + part)
        return carry

    lax.fori_loop(0, total_blocks // unroll, body, 0)


def attend_back_kernel(
    block_count,
    head_count,
    scale,
    unroll,
    lens,
    owners,
    offsets,
    globals_,
    qkv,
    log_total,
    grad_attended,
    grad_qkv,
    sums,
    parts,
):
    total_blocks = qkv.shape[0] // BLK
    width = qkv.shape[1] // 3
    lanes = lax.broadcasted_iota(jnp.int32, (BLK, width), 1) // (width // head_count)
    inner_rows = lax.broadcasted_iota(jnp.int32, (BLK, head_count * BLK), 0)
    sums[...] = jnp.zeros_like(sums)

    def one(step, part):
        starts, limits = key_list(step, block_count, total_blocks, lens, owners, offsets, globals_)
        row = pl.multiple_of(step * BLK, BLK)
        queries = qkv[pl.ds(row, BLK), 0:width] * jnp.asarray(scale, low)
        query_rows = stack_heads(queries, lanes, head_count)
        grad_rows = stack_heads(grad_attended[pl.ds(row, BLK), :], lanes, head_count)
        keys = jnp.concatenate([qkv[pl.ds(s, BLK), width : 2 * width] for s in starts], axis=0)
        values = jnp.concatenate([qkv[pl.ds(s, BLK), 2 * width :] for s in starts], axis=0)
        score_values = masked(matmul_right(keys, query_rows), limits, inner_rows)
        probs = jnp.exp(score_values - log_total[step])
        grad_probs = matmul_right(values, grad_rows)
        correction = jnp.sum(probs * grad_probs, axis=0, keepdims=True)
        grad_scores = (probs * (grad_probs - correction)).astype(low)
        parts[part, :, :width] = matmul(grad_scores, query_rows)
        parts[part, :, width:] = matmul(probs.astype(low), grad_rows)
        grad_queries = merge_heads(matmul_left(grad_scores, keys), lanes, head_count) * scale
        grad_qkv[pl.ds(row, BLK), 0:width] = grad_queries.astype(low)
        return starts

    def body(index, carry):
        lists = [one(index * unroll + part, part) for part in range(unroll)]
        for part, starts in enumerate(lists):
            for j, s in enumerate(starts):
                sums[pl.ds(s, BLK), :] += parts[part, j * BLK : (j + 1) * BLK]
        return carry

    lax.fori_loop(0, total_blocks // unroll, body, 0)
    grad_qkv[:, width:] = sums[...].astype(low)


def unroll_of(steps, most):
    return max(u for u in range(1, most + 1) if steps % u == 0)


smem = pl.BlockSpec(memory_space=pltpu.SMEM)
vmem = pl.BlockSpec(memory_space=pltpu.VMEM)


def attend(tables, qkv, block_count, head_count, scale):
    rows, width = qkv.shape[0], qkv.shape[1] // 3
    total_blocks = rows // BLK
    return pl.pallas_call(
        functools.partial(attend_kernel, block_count, head_count, scale, unroll_of(total_blocks, 8)),
        out_shape=(
            jax.ShapeDtypeStruct((rows, width), low),
            jax.ShapeDtypeStruct((total_blocks, 1, head_count * BLK), full),
        ),
        in_specs=[smem] * 4 + [vmem],
        out_specs=(vmem, vmem),
        compiler_params=pltpu.CompilerParams(vmem_limit_bytes=40 * 2**20),
        cost_estimate=pl.CostEstimate(
            flops=total_blocks * 4 * 128 * 128 * 512, bytes_accessed=rows * width * 8, transcendentals=0
        ),
        name="attend",
    )(*tables, qkv)


def attend_back(tables, qkv, log_total, grad_attended, block_count, head_count, scale):
    rows, width = qkv.shape[0], qkv.shape[1] // 3
    total_blocks = rows // BLK
    return pl.pallas_call(
        functools.partial(attend_back_kernel, block_count, head_count, scale, unroll_of(total_blocks, 8)),
        out_shape=jax.ShapeDtypeStruct((rows, 3 * width), low),
        in_specs=[smem] * 4 + [vmem] * 3,
        out_specs=vmem,
        scratch_shapes=[
            pltpu.VMEM((rows, 2 * width), full),
            pltpu.VMEM((unroll_of(total_blocks, 8), KEY_BLOCKS * BLK, 2 * width), full),
        ],
        compiler_params=pltpu.CompilerParams(vmem_limit_bytes=40 * 2**20),
        cost_estimate=pl.CostEstimate(
            flops=total_blocks * 10 * 128 * 128 * 512, bytes_accessed=rows * width * 16, transcendentals=0
        ),
        name="attend_back",
    )(*tables, qkv, log_total, grad_attended)


def as_row(vector):
    return vector[...].astype(full).reshape(1, -1)


def row_stats(values):
    average = jnp.mean(values, axis=-1, keepdims=True)
    centered = values - average
    variance = jnp.mean(centered * centered, axis=-1, keepdims=True)
    inverse = lax.rsqrt(variance + norm_eps)
    return centered * inverse, inverse


def project_kernel(count, rows, column, *refs):
    parts, (gain, shift, w_query, w_key, w_value) = refs[:count], refs[count : count + 5]
    qkv, normed = refs[-2:]
    weights = jnp.concatenate([w_query[...], w_key[...], w_value[...]], axis=1)
    for i, part in enumerate(parts):
        at = pl.ds(pl.multiple_of(rows[i] * part.shape[0], part.shape[0]), part.shape[0])
        scaled, _ = row_stats(part[...].astype(full))
        result = (scaled * as_row(gain) + as_row(shift)).astype(low)
        normed[at, :] = result
        qkv[at, :] = matmul(result, weights).astype(low)


def project(rows, column, parts, gain, shift, weights, width):
    count = len(parts)
    tokens, model = parts[0].shape
    whole = pl.BlockSpec((tokens, model), lambda j, rows, column: (0, 0))
    row = pl.BlockSpec((model,), lambda j, rows, column: (0,))
    weight = pl.BlockSpec((model, width), lambda j, rows, column: (0, column[0]))
    return pl.pallas_call(
        functools.partial(project_kernel, count),
        grid_spec=pltpu.PrefetchScalarGridSpec(
            num_scalar_prefetch=2,
            grid=(1,),
            in_specs=[whole] * count + [row, row] + [weight] * 3,
            out_specs=(
                pl.BlockSpec((count * tokens, 3 * width), lambda j, rows, column: (0, 0)),
                pl.BlockSpec((count * tokens, model), lambda j, rows, column: (0, 0)),
            ),
        ),
        out_shape=(
            jax.ShapeDtypeStruct((count * tokens, 3 * width), low),
            jax.ShapeDtypeStruct((count * tokens, model), low),
        ),
        compiler_params=pltpu.CompilerParams(vmem_limit_bytes=vmem_limit),
        cost_estimate=pl.CostEstimate(
            flops=6 * count * tokens * model * width,
            bytes_accessed=4 * count * tokens * model,
            transcendentals=0,
        ),
        name="project",
    )(rows, column, *parts, gain, shift, *weights)


def project_back_kernel(
    width, inputs, gain, grad_middle, received, w_query, w_key, w_value, input_grad, gain_grads, total
):
    step = pl.program_id(0)

    @pl.when(step == 0)
    def _():
        total[...] = jnp.zeros_like(total)

    result = total[...]
    for part, weight in enumerate((w_query, w_key, w_value)):
        pieces = [
            received[i, :, part * width : (part + 1) * width] for i in range(received.shape[0])
        ]
        result += matmul_right(jnp.concatenate(pieces, axis=1), weight[...])
    total[...] = result

    @pl.when(step == pl.num_programs(0) - 1)
    def _():
        grad_normed = total[...]
        scaled, inverse = row_stats(inputs[...].astype(full))
        back = normalize_back(grad_normed, scaled, inverse, as_row(gain))
        input_grad[...] = (grad_middle[...] + back).astype(low)
        gain_grads[0:1, :] = jnp.sum(grad_normed * scaled, axis=0, keepdims=True)
        gain_grads[1:2, :] = jnp.sum(grad_normed, axis=0, keepdims=True)


def project_back(inputs, gain, grad_middle, received, w_query, w_key, w_value):
    tokens, model = inputs.shape
    columns = 256
    width = received.shape[2] // 3
    per_step = columns // width
    weight = pl.BlockSpec((model, columns), lambda j: (0, j))
    row = pl.BlockSpec((model,), lambda j: (0,))
    whole = pl.BlockSpec((tokens, model), lambda j: (0, 0))
    return pl.pallas_call(
        functools.partial(project_back_kernel, width),
        grid=(model // columns,),
        out_shape=(
            jax.ShapeDtypeStruct((tokens, model), low),
            jax.ShapeDtypeStruct((2, model), full),
        ),
        in_specs=[
            whole,
            row,
            whole,
            pl.BlockSpec((per_step, tokens, 3 * width), lambda j: (j, 0, 0)),
            weight,
            weight,
            weight,
        ],
        out_specs=(whole, pl.BlockSpec((2, model), lambda j: (0, 0))),
        scratch_shapes=[pltpu.VMEM((tokens, model), full)],
        compiler_params=pltpu.CompilerParams(vmem_limit_bytes=vmem_limit),
        cost_estimate=pl.CostEstimate(
            flops=6 * tokens * model * model, bytes_accessed=6 * model * model, transcendentals=0
        ),
        name="project_back",
    )(inputs, gain, grad_middle, received, w_query, w_key, w_value)


def hidden(normed, grad_out, w_in, b_in, w_back):
    inner = matmul(normed, w_in) + as_row(b_in)
    share = 0.5 * (1.0 + lax.erf(inner * 0.7071067811865476))
    density = jnp.exp(inner * inner * -0.5) * 0.3989422804014327
    grad_active = matmul_right(grad_out, w_back)
    grads = (grad_active * (share + inner * density)).astype(low)
    return (inner * share).astype(low), grads


def feed_kernel(
    received,
    inputs,
    grad_out,
    w_out,
    gain,
    shift,
    b_back,
    w_in,
    b_in,
    w_back,
    output,
    normed,
    grad_middle,
    grad_middle_low,
    grad_attended,
    gain_grads,
    b_in_grad,
    held_out,
    held_in,
    held_back,
    scaled,
    out_total,
    grad_total,
    arrived,
):
    groups, _, width = received.shape
    pieces, _, columns = held_in.shape
    first = pltpu.make_async_copy(w_out, held_out, arrived.at[2, 0])
    loads = []
    for i in range(pieces):
        at = pl.ds(i * columns, columns)
        loads.append(
            (
                pltpu.make_async_copy(w_in.at[:, at], held_in.at[i], arrived.at[0, i]),
                pltpu.make_async_copy(w_back.at[at, :], held_back.at[i], arrived.at[1, i]),
            )
        )
    first.start()
    for pair in loads:
        for load in pair:
            load.start()
    first.wait()
    attended = jnp.concatenate([received[i] for i in range(groups)], axis=1)
    rows = inputs[...].astype(full) + matmul(attended, held_out[...])
    unit, rate = row_stats(rows)
    scaled[...] = unit
    normed[...] = (unit * as_row(gain) + as_row(shift)).astype(low)
    out_total[...] = rows + as_row(b_back)
    for i, pair in enumerate(loads):
        at = slice(i * columns, (i + 1) * columns)
        for load in pair:
            load.wait()
        active, grads = hidden(
            normed[...], grad_out[...], held_in[i], b_in[at], held_back[i]
        )
        b_in_grad[:, at] = jnp.sum(grads.astype(full), axis=0, keepdims=True)
        out_total[...] += matmul(active, held_back[i])
        back = matmul_right(grads, held_in[i])
        if i:
            back += grad_total[...]
        grad_total[...] = back
    output[...] = out_total[...].astype(low)
    grad_normed = grad_total[...]
    unit = scaled[...]
    grad_full = grad_out[...].astype(full)
    grads_middle = grad_full + normalize_back(grad_normed, unit, rate, as_row(gain))
    grad_middle[...] = grads_middle
    grads_low = grads_middle.astype(low)
    grad_middle_low[...] = grads_low
    result = matmul_right(grads_low, held_out[...]).astype(low)
    for i in range(groups):
        grad_attended[i] = result[:, i * width : (i + 1) * width]
    gain_grads[0:1, :] = jnp.sum(grad_normed * unit, axis=0, keepdims=True)
    gain_grads[1:2, :] = jnp.sum(grad_normed, axis=0, keepdims=True)
    gain_grads[2:3, :] = jnp.sum(grad_full, axis=0, keepdims=True)


def feed(received, inputs, grad_out, w_out, gain, shift, b_back, w_in, b_in, w_back):
    tokens, model = inputs.shape
    ff = w_in.shape[1]
    groups, _, width = received.shape
    columns = 1024
    pieces = ff // columns
    anywhere = pl.BlockSpec(memory_space=pl.ANY)
    return pl.pallas_call(
        feed_kernel,
        out_shape=(
            jax.ShapeDtypeStruct((tokens, model), low),
            jax.ShapeDtypeStruct((tokens, model), low),
            jax.ShapeDtypeStruct((tokens, model), full),
            jax.ShapeDtypeStruct((tokens, model), low),
            jax.ShapeDtypeStruct((groups, tokens, width), low),
            jax.ShapeDtypeStruct((3, model), full),
            jax.ShapeDtypeStruct((1, ff), full),
        ),
        in_specs=[vmem, vmem, vmem, anywhere, vmem, vmem, vmem, anywhere, vmem, anywhere],
        out_specs=(vmem,) * 7,
        scratch_shapes=[
            pltpu.VMEM((model, model), low),
            pltpu.VMEM((pieces, model, columns), low),
            pltpu.VMEM((pieces, columns, model), low),
            pltpu.VMEM((tokens, model), full),
            pltpu.VMEM((tokens, model), full),
            pltpu.VMEM((tokens, model), full),
            pltpu.SemaphoreType.DMA((3, pieces)),
        ],
        compiler_params=pltpu.CompilerParams(vmem_limit_bytes=vmem_limit),
        cost_estimate=pl.CostEstimate(
            flops=8 * tokens * model * ff, bytes_accessed=4 * model * ff, transcendentals=0
        ),
        name="feed",
    )(received, inputs, grad_out, w_out, gain, shift, b_back, w_in, b_in, w_back)


def pick_blocks(index, total, sent, own, other):
    def block(distance):
        return total[:, pl.ds(index ^ distance, 1)][:, 0].astype(low)

    sent[0] = block(1)
    sent[1] = block(3)
    own[...] = block(0)
    other[...] = block(2)


def picked_shapes(outer, rows, columns):
    shape = (outer, rows, columns)
    return [jax.ShapeDtypeStruct((2,) + shape, low)] + [jax.ShapeDtypeStruct(shape, low)] * 2


def picked_specs(outer, rows, columns):
    whole = pl.BlockSpec((outer, rows, columns), lambda j, places: (0, 0, 0))
    return [pl.BlockSpec((2, outer, rows, columns), lambda j, places: (0, 0, 0, 0)), whole, whole]


def accumulate(total, value):
    @pl.when(pl.program_id(0) == 0)
    def _():
        total[...] = value.reshape(total.shape)

    @pl.when(pl.program_id(0) > 0)
    def _():
        total[...] += value.reshape(total.shape)


def product_kernel(places, left, right, sent, own, other, total):
    accumulate(total, matmul_left(left[...], right[...]))

    @pl.when(pl.program_id(0) == pl.num_programs(0) - 1)
    def _():
        pick_blocks(places[1], total, sent, own, other)


def product(places, left, left_columns, right, outer, name):
    tokens, columns = right.shape
    chunk = 768
    rows = left_columns // (4 * outer)
    return pl.pallas_call(
        product_kernel,
        grid_spec=pltpu.PrefetchScalarGridSpec(
            num_scalar_prefetch=1,
            grid=(tokens // chunk,),
            in_specs=[
                pl.BlockSpec((chunk, left_columns), lambda j, places: (j, 0)),
                pl.BlockSpec((chunk, columns), lambda j, places: (j, 0)),
            ],
            out_specs=picked_specs(outer, rows, columns),
            scratch_shapes=[pltpu.VMEM((outer, 4, rows, columns), full)],
        ),
        out_shape=picked_shapes(outer, rows, columns),
        compiler_params=pltpu.CompilerParams(vmem_limit_bytes=vmem_limit),
        cost_estimate=pl.CostEstimate(
            flops=2 * tokens * left_columns * columns,
            bytes_accessed=2 * tokens * (left_columns + columns),
            transcendentals=0,
        ),
        name=name,
    )(places, left, right)


def whole_product_kernel(left, right, result, total):
    accumulate(total, matmul_left(left[...], right[...]))

    @pl.when(pl.program_id(0) == pl.num_programs(0) - 1)
    def _():
        result[...] = total[...].astype(low)


def whole_product(left, right, name):
    tokens, columns = right.shape
    rows = left.shape[1]
    chunk = 768
    return pl.pallas_call(
        whole_product_kernel,
        grid=(tokens // chunk,),
        in_specs=[
            pl.BlockSpec((chunk, rows), lambda j: (j, 0)),
            pl.BlockSpec((chunk, columns), lambda j: (j, 0)),
        ],
        out_specs=pl.BlockSpec((rows, columns), lambda j: (0, 0)),
        out_shape=jax.ShapeDtypeStruct((rows, columns), low),
        scratch_shapes=[pltpu.VMEM((rows, columns), full)],
        compiler_params=pltpu.CompilerParams(vmem_limit_bytes=vmem_limit),
        cost_estimate=pl.CostEstimate(
            flops=2 * tokens * rows * columns,
            bytes_accessed=2 * tokens * (rows + columns),
            transcendentals=0,
        ),
        name=name,
    )(left, right)


def feed_products_kernel(
    places,
    normed,
    grad_out,
    w_in,
    b_in,
    w_back,
    in_sent,
    in_own,
    in_other,
    back_sent,
    back_own,
    back_other,
    held_normed,
    held_grad,
    held_in,
    held_back,
    active,
    grads,
    in_total,
    back_total,
    arrived,
):
    pieces, chunk, _ = held_normed.shape
    columns = held_in.shape[1]
    own = pl.ds(pl.multiple_of(places[0] * columns, columns), columns)
    weights = (
        pltpu.make_async_copy(w_in.at[:, own], held_in, arrived.at[0, pieces]),
        pltpu.make_async_copy(w_back.at[own, :], held_back, arrived.at[1, pieces]),
    )
    loads = [
        (
            pltpu.make_async_copy(normed.at[pl.ds(i * chunk, chunk)], held_normed.at[i], arrived.at[0, i]),
            pltpu.make_async_copy(grad_out.at[pl.ds(i * chunk, chunk)], held_grad.at[i], arrived.at[1, i]),
        )
        for i in range(pieces)
    ]
    for pair in (weights, *loads):
        for load in pair:
            load.start()
    for load in weights:
        load.wait()
    for i, pair in enumerate(loads):
        for load in pair:
            load.wait()
        active[i], grads[i] = hidden(held_normed[i], held_grad[i], held_in[...], b_in, held_back[...])
    rows = pieces * chunk
    model = held_normed.shape[2]
    in_total[...] = matmul_left(
        held_normed[...].reshape(rows, model), grads[...].reshape(rows, columns)
    ).reshape(in_total.shape)
    pick_blocks(places[1], in_total, in_sent, in_own, in_other)
    back_total[...] = matmul_left(
        active[...].reshape(rows, columns), held_grad[...].reshape(rows, model)
    ).reshape(back_total.shape)
    pick_blocks(places[1], back_total, back_sent, back_own, back_other)


def feed_products(places, normed, grad_out, w_in, b_in, w_back, seq_count):
    tokens, model = normed.shape
    columns = w_in.shape[1] // seq_count
    chunk = 384
    pieces = tokens // chunk
    slim = model // (4 * seq_count)
    back_slim = columns // 4
    anywhere = pl.BlockSpec(memory_space=pl.ANY)
    return pl.pallas_call(
        feed_products_kernel,
        grid_spec=pltpu.PrefetchScalarGridSpec(
            num_scalar_prefetch=1,
            grid=(1,),
            in_specs=[
                anywhere,
                anywhere,
                anywhere,
                pl.BlockSpec((1, columns), lambda j, places: (0, places[0])),
                anywhere,
            ],
            out_specs=picked_specs(seq_count, slim, columns) + picked_specs(1, back_slim, model),
            scratch_shapes=[
                pltpu.VMEM((pieces, chunk, model), low),
                pltpu.VMEM((pieces, chunk, model), low),
                pltpu.VMEM((model, columns), low),
                pltpu.VMEM((columns, model), low),
                pltpu.VMEM((pieces, chunk, columns), low),
                pltpu.VMEM((pieces, chunk, columns), low),
                pltpu.VMEM((seq_count, 4, slim, columns), full),
                pltpu.VMEM((1, 4, back_slim, model), full),
                pltpu.SemaphoreType.DMA((2, pieces + 1)),
            ],
        ),
        out_shape=picked_shapes(seq_count, slim, columns) + picked_shapes(1, back_slim, model),
        compiler_params=pltpu.CompilerParams(vmem_limit_bytes=vmem_limit),
        cost_estimate=pl.CostEstimate(
            flops=8 * tokens * model * columns,
            bytes_accessed=4 * tokens * model + 4 * model * columns,
            transcendentals=0,
        ),
        name="feed_products",
    )(places, normed, grad_out, w_in, b_in.reshape(1, -1), w_back)


def swap(blocks, axes):
    return lax.all_to_all(blocks, axes, split_axis=0, concat_axis=0, tiled=True)


def gather_rows(rows):
    return lax.all_gather(rows, "seq", axis=0, tiled=True)


def gather_parts(rows):
    count = lax.axis_size("seq")

    def move(block, distance):
        return lax.ppermute(block, "seq", [(i, i ^ distance) for i in range(count)])

    parts = [rows, None] + [None] * (count - 2)
    for distance in range(2, count, 2):
        parts[distance] = move(rows, distance)
    for distance in range(0, count, 2):
        parts[distance + 1] = move(parts[distance], 1)
    return parts


def trade(block, distance):
    return lax.ppermute(block, "batch", [(i, i ^ distance) for i in range(4)])


def first_sum(got, own, other):
    own = own.astype(full) + got[0].astype(full)
    other = (other.astype(full) + got[1].astype(full)).astype(low)
    return own, other


def together(*values):
    return lax.optimization_barrier(values)


def shards(
    inputs,
    cotangent,
    lengths,
    rand_owners,
    rand_offsets,
    global_ids,
    ln1_gain,
    ln1_shift,
    w_query,
    w_key,
    w_value,
    w_out,
    ln2_gain,
    ln2_shift,
    w_in,
    b_in,
    w_back,
    b_back,
):
    seq_count = lax.axis_size("seq")
    batch_count = lax.axis_size("batch")
    device_count = seq_count * batch_count
    token_count = inputs.shape[1]
    model_width = inputs.shape[2]
    ff_width = w_in.shape[1]
    block_count = token_count // BLK
    head_dim = model_width // HEADS
    scale = head_dim ** (-0.5)
    total_tokens = seq_count * token_count
    head_groups = min(HEADS, seq_count)
    copies = seq_count // head_groups
    head_count = HEADS // head_groups
    width = head_count * head_dim
    tables = (lengths, rand_owners, rand_offsets, global_ids)

    def to_heads(sent):
        if copies > 1:
            sent = jnp.repeat(sent, copies, axis=0)
        return swap(sent, "seq").reshape(total_tokens, -1)

    def to_tokens(rows):
        return swap(rows.reshape(seq_count, token_count, -1), "seq")[::copies]

    rows_in, grad_out = inputs[0], cotangent[0]
    gain_one, gain_two = ln1_gain, ln2_gain
    places = jnp.stack([lax.axis_index("seq"), lax.axis_index("batch")]).astype(jnp.int32)
    parts = gather_parts(rows_in)
    place = lax.axis_index("seq").astype(jnp.int32)
    column = (place // copies).reshape(1)
    weights = [w_query, w_key, w_value]
    if width % 128:
        weights = [
            lax.dynamic_slice_in_dim(w, place // copies * width, width, axis=1) for w in weights
        ]
        column = jnp.zeros_like(column)
    qkv, normed_all = project(
        place ^ jnp.arange(seq_count, dtype=jnp.int32),
        column,
        parts,
        gain_one,
        ln1_shift,
        weights,
        width,
    )
    late_grad_out, qkv = together(grad_out, qkv)
    grad_out_all = gather_rows(late_grad_out)
    attended_all, log_total = attend(tables, qkv, block_count, head_count, scale)
    output, normed_two, grad_middle, grad_middle_low, grad_attended, gain_two_grads, grad_b_in = feed(
        to_tokens(attended_all),
        rows_in,
        grad_out,
        w_out,
        gain_two,
        ln2_shift,
        b_back,
        w_in,
        b_in,
        w_back,
    )
    normed_two_all = gather_rows(normed_two)
    grad_middle_all = gather_rows(grad_middle_low)
    grad_rows, grad_out_all = together(to_heads(grad_attended), grad_out_all)
    grad_qkv = attend_back(tables, qkv, log_total, grad_rows, block_count, head_count, scale)
    grad_qkv_near = to_tokens(grad_qkv)

    slim = model_width // device_count
    inner_columns = ff_width // seq_count
    qkv_sent, qkv_own, qkv_other = product(
        places, normed_all, model_width, grad_qkv, seq_count, "qkv_product"
    )
    qkv_got = trade(qkv_sent, 1)
    normed_two_all, qkv_own = together(normed_two_all, qkv_own)
    in_sent, in_own, in_other, back_sent, back_own, back_other = feed_products(
        places, normed_two_all, grad_out_all, w_in, b_in, w_back, seq_count
    )
    in_got = trade(in_sent, 1)
    qkv_got, in_own = together(qkv_got, in_own)
    qkv_own, qkv_other = first_sum(qkv_got, qkv_own, qkv_other)
    grad_qkv_near, qkv_other, back_sent = together(grad_qkv_near, qkv_other, back_sent)
    back_got = trade(back_sent, 1)
    qkv_last = trade(qkv_other, 2)
    input_grad, gain_one_grads = project_back(
        rows_in, gain_one, grad_middle, grad_qkv_near, w_query, w_key, w_value
    )
    small = [gain_one_grads[0], gain_one_grads[1], *gain_two_grads, grad_b_in[0]]
    packed = jnp.concatenate([v.reshape(device_count, -1) for v in small], axis=1)
    packed = swap(packed, ("seq", "batch"))
    in_got, qkv_last, packed = together(in_got, qkv_last, packed)
    in_own, in_other = first_sum(in_got, in_own, in_other)
    in_last = trade(in_other, 2)
    own_rows = width // copies
    back_own, back_other = first_sum(back_got, back_own, back_other)
    own_attended, in_own = together(attended_all, in_own)
    if copies > 1:
        at = lax.axis_index("seq") % copies * own_rows
        own_attended = lax.dynamic_slice_in_dim(own_attended, at, own_rows, axis=1)
    out_partial = whole_product(own_attended, grad_middle_all, "out_product")
    out_rows = lax.psum_scatter(out_partial, "batch", scatter_dimension=0, tiled=True).astype(full)
    in_last, back_other = together(in_last, back_other)
    mixed = [
        (own + last.astype(full)).astype(low)
        for own, last in ((in_own, in_last), (qkv_own, qkv_last))
    ]
    mixed = swap(jnp.concatenate(mixed, axis=2), "seq")
    back_rows = (back_own + trade(back_other, 2).astype(full))[0]
    in_rows = mixed[:, :, :inner_columns].transpose(1, 0, 2).reshape(slim, ff_width).astype(full)
    qkv_rows = mixed[::copies, :, inner_columns:].transpose(1, 0, 2).astype(full)
    qkv_rows = [
        qkv_rows[:, :, i * width : (i + 1) * width].reshape(slim, model_width) for i in range(3)
    ]
    packed = jnp.sum(packed, axis=0)
    cuts, at = [], 0
    for v in small:
        size = v.shape[0] // device_count
        cuts.append(packed[at : at + size])
        at += size
    return (
        output[None],
        input_grad[None],
        cuts[0],
        cuts[1],
        qkv_rows[0],
        qkv_rows[1],
        qkv_rows[2],
        out_rows,
        cuts[2],
        cuts[3],
        in_rows,
        cuts[5],
        back_rows,
        cuts[4],
    )


def solution(mesh):
    rows = P("batch", "seq", None)
    table = P("batch", None, None)
    thin = P(("seq", "batch"))
    wide = P(("seq", "batch"), None)
    return jax.shard_map(
        shards,
        mesh=mesh,
        in_specs=(rows, rows, P("batch", None), table, table, table) + (P(),) * 12,
        out_specs=(rows, rows, thin, thin, wide, wide, wide, wide, thin, thin, wide, thin, wide, thin),
        check_vma=False,
    )
```

```python
import functools

import jax
import jax.numpy as jnp
from jax import lax
from jax.experimental import pallas as pl
from jax.experimental.pallas import tpu as pltpu
from jax.sharding import PartitionSpec as P

HEADS = 16
BLK = 64
RAND = 3
KEY_BLOCKS = 3 + RAND + 2

norm_eps = 1e-05
masked_score = -1e30
vmem_limit = 60 * 2**20
low = jnp.bfloat16
full = jnp.float32


def matmul(left, right):
    return jnp.dot(left, right, preferred_element_type=full)


def matmul_left(left, right):
    return lax.dot_general(left, right, (((0,), (0,)), ((), ())), preferred_element_type=full)


def matmul_right(left, right):
    return lax.dot_general(left, right, (((1,), (1,)), ((), ())), preferred_element_type=full)


def normalize_back(grad_normed, scaled, inverse, ln_gain):
    grad_scaled = grad_normed * ln_gain
    inner_mean = jnp.mean(grad_scaled, axis=-1, keepdims=True)
    along_mean = jnp.mean(grad_scaled * scaled, axis=-1, keepdims=True)
    return inverse * (grad_scaled - inner_mean - scaled * along_mean)


def key_list(step, block_count, total_blocks, lens, owners, offsets, globals_):
    length = lens[0, 0]
    ids = [step - 1, step, step + 1]
    ids += [owners[0, step, r] * block_count + offsets[0, step, r] for r in range(RAND)]
    ids += [globals_[0, 0, g] for g in range(globals_.shape[2])]
    starts, limits = [], []
    for block in ids:
        inside = jnp.logical_and(block >= 0, block < total_blocks)
        clamped = jnp.clip(block, 0, total_blocks - 1)
        starts.append(pl.multiple_of(clamped * BLK, BLK))
        limits.append(jnp.where(inside, length - clamped * BLK, 0))
    return starts, limits


def stack_heads(rows, lanes, head_count):
    if head_count == 1:
        return rows
    zero = jnp.zeros_like(rows)
    return jnp.concatenate([jnp.where(lanes == h, rows, zero) for h in range(head_count)], axis=0)


def merge_heads(stacked, lanes, head_count):
    merged = stacked[:BLK]
    for h in range(1, head_count):
        merged = jnp.where(lanes == h, stacked[h * BLK : (h + 1) * BLK], merged)
    return merged


def masked(score_values, limits, inner_rows):
    parts = [
        jnp.where(inner_rows < limit, score_values[j * BLK : (j + 1) * BLK], masked_score)
        for j, limit in enumerate(limits)
    ]
    return jnp.concatenate(parts, axis=0)


def attend_kernel(
    block_count, head_count, scale, unroll, lens, owners, offsets, globals_, qkv, attended, log_total
):
    total_blocks = qkv.shape[0] // BLK
    width = qkv.shape[1] // 3
    lanes = lax.broadcasted_iota(jnp.int32, (BLK, width), 1) // (width // head_count)
    inner_rows = lax.broadcasted_iota(jnp.int32, (BLK, head_count * BLK), 0)

    def one(step):
        starts, limits = key_list(step, block_count, total_blocks, lens, owners, offsets, globals_)
        row = pl.multiple_of(step * BLK, BLK)
        queries = qkv[pl.ds(row, BLK), 0:width] * jnp.asarray(scale, low)
        query_rows = stack_heads(queries, lanes, head_count)
        keys = jnp.concatenate([qkv[pl.ds(s, BLK), width : 2 * width] for s in starts], axis=0)
        values = jnp.concatenate([qkv[pl.ds(s, BLK), 2 * width :] for s in starts], axis=0)
        score_values = masked(matmul_right(keys, query_rows), limits, inner_rows)
        top = jnp.max(score_values, axis=0, keepdims=True)
        raised = jnp.exp(score_values - top)
        total = jnp.sum(raised, axis=0, keepdims=True)
        weights = (raised * (1.0 / total)).astype(low)
        result = matmul_left(weights, values)
        attended[pl.ds(row, BLK), :] = merge_heads(result, lanes, head_count).astype(low)
        log_total[step] = top + jnp.log(total)

    def body(index, carry):
        for part in range(unroll):
            one(index * unroll + part)
        return carry

    lax.fori_loop(0, total_blocks // unroll, body, 0)


def attend_back_kernel(
    block_count,
    head_count,
    scale,
    unroll,
    lens,
    owners,
    offsets,
    globals_,
    qkv,
    log_total,
    grad_attended,
    grad_qkv,
    sums,
    parts,
):
    total_blocks = qkv.shape[0] // BLK
    width = qkv.shape[1] // 3
    lanes = lax.broadcasted_iota(jnp.int32, (BLK, width), 1) // (width // head_count)
    inner_rows = lax.broadcasted_iota(jnp.int32, (BLK, head_count * BLK), 0)
    sums[...] = jnp.zeros_like(sums)

    def one(step, part):
        starts, limits = key_list(step, block_count, total_blocks, lens, owners, offsets, globals_)
        row = pl.multiple_of(step * BLK, BLK)
        queries = qkv[pl.ds(row, BLK), 0:width] * jnp.asarray(scale, low)
        query_rows = stack_heads(queries, lanes, head_count)
        grad_rows = stack_heads(grad_attended[pl.ds(row, BLK), :], lanes, head_count)
        keys = jnp.concatenate([qkv[pl.ds(s, BLK), width : 2 * width] for s in starts], axis=0)
        values = jnp.concatenate([qkv[pl.ds(s, BLK), 2 * width :] for s in starts], axis=0)
        score_values = masked(matmul_right(keys, query_rows), limits, inner_rows)
        probs = jnp.exp(score_values - log_total[step])
        grad_probs = matmul_right(values, grad_rows)
        correction = jnp.sum(probs * grad_probs, axis=0, keepdims=True)
        grad_scores = (probs * (grad_probs - correction)).astype(low)
        parts[part, :, :width] = matmul(grad_scores, query_rows)
        parts[part, :, width:] = matmul(probs.astype(low), grad_rows)
        grad_queries = merge_heads(matmul_left(grad_scores, keys), lanes, head_count) * scale
        grad_qkv[pl.ds(row, BLK), 0:width] = grad_queries.astype(low)
        return starts

    def body(index, carry):
        lists = [one(index * unroll + part, part) for part in range(unroll)]
        for part, starts in enumerate(lists):
            for j, s in enumerate(starts):
                sums[pl.ds(s, BLK), :] += parts[part, j * BLK : (j + 1) * BLK]
        return carry

    lax.fori_loop(0, total_blocks // unroll, body, 0)
    grad_qkv[:, width:] = sums[...].astype(low)


def unroll_of(steps, most):
    return max(u for u in range(1, most + 1) if steps % u == 0)


smem = pl.BlockSpec(memory_space=pltpu.SMEM)
vmem = pl.BlockSpec(memory_space=pltpu.VMEM)


def attend(tables, qkv, block_count, head_count, scale):
    rows, width = qkv.shape[0], qkv.shape[1] // 3
    total_blocks = rows // BLK
    return pl.pallas_call(
        functools.partial(attend_kernel, block_count, head_count, scale, unroll_of(total_blocks, 6)),
        out_shape=(
            jax.ShapeDtypeStruct((rows, width), low),
            jax.ShapeDtypeStruct((total_blocks, 1, head_count * BLK), full),
        ),
        in_specs=[smem] * 4 + [vmem],
        out_specs=(vmem, vmem),
        compiler_params=pltpu.CompilerParams(vmem_limit_bytes=40 * 2**20),
        cost_estimate=pl.CostEstimate(
            flops=total_blocks * 4 * 128 * 128 * 512, bytes_accessed=rows * width * 8, transcendentals=0
        ),
        name="attend",
    )(*tables, qkv)


def attend_back(tables, qkv, log_total, grad_attended, block_count, head_count, scale):
    rows, width = qkv.shape[0], qkv.shape[1] // 3
    total_blocks = rows // BLK
    return pl.pallas_call(
        functools.partial(attend_back_kernel, block_count, head_count, scale, unroll_of(total_blocks, 8)),
        out_shape=jax.ShapeDtypeStruct((rows, 3 * width), low),
        in_specs=[smem] * 4 + [vmem] * 3,
        out_specs=vmem,
        scratch_shapes=[
            pltpu.VMEM((rows, 2 * width), full),
            pltpu.VMEM((unroll_of(total_blocks, 8), KEY_BLOCKS * BLK, 2 * width), full),
        ],
        compiler_params=pltpu.CompilerParams(vmem_limit_bytes=40 * 2**20),
        cost_estimate=pl.CostEstimate(
            flops=total_blocks * 10 * 128 * 128 * 512, bytes_accessed=rows * width * 16, transcendentals=0
        ),
        name="attend_back",
    )(*tables, qkv, log_total, grad_attended)


def as_row(vector):
    return vector[...].astype(full).reshape(1, -1)


def row_stats(values):
    average = jnp.mean(values, axis=-1, keepdims=True)
    centered = values - average
    variance = jnp.mean(centered * centered, axis=-1, keepdims=True)
    inverse = lax.rsqrt(variance + norm_eps)
    return centered * inverse, inverse


def project_kernel(count, rows, column, *refs):
    parts, (gain, shift, w_query, w_key, w_value) = refs[:count], refs[count : count + 5]
    qkv, normed = refs[-2:]
    weights = jnp.concatenate([w_query[...], w_key[...], w_value[...]], axis=1)
    for i, part in enumerate(parts):
        at = pl.ds(pl.multiple_of(rows[i] * part.shape[0], part.shape[0]), part.shape[0])
        scaled, _ = row_stats(part[...].astype(full))
        result = (scaled * as_row(gain) + as_row(shift)).astype(low)
        normed[at, :] = result
        qkv[at, :] = matmul(result, weights).astype(low)


def project(rows, column, parts, gain, shift, weights, width):
    count = len(parts)
    tokens, model = parts[0].shape
    whole = pl.BlockSpec((tokens, model), lambda j, rows, column: (0, 0))
    row = pl.BlockSpec((model,), lambda j, rows, column: (0,))
    weight = pl.BlockSpec((model, width), lambda j, rows, column: (0, column[0]))
    return pl.pallas_call(
        functools.partial(project_kernel, count),
        grid_spec=pltpu.PrefetchScalarGridSpec(
            num_scalar_prefetch=2,
            grid=(1,),
            in_specs=[whole] * count + [row, row] + [weight] * 3,
            out_specs=(
                pl.BlockSpec((count * tokens, 3 * width), lambda j, rows, column: (0, 0)),
                pl.BlockSpec((count * tokens, model), lambda j, rows, column: (0, 0)),
            ),
        ),
        out_shape=(
            jax.ShapeDtypeStruct((count * tokens, 3 * width), low),
            jax.ShapeDtypeStruct((count * tokens, model), low),
        ),
        compiler_params=pltpu.CompilerParams(vmem_limit_bytes=vmem_limit),
        cost_estimate=pl.CostEstimate(
            flops=6 * count * tokens * model * width,
            bytes_accessed=4 * count * tokens * model,
            transcendentals=0,
        ),
        name="project",
    )(rows, column, *parts, gain, shift, *weights)


def project_back_kernel(
    width, inputs, gain, grad_middle, received, w_query, w_key, w_value, input_grad, gain_grads, total
):
    step = pl.program_id(0)

    @pl.when(step == 0)
    def _():
        total[...] = jnp.zeros_like(total)

    result = total[...]
    for part, weight in enumerate((w_query, w_key, w_value)):
        pieces = [
            received[i, :, part * width : (part + 1) * width] for i in range(received.shape[0])
        ]
        result += matmul_right(jnp.concatenate(pieces, axis=1), weight[...])
    total[...] = result

    @pl.when(step == pl.num_programs(0) - 1)
    def _():
        grad_normed = total[...]
        scaled, inverse = row_stats(inputs[...].astype(full))
        back = normalize_back(grad_normed, scaled, inverse, as_row(gain))
        input_grad[...] = (grad_middle[...] + back).astype(low)
        gain_grads[0:1, :] = jnp.sum(grad_normed * scaled, axis=0, keepdims=True)
        gain_grads[1:2, :] = jnp.sum(grad_normed, axis=0, keepdims=True)


def project_back(inputs, gain, grad_middle, received, w_query, w_key, w_value):
    tokens, model = inputs.shape
    columns = 256
    width = received.shape[2] // 3
    per_step = columns // width
    weight = pl.BlockSpec((model, columns), lambda j: (0, j))
    row = pl.BlockSpec((model,), lambda j: (0,))
    whole = pl.BlockSpec((tokens, model), lambda j: (0, 0))
    return pl.pallas_call(
        functools.partial(project_back_kernel, width),
        grid=(model // columns,),
        out_shape=(
            jax.ShapeDtypeStruct((tokens, model), low),
            jax.ShapeDtypeStruct((2, model), full),
        ),
        in_specs=[
            whole,
            row,
            whole,
            pl.BlockSpec((per_step, tokens, 3 * width), lambda j: (j, 0, 0)),
            weight,
            weight,
            weight,
        ],
        out_specs=(whole, pl.BlockSpec((2, model), lambda j: (0, 0))),
        scratch_shapes=[pltpu.VMEM((tokens, model), full)],
        compiler_params=pltpu.CompilerParams(vmem_limit_bytes=vmem_limit),
        cost_estimate=pl.CostEstimate(
            flops=6 * tokens * model * model, bytes_accessed=6 * model * model, transcendentals=0
        ),
        name="project_back",
    )(inputs, gain, grad_middle, received, w_query, w_key, w_value)


def hidden(normed, grad_out, w_in, b_in, w_back):
    inner = matmul(normed, w_in) + as_row(b_in)
    share = 0.5 * (1.0 + lax.erf(inner * 0.7071067811865476))
    density = jnp.exp(inner * inner * -0.5) * 0.3989422804014327
    grad_active = matmul_right(grad_out, w_back)
    grads = (grad_active * (share + inner * density)).astype(low)
    return (inner * share).astype(low), grads


def feed_kernel(
    received,
    inputs,
    grad_out,
    w_out,
    gain,
    shift,
    b_back,
    w_in,
    b_in,
    w_back,
    output,
    normed,
    grad_middle,
    grad_middle_low,
    grad_attended,
    gain_grads,
    b_in_grad,
    held_out,
    held_in,
    held_back,
    scaled,
    out_total,
    grad_total,
    arrived,
):
    groups, _, width = received.shape
    pieces, _, columns = held_in.shape
    first = pltpu.make_async_copy(w_out, held_out, arrived.at[2, 0])
    loads = []
    for i in range(pieces):
        at = pl.ds(i * columns, columns)
        loads.append(
            (
                pltpu.make_async_copy(w_in.at[:, at], held_in.at[i], arrived.at[0, i]),
                pltpu.make_async_copy(w_back.at[at, :], held_back.at[i], arrived.at[1, i]),
            )
        )
    first.start()
    for pair in loads:
        for load in pair:
            load.start()
    first.wait()
    attended = jnp.concatenate([received[i] for i in range(groups)], axis=1)
    rows = inputs[...].astype(full) + matmul(attended, held_out[...])
    unit, rate = row_stats(rows)
    scaled[...] = unit
    normed[...] = (unit * as_row(gain) + as_row(shift)).astype(low)
    out_total[...] = rows + as_row(b_back)
    for i, pair in enumerate(loads):
        at = slice(i * columns, (i + 1) * columns)
        for load in pair:
            load.wait()
        active, grads = hidden(
            normed[...], grad_out[...], held_in[i], b_in[at], held_back[i]
        )
        b_in_grad[:, at] = jnp.sum(grads.astype(full), axis=0, keepdims=True)
        out_total[...] += matmul(active, held_back[i])
        back = matmul_right(grads, held_in[i])
        if i:
            back += grad_total[...]
        grad_total[...] = back
    output[...] = out_total[...].astype(low)
    grad_normed = grad_total[...]
    unit = scaled[...]
    grad_full = grad_out[...].astype(full)
    grads_middle = grad_full + normalize_back(grad_normed, unit, rate, as_row(gain))
    grad_middle[...] = grads_middle
    grads_low = grads_middle.astype(low)
    grad_middle_low[...] = grads_low
    result = matmul_right(grads_low, held_out[...]).astype(low)
    for i in range(groups):
        grad_attended[i] = result[:, i * width : (i + 1) * width]
    gain_grads[0:1, :] = jnp.sum(grad_normed * unit, axis=0, keepdims=True)
    gain_grads[1:2, :] = jnp.sum(grad_normed, axis=0, keepdims=True)
    gain_grads[2:3, :] = jnp.sum(grad_full, axis=0, keepdims=True)


def feed(received, inputs, grad_out, w_out, gain, shift, b_back, w_in, b_in, w_back):
    tokens, model = inputs.shape
    ff = w_in.shape[1]
    groups, _, width = received.shape
    columns = 1024
    pieces = ff // columns
    anywhere = pl.BlockSpec(memory_space=pl.ANY)
    return pl.pallas_call(
        feed_kernel,
        out_shape=(
            jax.ShapeDtypeStruct((tokens, model), low),
            jax.ShapeDtypeStruct((tokens, model), low),
            jax.ShapeDtypeStruct((tokens, model), full),
            jax.ShapeDtypeStruct((tokens, model), low),
            jax.ShapeDtypeStruct((groups, tokens, width), low),
            jax.ShapeDtypeStruct((3, model), full),
            jax.ShapeDtypeStruct((1, ff), full),
        ),
        in_specs=[vmem, vmem, vmem, anywhere, vmem, vmem, vmem, anywhere, vmem, anywhere],
        out_specs=(vmem,) * 7,
        scratch_shapes=[
            pltpu.VMEM((model, model), low),
            pltpu.VMEM((pieces, model, columns), low),
            pltpu.VMEM((pieces, columns, model), low),
            pltpu.VMEM((tokens, model), full),
            pltpu.VMEM((tokens, model), full),
            pltpu.VMEM((tokens, model), full),
            pltpu.SemaphoreType.DMA((3, pieces)),
        ],
        compiler_params=pltpu.CompilerParams(vmem_limit_bytes=vmem_limit),
        cost_estimate=pl.CostEstimate(
            flops=8 * tokens * model * ff, bytes_accessed=4 * model * ff, transcendentals=0
        ),
        name="feed",
    )(received, inputs, grad_out, w_out, gain, shift, b_back, w_in, b_in, w_back)


def pick_blocks(index, total, sent, own, other):
    def block(distance):
        return total[:, pl.ds(index ^ distance, 1)][:, 0].astype(low)

    sent[0] = block(1)
    sent[1] = block(3)
    own[...] = block(0)
    other[...] = block(2)


def picked_shapes(outer, rows, columns):
    shape = (outer, rows, columns)
    return [jax.ShapeDtypeStruct((2,) + shape, low)] + [jax.ShapeDtypeStruct(shape, low)] * 2


def picked_specs(outer, rows, columns):
    whole = pl.BlockSpec((outer, rows, columns), lambda j, places: (0, 0, 0))
    return [pl.BlockSpec((2, outer, rows, columns), lambda j, places: (0, 0, 0, 0)), whole, whole]


def accumulate(total, value):
    @pl.when(pl.program_id(0) == 0)
    def _():
        total[...] = value.reshape(total.shape)

    @pl.when(pl.program_id(0) > 0)
    def _():
        total[...] += value.reshape(total.shape)


def product_kernel(places, left, right, sent, own, other, total):
    accumulate(total, matmul_left(left[...], right[...]))

    @pl.when(pl.program_id(0) == pl.num_programs(0) - 1)
    def _():
        pick_blocks(places[1], total, sent, own, other)


def product(places, left, left_columns, right, outer, name):
    tokens, columns = right.shape
    chunk = 768
    rows = left_columns // (4 * outer)
    return pl.pallas_call(
        product_kernel,
        grid_spec=pltpu.PrefetchScalarGridSpec(
            num_scalar_prefetch=1,
            grid=(tokens // chunk,),
            in_specs=[
                pl.BlockSpec((chunk, left_columns), lambda j, places: (j, 0)),
                pl.BlockSpec((chunk, columns), lambda j, places: (j, 0)),
            ],
            out_specs=picked_specs(outer, rows, columns),
            scratch_shapes=[pltpu.VMEM((outer, 4, rows, columns), full)],
        ),
        out_shape=picked_shapes(outer, rows, columns),
        compiler_params=pltpu.CompilerParams(vmem_limit_bytes=vmem_limit),
        cost_estimate=pl.CostEstimate(
            flops=2 * tokens * left_columns * columns,
            bytes_accessed=2 * tokens * (left_columns + columns),
            transcendentals=0,
        ),
        name=name,
    )(places, left, right)


def whole_product_kernel(left, right, result, total):
    accumulate(total, matmul_left(left[...], right[...]))

    @pl.when(pl.program_id(0) == pl.num_programs(0) - 1)
    def _():
        result[...] = total[...].astype(low)


def whole_product(left, right, name):
    tokens, columns = right.shape
    rows = left.shape[1]
    chunk = 768
    return pl.pallas_call(
        whole_product_kernel,
        grid=(tokens // chunk,),
        in_specs=[
            pl.BlockSpec((chunk, rows), lambda j: (j, 0)),
            pl.BlockSpec((chunk, columns), lambda j: (j, 0)),
        ],
        out_specs=pl.BlockSpec((rows, columns), lambda j: (0, 0)),
        out_shape=jax.ShapeDtypeStruct((rows, columns), low),
        scratch_shapes=[pltpu.VMEM((rows, columns), full)],
        compiler_params=pltpu.CompilerParams(vmem_limit_bytes=vmem_limit),
        cost_estimate=pl.CostEstimate(
            flops=2 * tokens * rows * columns,
            bytes_accessed=2 * tokens * (rows + columns),
            transcendentals=0,
        ),
        name=name,
    )(left, right)


def feed_products_kernel(
    places,
    normed,
    grad_out,
    w_in,
    b_in,
    w_back,
    in_sent,
    in_own,
    in_other,
    back_sent,
    back_own,
    back_other,
    held_normed,
    held_grad,
    held_in,
    held_back,
    active,
    grads,
    in_total,
    back_total,
    arrived,
):
    pieces, chunk, _ = held_normed.shape
    columns = held_in.shape[1]
    own = pl.ds(pl.multiple_of(places[0] * columns, columns), columns)
    weights = (
        pltpu.make_async_copy(w_in.at[:, own], held_in, arrived.at[0, pieces]),
        pltpu.make_async_copy(w_back.at[own, :], held_back, arrived.at[1, pieces]),
    )
    loads = [
        (
            pltpu.make_async_copy(normed.at[pl.ds(i * chunk, chunk)], held_normed.at[i], arrived.at[0, i]),
            pltpu.make_async_copy(grad_out.at[pl.ds(i * chunk, chunk)], held_grad.at[i], arrived.at[1, i]),
        )
        for i in range(pieces)
    ]
    for pair in (weights, *loads):
        for load in pair:
            load.start()
    for load in weights:
        load.wait()
    for i, pair in enumerate(loads):
        for load in pair:
            load.wait()
        active[i], grads[i] = hidden(held_normed[i], held_grad[i], held_in[...], b_in, held_back[...])
    rows = pieces * chunk
    model = held_normed.shape[2]
    in_total[...] = matmul_left(
        held_normed[...].reshape(rows, model), grads[...].reshape(rows, columns)
    ).reshape(in_total.shape)
    pick_blocks(places[1], in_total, in_sent, in_own, in_other)
    back_total[...] = matmul_left(
        active[...].reshape(rows, columns), held_grad[...].reshape(rows, model)
    ).reshape(back_total.shape)
    pick_blocks(places[1], back_total, back_sent, back_own, back_other)


def feed_products(places, normed, grad_out, w_in, b_in, w_back, seq_count):
    tokens, model = normed.shape
    columns = w_in.shape[1] // seq_count
    chunk = 384
    pieces = tokens // chunk
    slim = model // (4 * seq_count)
    back_slim = columns // 4
    anywhere = pl.BlockSpec(memory_space=pl.ANY)
    return pl.pallas_call(
        feed_products_kernel,
        grid_spec=pltpu.PrefetchScalarGridSpec(
            num_scalar_prefetch=1,
            grid=(1,),
            in_specs=[
                anywhere,
                anywhere,
                anywhere,
                pl.BlockSpec((1, columns), lambda j, places: (0, places[0])),
                anywhere,
            ],
            out_specs=picked_specs(seq_count, slim, columns) + picked_specs(1, back_slim, model),
            scratch_shapes=[
                pltpu.VMEM((pieces, chunk, model), low),
                pltpu.VMEM((pieces, chunk, model), low),
                pltpu.VMEM((model, columns), low),
                pltpu.VMEM((columns, model), low),
                pltpu.VMEM((pieces, chunk, columns), low),
                pltpu.VMEM((pieces, chunk, columns), low),
                pltpu.VMEM((seq_count, 4, slim, columns), full),
                pltpu.VMEM((1, 4, back_slim, model), full),
                pltpu.SemaphoreType.DMA((2, pieces + 1)),
            ],
        ),
        out_shape=picked_shapes(seq_count, slim, columns) + picked_shapes(1, back_slim, model),
        compiler_params=pltpu.CompilerParams(vmem_limit_bytes=vmem_limit),
        cost_estimate=pl.CostEstimate(
            flops=8 * tokens * model * columns,
            bytes_accessed=4 * tokens * model + 4 * model * columns,
            transcendentals=0,
        ),
        name="feed_products",
    )(places, normed, grad_out, w_in, b_in.reshape(1, -1), w_back)


def swap(blocks, axes):
    return lax.all_to_all(blocks, axes, split_axis=0, concat_axis=0, tiled=True)


def gather_rows(rows):
    return lax.all_gather(rows, "seq", axis=0, tiled=True)


def gather_parts(rows):
    count = lax.axis_size("seq")

    def move(block, distance):
        return lax.ppermute(block, "seq", [(i, i ^ distance) for i in range(count)])

    parts = [rows, None] + [None] * (count - 2)
    for distance in range(2, count, 2):
        parts[distance] = move(rows, distance)
    for distance in range(0, count, 2):
        parts[distance + 1] = move(parts[distance], 1)
    return parts


def trade(block, distance):
    return lax.ppermute(block, "batch", [(i, i ^ distance) for i in range(4)])


def first_sum(got, own, other):
    own = own.astype(full) + got[0].astype(full)
    other = (other.astype(full) + got[1].astype(full)).astype(low)
    return own, other


def together(*values):
    return lax.optimization_barrier(values)


def shards(
    inputs,
    cotangent,
    lengths,
    rand_owners,
    rand_offsets,
    global_ids,
    ln1_gain,
    ln1_shift,
    w_query,
    w_key,
    w_value,
    w_out,
    ln2_gain,
    ln2_shift,
    w_in,
    b_in,
    w_back,
    b_back,
):
    seq_count = lax.axis_size("seq")
    batch_count = lax.axis_size("batch")
    device_count = seq_count * batch_count
    token_count = inputs.shape[1]
    model_width = inputs.shape[2]
    ff_width = w_in.shape[1]
    block_count = token_count // BLK
    head_dim = model_width // HEADS
    scale = head_dim ** (-0.5)
    total_tokens = seq_count * token_count
    head_groups = min(HEADS, seq_count)
    copies = seq_count // head_groups
    head_count = HEADS // head_groups
    width = head_count * head_dim
    tables = (lengths, rand_owners, rand_offsets, global_ids)

    def to_heads(sent):
        if copies > 1:
            sent = jnp.repeat(sent, copies, axis=0)
        return swap(sent, "seq").reshape(total_tokens, -1)

    def to_tokens(rows):
        return swap(rows.reshape(seq_count, token_count, -1), "seq")[::copies]

    rows_in, grad_out = inputs[0], cotangent[0]
    gain_one, gain_two = ln1_gain, ln2_gain
    places = jnp.stack([lax.axis_index("seq"), lax.axis_index("batch")]).astype(jnp.int32)
    parts = gather_parts(rows_in)
    place = lax.axis_index("seq").astype(jnp.int32)
    column = (place // copies).reshape(1)
    weights = [w_query, w_key, w_value]
    if width % 128:
        weights = [
            lax.dynamic_slice_in_dim(w, place // copies * width, width, axis=1) for w in weights
        ]
        column = jnp.zeros_like(column)
    qkv, normed_all = project(
        place ^ jnp.arange(seq_count, dtype=jnp.int32),
        column,
        parts,
        gain_one,
        ln1_shift,
        weights,
        width,
    )
    late_grad_out, qkv = together(grad_out, qkv)
    grad_out_all = gather_rows(late_grad_out)
    attended_all, log_total = attend(tables, qkv, block_count, head_count, scale)
    output, normed_two, grad_middle, grad_middle_low, grad_attended, gain_two_grads, grad_b_in = feed(
        to_tokens(attended_all),
        rows_in,
        grad_out,
        w_out,
        gain_two,
        ln2_shift,
        b_back,
        w_in,
        b_in,
        w_back,
    )
    normed_two_all = gather_rows(normed_two)
    grad_middle_all = gather_rows(grad_middle_low)
    grad_rows, grad_out_all = together(to_heads(grad_attended), grad_out_all)
    grad_qkv = attend_back(tables, qkv, log_total, grad_rows, block_count, head_count, scale)
    grad_qkv_near = to_tokens(grad_qkv)

    slim = model_width // device_count
    inner_columns = ff_width // seq_count
    qkv_sent, qkv_own, qkv_other = product(
        places, normed_all, model_width, grad_qkv, seq_count, "qkv_product"
    )
    qkv_got = trade(qkv_sent, 1)
    normed_two_all, qkv_own = together(normed_two_all, qkv_own)
    in_sent, in_own, in_other, back_sent, back_own, back_other = feed_products(
        places, normed_two_all, grad_out_all, w_in, b_in, w_back, seq_count
    )
    in_got = trade(in_sent, 1)
    qkv_got, in_own = together(qkv_got, in_own)
    qkv_own, qkv_other = first_sum(qkv_got, qkv_own, qkv_other)
    grad_qkv_near, qkv_other, back_sent = together(grad_qkv_near, qkv_other, back_sent)
    back_got = trade(back_sent, 1)
    qkv_last = trade(qkv_other, 2)
    input_grad, gain_one_grads = project_back(
        rows_in, gain_one, grad_middle, grad_qkv_near, w_query, w_key, w_value
    )
    small = [gain_one_grads[0], gain_one_grads[1], *gain_two_grads, grad_b_in[0]]
    packed = jnp.concatenate([v.reshape(device_count, -1) for v in small], axis=1)
    packed = swap(packed, ("seq", "batch"))
    in_got, qkv_last, packed = together(in_got, qkv_last, packed)
    in_own, in_other = first_sum(in_got, in_own, in_other)
    in_last = trade(in_other, 2)
    own_rows = width // copies
    back_own, back_other = first_sum(back_got, back_own, back_other)
    own_attended, in_own = together(attended_all, in_own)
    if copies > 1:
        at = lax.axis_index("seq") % copies * own_rows
        own_attended = lax.dynamic_slice_in_dim(own_attended, at, own_rows, axis=1)
    out_partial = whole_product(own_attended, grad_middle_all, "out_product")
    out_rows = lax.psum_scatter(out_partial, "batch", scatter_dimension=0, tiled=True).astype(full)
    in_last, back_other = together(in_last, back_other)
    mixed = [
        (own + last.astype(full)).astype(low)
        for own, last in ((in_own, in_last), (qkv_own, qkv_last))
    ]
    mixed = swap(jnp.concatenate(mixed, axis=2), "seq")
    back_rows = (back_own + trade(back_other, 2).astype(full))[0]
    in_rows = mixed[:, :, :inner_columns].transpose(1, 0, 2).reshape(slim, ff_width).astype(full)
    qkv_rows = mixed[::copies, :, inner_columns:].transpose(1, 0, 2).astype(full)
    qkv_rows = [
        qkv_rows[:, :, i * width : (i + 1) * width].reshape(slim, model_width) for i in range(3)
    ]
    packed = jnp.sum(packed, axis=0)
    cuts, at = [], 0
    for v in small:
        size = v.shape[0] // device_count
        cuts.append(packed[at : at + size])
        at += size
    return (
        output[None],
        input_grad[None],
        cuts[0],
        cuts[1],
        qkv_rows[0],
        qkv_rows[1],
        qkv_rows[2],
        out_rows,
        cuts[2],
        cuts[3],
        in_rows,
        cuts[5],
        back_rows,
        cuts[4],
    )


def solution(mesh):
    rows = P("batch", "seq", None)
    table = P("batch", None, None)
    thin = P(("seq", "batch"))
    wide = P(("seq", "batch"), None)
    return jax.shard_map(
        shards,
        mesh=mesh,
        in_specs=(rows, rows, P("batch", None), table, table, table) + (P(),) * 12,
        out_specs=(rows, rows, thin, thin, wide, wide, wide, wide, thin, thin, wide, thin, wide, thin),
        check_vma=False,
    )
```
